128 devices in a mesh: blk: 32 (over z_lo, y, x), tensor: 4 (over z_hi, core).
Axes of the slice: x: 4, y: 4, z: 4 (z_hi: 2, z_lo: 2; z = z_hi * 2 + z_lo), core: 2. Of those that a mesh axis runs over, the one named last changes fastest.
Arguments:
- inputs: bfloat16 [2, 4096, 2304], P(None, 'blk'), may hold values from -6 to 6
- out_grad: bfloat16 [2, 4096, 2304], P(None, 'blk'), may hold values from -6 to 6
- segment_ids: int32 [2, 4096], P(None, 'blk'), may hold values from 0 to 1, never falling along the last dimension, each value on 1 to 3968 neighbouring positions
- keep_mask: int32 [2, 4096], P(None, 'blk'), may hold values 0 or 1
- query_codes: bfloat16 [2304, 2048], P(None, 'tensor'), may hold values from -128 to 127, as said below
- key_codes: bfloat16 [2304, 1024], P(None, 'tensor'), may hold values from -128 to 127, as said below
- value_codes: bfloat16 [2304, 1024], P(None, 'tensor'), may hold values from -128 to 127, as said below
- output_codes: bfloat16 [2048, 2304], P('tensor'), may hold values from -128 to 127, as said below
- gate_codes: bfloat16 [2304, 9216], P(None, 'tensor'), may hold values from -128 to 127, as said below
- up_codes: bfloat16 [2304, 9216], P(None, 'tensor'), may hold values from -128 to 127, as said below
- down_codes: bfloat16 [9216, 2304], P('tensor'), may hold values from -128 to 127, as said below
- norm_attn_in: float32 [2304], replicated, may hold values from 0.25 to 1.75
- norm_attn_out: float32 [2304], replicated, may hold values from 0.25 to 1.75
- norm_ffn_in: float32 [2304], replicated, may hold values from 0.25 to 1.75
- norm_ffn_out: float32 [2304], replicated, may hold values from 0.25 to 1.75
Outputs:
- out_rows: bfloat16 [2, 4096, 2304], P(None, 'blk')
- input_grad: bfloat16 [2, 4096, 2304], P(None, 'blk')
- grad_query: float32 [2304, 2048], P('blk', 'tensor')
- grad_key: float32 [2304, 1024], P('blk', 'tensor')
- grad_value: float32 [2304, 1024], P('blk', 'tensor')
- grad_output: float32 [2048, 2304], P('tensor', 'blk')
- grad_gate: float32 [2304, 9216], P('blk', 'tensor')
- grad_up: float32 [2304, 9216], P('blk', 'tensor')
- grad_down: float32 [9216, 2304], P('tensor', 'blk')
- grad_attn_in: float32 [2304], P('blk')
- grad_attn_out: float32 [2304], P('blk')
- grad_ffn_in: float32 [2304], P('blk')
- grad_ffn_out: float32 [2304], P('blk')
The draws below stay inside these ranges and needn't reach their ends.
Inputs may be any that keep to these rules, and one draw needn't show every extreme that they name: `segment_ids`: document numbers never fall along a row; a document has at most 3968 tokens. `query_codes`: whole numbers. `key_codes`: whole numbers. `value_codes`: whole numbers. `output_codes`: whole numbers. `gate_codes`: whole numbers. `up_codes`: whole numbers. `down_codes`: whole numbers.
All inputs are finite; a program needn't handle non-finite values. No bound on the sum of `keep_mask` on one device may be relied on, other than what follows from the above.
Results may differ from the reference program's by a relative error of at most 0.035.
Values may be sent and summed in bfloat16 or wider, within the bound.
A program may use at most 320 MiB of HBM per device.

```python
import math
import jax
import jax.numpy as jnp
import numpy as np
from jax import lax

D = 2304
HEADS = 8
KVH = 4
HD = 256
FF = 9216
MB = 2
SEGS = 2
SEQ = 4096
LONGEST = 3968


def draw_codes(key, salt, height, width):
    picked = jax.random.randint(jax.random.fold_in(key, salt), (height, width), -128, 128, dtype=jnp.int32)
    return picked.astype(jnp.float32).astype(jnp.bfloat16)


def draw_query_codes(key, part):
    return draw_codes(key, 101, D, HEADS * HD)


def draw_key_codes(key, part):
    return draw_codes(key, 102, D, KVH * HD)


def draw_value_codes(key, part):
    return draw_codes(key, 103, D, KVH * HD)


def draw_output_codes(key, part):
    return draw_codes(key, 104, HEADS * HD, D)


def draw_gate_codes(key, part):
    return draw_codes(key, 105, D, FF)


def draw_up_codes(key, part):
    return draw_codes(key, 106, D, FF)


def draw_down_codes(key, part):
    return draw_codes(key, 107, FF, D)


def with_ends(values, stream_key, smallest, top_value):
    spot = [jax.random.randint(jax.random.fold_in(stream_key, axis), (), 0, length) for axis, length in enumerate(values.shape)]
    widest = values.shape.index(max(values.shape))
    beside = spot[:widest] + [(spot[widest] + 1) % values.shape[widest]] + spot[widest + 1:]
    return values.at[tuple(spot)].set(smallest).at[tuple(beside)].set(top_value)


def with_spikes(values, key, source, target, blocks, factor):
    def block_of(position):
        return (jnp.arange(values.shape[position]) // (values.shape[position] // blocks)).reshape((-1,) + (1,) * (values.ndim - 1 - position))

    near = jax.random.permutation(key, blocks)[block_of(target)]
    far = (block_of(target) + blocks // 2) % blocks
    return jnp.where((block_of(source) == near) | (block_of(source) == far), factor * values, values)


def block_scale(stream_key, dims, pieces, smallest, largest):
    level = 1.0
    for position, blocks in pieces:
        heights = jax.random.uniform(jax.random.fold_in(jax.random.fold_in(stream_key, 6), position), (blocks,), jnp.float32, smallest / len(pieces), largest / len(pieces))
        level = level * jnp.repeat(jnp.exp(heights), dims[position] // blocks).reshape((-1,) + (1,) * (len(dims) - 1 - position))
    return level


def split_up(count, total, reach, slope):
    portions = [(1 << 20) // math.isqrt(grade ** slope) + 1 for grade in range(2, count + 1)]
    surplus, holding = total - reach - (count - 1), [1] * (count - 1)
    while surplus > 0:
        free = [i for i in range(count - 1) if holding[i] < reach]
        mass, remaining = sum([portions[i] for i in free]), surplus
        for i in free:
            more = min(reach - holding[i], max(1, remaining * portions[i] // mass), surplus)
            holding[i] = holding[i] + more
            surplus = surplus - more
    return np.array([reach] + holding)


def uneven(stream_key, amount, total, bound, slope):
    if amount == 2:
        one = jax.random.randint(stream_key, (), max(1, total - bound), min(bound, total - 1) + 1)
        return jnp.stack([one, total - one])
    tallies = jnp.asarray(split_up(amount, total, bound, slope), jnp.int32)
    pairs = (amount - 1) // 2
    giver, receiver = tallies[1:1 + 2 * pairs:2], tallies[2:2 + 2 * pairs:2]
    room = jnp.minimum(giver - 1, bound - receiver)
    passed = jax.random.randint(jax.random.fold_in(stream_key, 1), (pairs,), 0, 1 << 20) % (room + 1)
    tallies = tallies.at[1:1 + 2 * pairs:2].set(giver - passed).at[2:2 + 2 * pairs:2].set(receiver + passed)
    return tallies[jax.random.permutation(jax.random.fold_in(stream_key, 2), amount)]


def noise_with(stream_key, dims, spread, limit, pieces, heavy, held_as=jnp.bfloat16):
    values = spread * jax.random.normal(stream_key, dims, jnp.float32)
    if pieces:
        values = values * block_scale(stream_key, dims, pieces, -0.22, 0.18)
    return jnp.clip(with_spikes(values, jax.random.fold_in(stream_key, 3), *heavy), -limit, limit).astype(held_as)


def setup_inputs(seed: int = 0) -> dict:
    streams_of = jax.random.split(jax.random.key(seed), 16)
    return {
        "inputs": noise_with(streams_of[0], (MB, SEQ, D), 1.0, 6.0, ((1, 32),), (1, 2, 32, 2.75)),
        "out_grad": noise_with(streams_of[1], (MB, SEQ, D), 1.0, 6.0, ((1, 32),), (1, 2, 32, 2.75)),
        "segment_ids": jax.vmap(lambda own: jnp.searchsorted(jnp.cumsum(uneven(own, SEGS, SEQ, LONGEST, 2)), jnp.arange(SEQ), side="right"))(jax.random.split(streams_of[2], MB)).reshape((MB, SEQ)).astype(jnp.int32),
        "keep_mask": with_ends((jax.random.randint(streams_of[3], (MB, SEQ), 0, 8) < 7).astype(jnp.int32), jax.random.fold_in(streams_of[3], 1), 0, 1),
        "query_codes": draw_query_codes(jax.random.fold_in(streams_of[15], 71), 0),
        "key_codes": draw_key_codes(jax.random.fold_in(streams_of[15], 71), 0),
        "value_codes": draw_value_codes(jax.random.fold_in(streams_of[15], 71), 0),
        "output_codes": draw_output_codes(jax.random.fold_in(streams_of[15], 71), 0),
        "gate_codes": draw_gate_codes(jax.random.fold_in(streams_of[15], 71), 0),
        "up_codes": draw_up_codes(jax.random.fold_in(streams_of[15], 71), 0),
        "down_codes": draw_down_codes(jax.random.fold_in(streams_of[15], 71), 0),
        "norm_attn_in": jnp.clip(1.0 + 0.15 * jax.random.normal(streams_of[11], (D,), jnp.float32), 0.25, 1.75),
        "norm_attn_out": jnp.clip(1.0 + 0.15 * jax.random.normal(streams_of[12], (D,), jnp.float32), 0.25, 1.75),
        "norm_ffn_in": jnp.clip(1.0 + 0.15 * jax.random.normal(streams_of[13], (D,), jnp.float32), 0.25, 1.75),
        "norm_ffn_out": jnp.clip(1.0 + 0.15 * jax.random.normal(streams_of[14], (D,), jnp.float32), 0.25, 1.75),
    }


@jax.custom_vjp
def low(v):
    return lax.optimization_barrier(v.astype(jnp.bfloat16)).astype(jnp.float32)

@jax.custom_vjp
def low_back(v):
    return v

def low_keep(v):
    return (low(v), None)

def low_pass(kept, grad):
    return (grad,)

def back_keep(v):
    return (v, None)

def back_low(kept, grad):
    return (low(grad),)
low.defvjp(low_keep, low_pass)
low_back.defvjp(back_keep, back_low)
HIGH = lax.Precision.HIGHEST
CAP = 50.0
EPS = 1e-06
LEVEL_SCALE = 1.0 / 74.0
WIDTHS = (8, 4, 2)
FLOOR_SCORE = -1e+30

def sliced(codes, bits):
    spacing = 2.0 ** (8 - bits)
    upper = 2.0 ** (bits - 1)
    return jnp.clip(jnp.floor(codes / spacing + 0.5), -upper, upper - 1.0) * spacing

def norm_rows(values, gain):
    return values * lax.rsqrt(lax.optimization_barrier(jnp.mean(values * values, axis=-1, keepdims=True)) + EPS) * gain

def matmul(left, right):
    return jnp.dot(left, right, precision=HIGH, preferred_element_type=jnp.float32)

def rotate(values, cosine, sine):
    half = values.shape[-1] // 2
    first = values[..., :half]
    second = values[..., half:]
    return jnp.concatenate([first * cosine - second * sine, second * cosine + first * sine], axis=-1)

def gelu_mix(gate, upper):
    return jax.nn.gelu(gate, approximate=True) * upper

def layer(tokens, weights, gains, segment, keep):
    w_query, w_key, w_value, w_output, w_gate, w_up, w_down = weights
    gain_attn_in, gain_attn_out, gain_ffn_in, gain_ffn_out = gains
    length = tokens.shape[0]
    group = HEADS // KVH
    place = jnp.arange(length, dtype=jnp.int32)
    freqs = 10000.0 ** (-jnp.arange(HD // 2, dtype=jnp.float32) * 2.0 / HD)
    angles = jnp.arange(length, dtype=jnp.float32)[:, None] * freqs[None, :]
    cosine = jnp.cos(angles)
    sine = jnp.sin(angles)
    normed = low(norm_rows(tokens, gain_attn_in))
    queries = matmul(normed, w_query).reshape(length, HEADS, HD).transpose(1, 0, 2)
    queries = low(rotate(low_back(queries), cosine, sine))
    keys = matmul(normed, w_key).reshape(length, KVH, HD).transpose(1, 0, 2)
    keys = low(rotate(low_back(keys), cosine, sine))
    values = low_back(low(matmul(normed, w_value).reshape(length, KVH, HD).transpose(1, 0, 2)))
    keys = jnp.repeat(keys, group, axis=0)
    values = jnp.repeat(values, group, axis=0)
    key_tag = jnp.where(keep == 1, segment, -1)
    block = min(512, length)
    count = length // block

    def one_block(parts):
        query_block, tag_block, place_block = parts
        raw = low_back(jnp.einsum('hqd,hkd->hqk', query_block, keys, precision=HIGH, preferred_element_type=jnp.float32))
        bent = jnp.tanh(raw * HD ** (-0.5) / CAP)
        mask = (place[None, :] <= place_block[:, None]) & (key_tag[None, :] == tag_block[:, None]) | (place[None, :] == place_block[:, None])
        capped = jnp.where(mask[None], CAP * bent, FLOOR_SCORE)
        top = lax.optimization_barrier(jnp.max(capped, axis=-1, keepdims=True))
        weights_here = jnp.exp(capped - top)
        probs = weights_here / lax.optimization_barrier(jnp.sum(weights_here, axis=-1, keepdims=True))
        return jnp.einsum('hqk,hkd->hqd', low(probs), values, precision=HIGH, preferred_element_type=jnp.float32)
    query_blocks = queries.reshape(HEADS, count, block, HD).transpose(1, 0, 2, 3)
    blocks_out = lax.map(jax.checkpoint(one_block), (query_blocks, segment.reshape(count, block), place.reshape(count, block)))
    attended = blocks_out.transpose(1, 0, 2, 3).reshape(HEADS, length, HD)
    attended = low_back(low(attended))
    attended_flat = attended.transpose(1, 0, 2).reshape(length, HEADS * HD)
    branch = low_back(matmul(attended_flat, w_output))
    middle = tokens + norm_rows(branch, gain_attn_out)
    ffn_in = low(norm_rows(middle, gain_ffn_in))
    gate = low_back(matmul(ffn_in, w_gate))
    upper = low_back(matmul(ffn_in, w_up))
    hidden = low(gelu_mix(gate, upper))
    down = low_back(matmul(hidden, w_down))
    return middle + norm_rows(down, gain_ffn_out)

def reference(inputs, out_grad, segment_ids, keep_mask, query_codes, key_codes, value_codes, output_codes, gate_codes, up_codes, down_codes, norm_attn_in, norm_attn_out, norm_ffn_in, norm_ffn_out):
    codes = tuple((w.astype(jnp.float32) for w in (query_codes, key_codes, value_codes, output_codes, gate_codes, up_codes, down_codes)))
    gains = tuple((g.astype(jnp.float32) for g in (norm_attn_in, norm_attn_out, norm_ffn_in, norm_ffn_out)))
    in_scale = LEVEL_SCALE * D ** (-0.5)
    mid_scale = LEVEL_SCALE * (HEADS * HD) ** (-0.5)
    ff_scale = LEVEL_SCALE * FF ** (-0.5)
    scales = (in_scale, in_scale, in_scale, mid_scale, in_scale, in_scale, ff_scale)
    totals = [jnp.zeros_like(w) for w in codes] + [jnp.zeros_like(g) for g in gains]
    out_list = []
    grad_list = []
    for batch in range(MB):
        bits = WIDTHS[batch % 3]
        offsets = tuple((sliced(w, bits) - w for w in codes))
        segment = segment_ids[batch]
        keep = keep_mask[batch]

        def forward(tokens, *params):
            weights = tuple((low(factor * (w + shift)) for factor, w, shift in zip(scales, params[:7], offsets)))
            return layer(tokens, weights, params[7:], segment, keep)
        result, pull = jax.vjp(forward, inputs[batch].astype(jnp.float32), *codes, *gains)
        grads = pull(out_grad[batch].astype(jnp.float32))
        out_list.append(result.astype(jnp.bfloat16))
        grad_list.append(grads[0].astype(jnp.bfloat16))
        totals = [left + right for left, right in zip(totals, grads[1:])]
    return (jnp.stack(out_list), jnp.stack(grad_list), totals[0], totals[1], totals[2], totals[3], totals[4], totals[5], totals[6], totals[7], totals[8], totals[9], totals[10])
```

```python
import functools

import jax
import jax.numpy as jnp
from jax import lax
from jax.experimental import pallas as pl
from jax.experimental.pallas import tpu as pltpu
from jax.sharding import PartitionSpec as P

D = 2304
HEADS = 8
HD = 256
FF = 9216

CAP = 50.0
EPS = 1e-06
LEVEL_SCALE = 1.0 / 74.0
WIDTHS = (8, 4, 2)

MESH = pl.DeviceIdType.MESH
VMEM = pltpu.VMEM
BF = jnp.bfloat16
F32 = jnp.float32
SEQ = 4096
ROWS = 128
TAGROW = 256
MASKED = -2.0


def place_of():
    b = lax.axis_index("blk")
    t = lax.axis_index("tensor")
    return b % 4, (b // 4) % 4, b // 16, t // 2, t % 2


def device_at(x, y, z, zh, c):
    return ((z * 4 + y) * 4 + x, zh * 2 + c)


def greet(peers):
    barrier = pltpu.get_barrier_semaphore()
    for peer in peers:
        pl.semaphore_signal(barrier, inc=1, device_id=peer, device_id_type=MESH)
    pl.semaphore_wait(barrier, len(peers))


def send(src, dst, ssem, rsem, peer):
    copy = pltpu.make_async_remote_copy(
        src_ref=src, dst_ref=dst, send_sem=ssem, recv_sem=rsem, device_id=peer, device_id_type=MESH
    )
    copy.start()
    return copy


def params(collective_id=None, limit=60):
    if collective_id is None:
        return pltpu.CompilerParams(vmem_limit_bytes=limit << 20)
    return pltpu.CompilerParams(
        vmem_limit_bytes=limit << 20, collective_id=collective_id, has_side_effects=True
    )


def whole(space=VMEM):
    return pl.BlockSpec(memory_space=space)


def gather_kernel(a_ref, b_ref, oa, ob, lsem, ssem, rsem):
    x, y, z, zh, c = place_of()
    xs = [device_at((x + j) % 4, y, z, zh, c) for j in (1, 2, 3)]
    ys = [device_at(x, (y + j) % 4, z, zh, c) for j in (1, 2, 3)]
    zp = device_at(x, y, 1 - z, zh, c)
    greet(xs + ys + [zp])
    mine_a = pltpu.make_async_copy(a_ref, oa.at[z, y, x], lsem.at[0])
    mine_b = pltpu.make_async_copy(b_ref, ob.at[z, y, x], lsem.at[1])
    mine_a.start()
    mine_b.start()
    za = send(a_ref, oa.at[z, y, x], ssem.at[0], rsem.at[0], zp)
    zb = send(b_ref, ob.at[z, y, x], ssem.at[1], rsem.at[1], zp)
    done = [za, zb]
    first_a = [send(a_ref, oa.at[z, y, x], ssem.at[2 + j], rsem.at[2 + j], xs[j]) for j in range(3)]
    first_b = [send(b_ref, ob.at[z, y, x], ssem.at[5 + j], rsem.at[5 + j], ys[j]) for j in range(3)]
    za.wait_recv()
    other = 1 - z
    next_a = [
        send(oa.at[other, y, x], oa.at[other, y, x], ssem.at[8 + j], rsem.at[8 + j], xs[j])
        for j in range(3)
    ]
    zb.wait_recv()
    next_b = [
        send(ob.at[other, y, x], ob.at[other, y, x], ssem.at[11 + j], rsem.at[11 + j], ys[j])
        for j in range(3)
    ]
    mine_a.wait()
    mine_b.wait()
    last = []
    for step, (level, copies_a, copies_b) in enumerate(((z, first_a, first_b), (other, next_a, next_b))):
        for copy in copies_a:
            copy.wait_recv()
        for j in range(3):
            k = 14 + 6 * step + j
            last.append(send(oa.at[level, y], oa.at[level, y], ssem.at[k], rsem.at[k], ys[j]))
        for copy in copies_b:
            copy.wait_recv()
        for j in range(3):
            k = 17 + 6 * step + j
            last.append(send(ob.at[level, :, x], ob.at[level, :, x], ssem.at[k], rsem.at[k], xs[j]))
    for copy in last:
        copy.wait_recv()
    for copy in done + first_a + first_b + next_a + next_b + last:
        copy.wait_send()


def gather(a, b):
    return pl.pallas_call(
        gather_kernel,
        out_shape=(
            jax.ShapeDtypeStruct((2, 4, 4) + a.shape, a.dtype),
            jax.ShapeDtypeStruct((2, 4, 4) + b.shape, b.dtype),
        ),
        in_specs=[whole(), whole()],
        out_specs=(whole(), whole()),
        scratch_shapes=[
            pltpu.SemaphoreType.DMA((2,)),
            pltpu.SemaphoreType.DMA((26,)),
            pltpu.SemaphoreType.DMA((26,)),
        ],
        compiler_params=params(1, 30),
    )(a, b)


def scatter_kernel(a_ref, b_ref, oa, ob, r1a, r1b, s1a, s1b, r2a, r2b, s2a, s2b, r3a, r3b, ssem, rsem):
    x, y, z, zh, c = place_of()
    xi = [(x + j) % 4 for j in (1, 2, 3)]
    yi = [(y + j) % 4 for j in (1, 2, 3)]
    xs = [device_at(i, y, z, zh, c) for i in xi]
    ys = [device_at(x, i, z, zh, c) for i in yi]
    zp = device_at(x, y, 1 - z, zh, c)
    greet(xs + ys + [zp])
    one_a = [send(a_ref.at[:, :, xi[j]], r1a.at[j], ssem.at[j], rsem.at[j], xs[j]) for j in range(3)]
    one_b = [send(b_ref.at[:, yi[j]], r1b.at[j], ssem.at[3 + j], rsem.at[3 + j], ys[j]) for j in range(3)]
    for copy in one_a:
        copy.wait_recv()

    def add_a(i, carry):
        zi, k = i // 4, i % 4
        total = a_ref[zi, k, x].astype(F32)
        for j in range(3):
            total = total + r1a[j, zi, k].astype(F32)
        s1a[zi, k] = total.astype(BF)
        return carry

    lax.fori_loop(0, 8, add_a, 0)
    two_a = [send(s1a.at[:, yi[j]], r2a.at[j], ssem.at[6 + j], rsem.at[6 + j], ys[j]) for j in range(3)]
    for copy in one_b:
        copy.wait_recv()

    def add_b(i, carry):
        zi, k = i // 4, i % 4
        total = b_ref[zi, y, k].astype(F32)
        for j in range(3):
            total = total + r1b[j, zi, k].astype(F32)
        s1b[zi, k] = total.astype(BF)
        return carry

    lax.fori_loop(0, 8, add_b, 0)
    two_b = [send(s1b.at[:, xi[j]], r2b.at[j], ssem.at[9 + j], rsem.at[9 + j], xs[j]) for j in range(3)]
    for copy in two_a:
        copy.wait_recv()
    for zi in range(2):
        total = s1a[zi, y].astype(F32)
        for j in range(3):
            total = total + r2a[j, zi].astype(F32)
        s2a[zi] = total.astype(BF)
    three_a = send(s2a.at[1 - z], r3a, ssem.at[12], rsem.at[12], zp)
    for copy in two_b:
        copy.wait_recv()
    for zi in range(2):
        total = s1b[zi, x].astype(F32)
        for j in range(3):
            total = total + r2b[j, zi].astype(F32)
        s2b[zi] = total.astype(BF)
    three_b = send(s2b.at[1 - z], r3b, ssem.at[13], rsem.at[13], zp)
    three_a.wait_recv()
    oa[...] = s2a[z].astype(F32) + r3a[...].astype(F32)
    three_b.wait_recv()
    ob[...] = s2b[z].astype(F32) + r3b[...].astype(F32)
    for copy in one_a + one_b + two_a + two_b + [three_a, three_b]:
        copy.wait_send()


def scatter(a, b):
    ta, tb = a.shape[3:], b.shape[3:]
    return pl.pallas_call(
        scatter_kernel,
        out_shape=(jax.ShapeDtypeStruct(ta, F32), jax.ShapeDtypeStruct(tb, F32)),
        in_specs=[whole(), whole()],
        out_specs=(whole(), whole()),
        scratch_shapes=[
            VMEM((3, 2, 4) + ta, BF),
            VMEM((3, 2, 4) + tb, BF),
            VMEM((2, 4) + ta, BF),
            VMEM((2, 4) + tb, BF),
            VMEM((3, 2) + ta, BF),
            VMEM((3, 2) + tb, BF),
            VMEM((2,) + ta, BF),
            VMEM((2,) + tb, BF),
            VMEM(ta, BF),
            VMEM(tb, BF),
            pltpu.SemaphoreType.DMA((14,)),
            pltpu.SemaphoreType.DMA((14,)),
        ],
        compiler_params=params(2, 40),
    )(a, b)


PIECES = 4


def total_kernel(p_ref, o_ref, r1, h, r2, ssem, rsem):
    x, y, z, zh, c = place_of()
    mate = device_at(x, y, z, zh, 1 - c)
    far = device_at(x, y, z, 1 - zh, c)
    greet([mate, far])
    size = p_ref.shape[1] // PIECES
    rows = [pl.ds(k * size, size) for k in range(PIECES)]
    one = [
        send(p_ref.at[1 - c, rows[k]], r1.at[rows[k]], ssem.at[k], rsem.at[k], mate)
        for k in range(PIECES)
    ]
    two, three = [], []
    for k in range(PIECES):
        one[k].wait_recv()
        h[rows[k]] = (p_ref[c, rows[k]].astype(F32) + r1[rows[k]].astype(F32)).astype(BF)
        i = PIECES + k
        two.append(send(h.at[rows[k]], r2.at[rows[k]], ssem.at[i], rsem.at[i], far))
    for k in range(PIECES):
        two[k].wait_recv()
        o_ref[c, rows[k]] = (h[rows[k]].astype(F32) + r2[rows[k]].astype(F32)).astype(BF)
        i = 2 * PIECES + k
        three.append(send(o_ref.at[c, rows[k]], o_ref.at[c, rows[k]], ssem.at[i], rsem.at[i], mate))
    for k in range(PIECES):
        three[k].wait_recv()
    for copy in one + two + three:
        copy.wait_send()


def total(p, collective_id):
    half = p.shape[1:]
    return pl.pallas_call(
        total_kernel,
        out_shape=jax.ShapeDtypeStruct(p.shape, BF),
        in_specs=[whole()],
        out_specs=whole(),
        scratch_shapes=[
            VMEM(half, BF),
            VMEM(half, BF),
            VMEM(half, BF),
            pltpu.SemaphoreType.DMA((3 * PIECES,)),
            pltpu.SemaphoreType.DMA((3 * PIECES,)),
        ],
        compiler_params=params(collective_id, 30),
    )(p)


CHUNK = 4
KEYS = CHUNK * ROWS


def nt(left, right):
    return lax.dot_general(left, right, (((1,), (1,)), ((), ())), preferred_element_type=F32)


def tn(left, right):
    return lax.dot_general(left, right, (((0,), (0,)), ((), ())), preferred_element_type=F32)


def nn(left, right):
    return jnp.dot(left, right, preferred_element_type=F32)


def load_chunk(k_ref, v_ref, step, m):
    blocks = pl.ds(step * CHUNK, CHUNK)
    keys = k_ref[blocks, m * ROWS : (m + 1) * ROWS, :].reshape(KEYS, HD)
    values = v_ref[blocks, m * ROWS : (m + 1) * ROWS, :].reshape(KEYS, HD)
    tags = k_ref[blocks, TAGROW : TAGROW + 16, m * ROWS : (m + 1) * ROWS].astype(F32)
    tag_row = jnp.concatenate([tags[i, 0:1, :] for i in range(CHUNK)], axis=1)
    return keys, values, tag_row


def allowed(step, tag_row, query_tag, query_place):
    key_place = step * KEYS + lax.broadcasted_iota(jnp.int32, (2 * ROWS, KEYS), 1)
    ok = (key_place <= query_place) & (tag_row == query_tag)
    return ok | (key_place == query_place)


def query_places():
    row = lax.broadcasted_iota(jnp.int32, (2 * ROWS, 1), 0)
    return lax.axis_index("blk") * ROWS + row % ROWS


def attend_kernel(q_ref, t_ref, k_ref, v_ref, o_ref, lse_ref):
    limit = lax.axis_index("blk") // CHUNK + 1
    where = query_places()
    for m in range(2):
        q = q_ref[m]
        tag = t_ref[m]

        def step(i, carry):
            acc, mass = carry
            keys, values, tag_row = load_chunk(k_ref, v_ref, i, m)
            bent = jnp.tanh(nt(q, keys) * (HD ** (-0.5) / CAP))
            e = jnp.where(allowed(i, tag_row, tag, where), jnp.exp(CAP * bent), 0.0)
            mass = mass + jnp.sum(e, axis=-1, keepdims=True)
            return acc + nn(e.astype(BF), values), mass

        acc, mass = lax.fori_loop(
            0, limit, step, (jnp.zeros((2 * ROWS, HD), F32), jnp.zeros((2 * ROWS, 1), F32))
        )
        o_ref[m] = acc / mass
        lse_ref[m] = jnp.log(mass)


def attend(q, tag, k, v):
    return pl.pallas_call(
        attend_kernel,
        out_shape=(
            jax.ShapeDtypeStruct((2, 2 * ROWS, HD), F32),
            jax.ShapeDtypeStruct((2, 2 * ROWS, 1), F32),
        ),
        in_specs=[whole()] * 4,
        out_specs=(whole(), whole()),
        compiler_params=params(None, 40),
    )(q, tag, k, v)


def attend_back_kernel(q_ref, g_ref, lse_ref, off_ref, t_ref, k_ref, v_ref, dq_ref, dk_ref, dv_ref):
    limit = lax.axis_index("blk") // CHUNK + 1
    where = query_places()
    for m in range(2):
        q = q_ref[m]
        g = g_ref[m]
        tag = t_ref[m]
        lse = lse_ref[m]
        off = off_ref[m]
        part = slice(m * ROWS, (m + 1) * ROWS)

        def step(i, dq):
            keys, values, tag_row = load_chunk(k_ref, v_ref, i, m)
            bent = jnp.tanh(nt(q, keys) * (HD ** (-0.5) / CAP))
            p = jnp.where(allowed(i, tag_row, tag, where), jnp.exp(CAP * bent - lse), 0.0)
            dp = nt(g, values)
            ds = (p * (dp - off) * (1.0 - bent * bent) * HD ** (-0.5)).astype(BF)
            blocks = pl.ds(i * CHUNK, CHUNK)
            dk_ref[blocks, part, :] = tn(ds, q).astype(BF).reshape(CHUNK, ROWS, HD)
            dv_ref[blocks, part, :] = tn(p.astype(BF), g).astype(BF).reshape(CHUNK, ROWS, HD)
            return dq + nn(ds, keys)

        dq_ref[m] = lax.fori_loop(0, limit, step, jnp.zeros((2 * ROWS, HD), F32))

        def blank(i, carry):
            blocks = pl.ds(i * CHUNK, CHUNK)
            dk_ref[blocks, part, :] = jnp.zeros((CHUNK, ROWS, HD), BF)
            dv_ref[blocks, part, :] = jnp.zeros((CHUNK, ROWS, HD), BF)
            return carry

        lax.fori_loop(limit, SEQ // KEYS, blank, 0)


def attend_back(q, g, lse, off, tag, k, v):
    return pl.pallas_call(
        attend_back_kernel,
        out_shape=(
            jax.ShapeDtypeStruct((2, 2 * ROWS, HD), F32),
            jax.ShapeDtypeStruct((32, 2 * ROWS, HD), BF),
            jax.ShapeDtypeStruct((32, 2 * ROWS, HD), BF),
        ),
        in_specs=[whole()] * 7,
        out_specs=(whole(),) * 3,
        compiler_params=params(None, 40),
    )(q, g, lse, off, tag, k, v)


PART = 576
SHARE = 72
TILE_A = 512
TILE_B = 256
COLS_A = 4608
COLS_B = 3840
SPANS_B = ((0, 9), (9, 13), (13, 15))
COLS_G = COLS_B + 128


def grads_kernel(
    da, ca, db, gb, cb, oa, ob,
    rda, rca, rdb, rgb, rcb, pa, pb, r2a, r2b, sa, sb, r3a, r3b, ssem, rsem,
):
    x, y, z, zh, c = place_of()
    xi = [(x + j) % 4 for j in (1, 2, 3)]
    yi = [(y + j) % 4 for j in (1, 2, 3)]
    xs = [device_at(i, y, z, zh, c) for i in xi]
    ys = [device_at(x, i, z, zh, c) for i in yi]
    zp = device_at(x, y, 1 - z, zh, c)
    greet(xs + ys + [zp])
    copies = []

    def post(src, dst, peer):
        k = len(copies)
        copies.append(send(src, dst, ssem.at[k], rsem.at[k], peer))
        return copies[k]

    got_a, got_b = [], []
    for j in range(3):
        got_a.append(post(da.at[xi[j]], rda.at[j], xs[j]))
        got_a.append(post(ca, rca.at[j], xs[j]))
        got_b.append(post(db.at[yi[j]], rdb.at[j], ys[j]))
        got_b.append(post(gb.at[yi[j]], rgb.at[j], ys[j]))
        got_b.append(post(cb, rcb.at[j], ys[j]))
    for copy in got_a:
        copy.wait_recv()

    def rows_a(t, carry):
        cols = pl.ds(pl.multiple_of(t * TILE_A, TILE_A), TILE_A)
        out = nn(da[x], ca[:, cols])
        for j in range(3):
            out = out + nn(rda[j], rca[j, :, cols])
        pa[:, :, :, cols] = out.reshape(2, 4, SHARE, TILE_A).astype(BF)
        return carry

    lax.fori_loop(0, COLS_A // TILE_A, rows_a, 0)
    two_a = [post(pa.at[:, yi[j]], r2a.at[j], ys[j]) for j in range(3)]
    for copy in got_b:
        copy.wait_recv()
    for which in range(3):

        def rows_b(t, carry):
            cols = pl.ds(pl.multiple_of(t * TILE_B, TILE_B), TILE_B)
            out = nn(db[y, which], cb[:, cols])
            for j in range(3):
                out = out + nn(rdb[j, which], rcb[j, :, cols])
            pb[:, :, :, cols] = out.reshape(2, 4, SHARE, TILE_B).astype(BF)
            return carry

        lax.fori_loop(*SPANS_B[which], rows_b, 0)
    gains = gb[y].astype(F32)
    for j in range(3):
        gains = gains + rgb[j].astype(F32)
    pb[:, :, :, COLS_B:] = gains.reshape(2, 4, SHARE, 128).astype(BF)
    two_b = [post(pb.at[:, xi[j]], r2b.at[j], xs[j]) for j in range(3)]

    for copy in two_a:
        copy.wait_recv()

    def adds_a(t, carry):
        cols = pl.ds(pl.multiple_of(t * TILE_A, TILE_A), TILE_A)
        for zi in range(2):
            out = pa[zi, y, :, cols].astype(F32)
            for j in range(3):
                out = out + r2a[j, zi, :, cols].astype(F32)
            sa[zi, :, cols] = out.astype(BF)
        return carry

    lax.fori_loop(0, COLS_A // TILE_A, adds_a, 0)
    three_a = post(sa.at[1 - z], r3a, zp)
    for copy in two_b:
        copy.wait_recv()

    def adds_b(t, carry):
        cols = pl.ds(pl.multiple_of(t * 128, 128), 128)
        for zi in range(2):
            out = pb[zi, x, :, cols].astype(F32)
            for j in range(3):
                out = out + r2b[j, zi, :, cols].astype(F32)
            sb[zi, :, cols] = out.astype(BF)
        return carry

    lax.fori_loop(0, COLS_G // 128, adds_b, 0)
    three_b = post(sb.at[1 - z], r3b, zp)
    three_a.wait_recv()
    oa[...] = sa[z].astype(F32) + r3a[...].astype(F32)
    three_b.wait_recv()
    ob[...] = sb[z].astype(F32) + r3b[...].astype(F32)
    for copy in copies:
        copy.wait_send()


def grads(da, ca, db, gb, cb):
    return pl.pallas_call(
        grads_kernel,
        out_shape=(
            jax.ShapeDtypeStruct((SHARE, COLS_A), F32),
            jax.ShapeDtypeStruct((SHARE, COLS_G), F32),
        ),
        in_specs=[whole()] * 5,
        out_specs=(whole(), whole()),
        scratch_shapes=[
            VMEM((3,) + da.shape[1:], BF),
            VMEM((3,) + ca.shape, BF),
            VMEM((3,) + db.shape[1:], BF),
            VMEM((3,) + gb.shape[1:], BF),
            VMEM((3,) + cb.shape, BF),
            VMEM((2, 4, SHARE, COLS_A), BF),
            VMEM((2, 4, SHARE, COLS_G), BF),
            VMEM((3, 2, SHARE, COLS_A), BF),
            VMEM((3, 2, SHARE, COLS_G), BF),
            VMEM((2, SHARE, COLS_A), BF),
            VMEM((2, SHARE, COLS_G), BF),
            VMEM((SHARE, COLS_A), BF),
            VMEM((SHARE, COLS_G), BF),
            pltpu.SemaphoreType.DMA((23,)),
            pltpu.SemaphoreType.DMA((23,)),
        ],
        compiler_params=params(3, 62),
    )(da, ca, db, gb, cb)


def rows_for_x(left):
    t = left.T.reshape(2, 4, 4, SHARE, left.shape[0])
    return t.transpose(2, 0, 1, 3, 4).reshape(4, PART, left.shape[0])


def rows_for_y(left):
    t = left.T.reshape(2, 4, 4, SHARE, left.shape[0])
    return t.transpose(1, 0, 2, 3, 4).reshape(4, PART, left.shape[0])


def sliced(codes, bits):
    if bits == 8:
        return codes
    spacing = 2.0 ** (8 - bits)
    upper = 2.0 ** (bits - 1)
    wide = codes.astype(F32)
    return (jnp.clip(jnp.floor(wide / spacing + 0.5), -upper, upper - 1.0) * spacing).astype(BF)


def norm_rows(values, gain):
    return values * lax.rsqrt(jnp.mean(values * values, axis=-1, keepdims=True) + EPS) * gain


def norm_back(values, gain, grad):
    q = lax.rsqrt(jnp.mean(values * values, axis=-1, keepdims=True) + EPS)
    lifted = grad * gain
    back = q * lifted - values * (q * q * q) * jnp.mean(lifted * values, axis=-1, keepdims=True)
    return back, jnp.sum(grad * values * q, axis=(0, 1))


def rotate(values, cosine, sine):
    half = values.shape[-1] // 2
    first = values[..., :half]
    second = values[..., half:]
    return jnp.concatenate(
        [first * cosine - second * sine, second * cosine + first * sine], axis=-1
    )


def gelu_mix(gate, upper):
    return jax.nn.gelu(gate, approximate=True) * upper


def shards(
    inputs,
    out_grad,
    segment_ids,
    keep_mask,
    query_codes,
    key_codes,
    value_codes,
    output_codes,
    gate_codes,
    up_codes,
    down_codes,
    norm_attn_in,
    norm_attn_out,
    norm_ffn_in,
    norm_ffn_out,
):
    rows = inputs.shape[1]
    place = lax.axis_index("blk") * rows + jnp.arange(rows, dtype=jnp.int32)
    freqs = 10000.0 ** (-jnp.arange(HD // 2, dtype=F32) * 2.0 / HD)
    angles = place.astype(F32)[:, None] * freqs[None, :]
    cosine = jnp.cos(angles)
    sine = jnp.sin(angles)
    in_scale = LEVEL_SCALE * D ** (-0.5)
    mid_scale = LEVEL_SCALE * (HEADS * HD) ** (-0.5)
    ff_scale = LEVEL_SCALE * FF ** (-0.5)

    def by_batch(left, codes, scale, back=False):
        parts = []
        for m in range(2):
            weight = sliced(codes, WIDTHS[m])
            parts.append((nt if back else nn)(left[m], weight) * scale)
        return jnp.stack(parts)

    tokens = inputs.astype(F32)
    normed = norm_rows(tokens, norm_attn_in).astype(BF)
    q_raw = by_batch(normed, query_codes, in_scale).reshape(2, rows, 2, HD).transpose(0, 2, 1, 3)
    queries = rotate(q_raw, cosine, sine).astype(BF).reshape(2, 2 * rows, HD)
    key_own = rotate(by_batch(normed, key_codes, in_scale), cosine, sine).astype(BF)
    value_own = by_batch(normed, value_codes, in_scale).astype(BF)
    key_tag = jnp.where(keep_mask == 1, segment_ids, -1).astype(BF).reshape(1, 2 * rows)
    packed = jnp.concatenate(
        [key_own.reshape(2 * rows, HD), jnp.broadcast_to(key_tag, (16, 2 * rows))], axis=0
    )
    keys, values = gather(packed, value_own.reshape(2 * rows, HD))
    keys = keys.reshape(32, 2 * rows + 16, HD)
    values = values.reshape(32, 2 * rows, HD)
    tag = segment_ids.astype(F32)
    tag = jnp.concatenate([tag, tag], axis=1)[:, :, None]
    attended, lse = attend(queries, tag, keys, values)

    def flat(heads):
        return heads.reshape(2, 2, rows, HD).transpose(0, 2, 1, 3).reshape(2, rows, 2 * HD)

    def headed(wide):
        return wide.reshape(2, rows, 2, HD).transpose(0, 2, 1, 3).reshape(2, 2 * rows, HD)

    attended_flat = flat(attended).astype(BF)
    branch = total(by_batch(attended_flat, output_codes, mid_scale).astype(BF), 4).astype(F32)
    middle = tokens + norm_rows(branch, norm_attn_out)
    ffn_in = norm_rows(middle, norm_ffn_in).astype(BF)
    gate = by_batch(ffn_in, gate_codes, in_scale)
    upper = by_batch(ffn_in, up_codes, in_scale)
    hidden = gelu_mix(gate, upper).astype(BF)
    down = total(by_batch(hidden, down_codes, ff_scale).astype(BF), 5).astype(F32)
    out_rows = (middle + norm_rows(down, norm_ffn_out)).astype(BF)

    upstream = out_grad.astype(F32)
    down_grad, gain_ffn_out = norm_back(down, norm_ffn_out, upstream)
    down_low = down_grad.astype(BF)
    hidden_grad = by_batch(down_low, down_codes, ff_scale, True)
    gate_grad, up_grad = jax.vjp(gelu_mix, gate, upper)[1](hidden_grad)
    gate_low = gate_grad.astype(BF)
    up_low = up_grad.astype(BF)
    ffn_in_grad = total(
        (
            by_batch(gate_low, gate_codes, in_scale, True)
            + by_batch(up_low, up_codes, in_scale, True)
        ).astype(BF),
        6,
    ).astype(F32)
    middle_part, gain_ffn_in = norm_back(middle, norm_ffn_in, ffn_in_grad)
    middle_grad = upstream + middle_part
    branch_grad, gain_attn_out = norm_back(branch, norm_attn_out, middle_grad)
    branch_low = branch_grad.astype(BF)
    attended_grad = headed(by_batch(branch_low, output_codes, mid_scale, True).astype(BF))
    offset = jnp.sum(attended_grad.astype(F32) * attended, axis=-1, keepdims=True)
    query_rot, key_part, value_part = attend_back(
        queries, attended_grad, lse, offset, tag, keys, values
    )
    box = (2, 4, 4, 2 * rows, HD)
    key_rot, value_grad = scatter(key_part.reshape(box), value_part.reshape(box))
    key_low = rotate(key_rot.reshape(2, rows, HD), cosine, -sine).astype(BF)
    value_low = value_grad.reshape(2, rows, HD).astype(BF)
    query_low = rotate(query_rot.reshape(2, 2, rows, HD), cosine, -sine)
    query_low = flat(query_low.reshape(2, 2 * rows, HD)).astype(BF)
    normed_grad = total(
        (
            by_batch(query_low, query_codes, in_scale, True)
            + by_batch(key_low, key_codes, in_scale, True)
            + by_batch(value_low, value_codes, in_scale, True)
        ).astype(BF),
        7,
    ).astype(F32)
    token_part, gain_attn_in = norm_back(tokens, norm_attn_in, normed_grad)
    input_grad = (middle_grad + token_part).astype(BF)

    def both(left):
        return left.reshape(2 * rows, left.shape[-1])

    gains = jnp.stack([gain_attn_in, gain_attn_out, gain_ffn_in, gain_ffn_out]).astype(BF)
    gains = jnp.concatenate([gains, jnp.zeros((124, D), BF)])
    da = rows_for_x(both(ffn_in))
    ca = jnp.concatenate([both(gate_low), both(up_low)], axis=1)
    db = jnp.stack([rows_for_y(both(v)) for v in (down_low, normed, branch_low)], axis=1)
    cb = jnp.concatenate(
        [both(hidden), both(query_low), both(key_low), both(value_low), both(attended_flat)], axis=1
    )
    ga, gb = grads(da, ca, db, rows_for_y(gains), cb)
    g_down = gb[:, :2304].T * ff_scale
    g_query = gb[:, 2304:2816] * in_scale
    g_key = gb[:, 2816:3072] * in_scale
    g_value = gb[:, 3072:3328] * in_scale
    g_output = gb[:, 3328:3840].T * mid_scale
    return (
        out_rows,
        input_grad,
        g_query,
        g_key,
        g_value,
        g_output,
        ga[:, :2304] * in_scale,
        ga[:, 2304:] * in_scale,
        g_down,
        gb[:, 3840],
        gb[:, 3841],
        gb[:, 3842],
        gb[:, 3843],
    )


def solution(mesh):
    placed = (
        P(None, "blk", None),
        P(None, "blk", None),
        P(None, "blk"),
        P(None, "blk"),
        P(None, "tensor"),
        P(None, "tensor"),
        P(None, "tensor"),
        P("tensor", None),
        P(None, "tensor"),
        P(None, "tensor"),
        P("tensor", None),
        P(),
        P(),
        P(),
        P(),
    )
    return jax.shard_map(
        shards,
        mesh=mesh,
        in_specs=placed,
        out_specs=(
            P(None, "blk", None),
            P(None, "blk", None),
            P("blk", "tensor"),
            P("blk", "tensor"),
            P("blk", "tensor"),
            P("tensor", "blk"),
            P("blk", "tensor"),
            P("blk", "tensor"),
            P("tensor", "blk"),
            P("blk"),
            P("blk"),
            P("blk"),
            P("blk"),
        ),
        check_vma=False,
    )
```

```python
import functools

import jax
import jax.numpy as jnp
from jax import lax
from jax.experimental import pallas as pl
from jax.experimental.pallas import tpu as pltpu
from jax.sharding import PartitionSpec as P

D = 2304
HEADS = 8
HD = 256
FF = 9216

CAP = 50.0
EPS = 1e-06
LEVEL_SCALE = 1.0 / 74.0
WIDTHS = (8, 4, 2)

MESH = pl.DeviceIdType.MESH
VMEM = pltpu.VMEM
BF = jnp.bfloat16
F32 = jnp.float32
SEQ = 4096
ROWS = 128
TAGROW = 256
MASKED = -2.0


def place_of():
    b = lax.axis_index("blk")
    t = lax.axis_index("tensor")
    return b % 4, (b // 4) % 4, b // 16, t // 2, t % 2


def device_at(x, y, z, zh, c):
    return ((z * 4 + y) * 4 + x, zh * 2 + c)


def greet(peers):
    barrier = pltpu.get_barrier_semaphore()
    for peer in peers:
        pl.semaphore_signal(barrier, inc=1, device_id=peer, device_id_type=MESH)
    pl.semaphore_wait(barrier, len(peers))


def send(src, dst, ssem, rsem, peer):
    copy = pltpu.make_async_remote_copy(
        src_ref=src, dst_ref=dst, send_sem=ssem, recv_sem=rsem, device_id=peer, device_id_type=MESH
    )
    copy.start()
    return copy


def params(collective_id=None, limit=60):
    if collective_id is None:
        return pltpu.CompilerParams(vmem_limit_bytes=limit << 20)
    return pltpu.CompilerParams(
        vmem_limit_bytes=limit << 20, collective_id=collective_id, has_side_effects=True
    )


def whole(space=VMEM):
    return pl.BlockSpec(memory_space=space)


def gather_kernel(a_ref, b_ref, oa, ob, lsem, ssem, rsem):
    x, y, z, zh, c = place_of()
    xs = [device_at((x + j) % 4, y, z, zh, c) for j in (1, 2, 3)]
    ys = [device_at(x, (y + j) % 4, z, zh, c) for j in (1, 2, 3)]
    zp = device_at(x, y, 1 - z, zh, c)
    greet(xs + ys + [zp])
    mine_a = pltpu.make_async_copy(a_ref, oa.at[z, y, x], lsem.at[0])
    mine_b = pltpu.make_async_copy(b_ref, ob.at[z, y, x], lsem.at[1])
    mine_a.start()
    mine_b.start()
    za = send(a_ref, oa.at[z, y, x], ssem.at[0], rsem.at[0], zp)
    zb = send(b_ref, ob.at[z, y, x], ssem.at[1], rsem.at[1], zp)
    done = [za, zb]
    first_a = [send(a_ref, oa.at[z, y, x], ssem.at[2 + j], rsem.at[2 + j], xs[j]) for j in range(3)]
    first_b = [send(b_ref, ob.at[z, y, x], ssem.at[5 + j], rsem.at[5 + j], ys[j]) for j in range(3)]
    za.wait_recv()
    other = 1 - z
    next_a = [
        send(oa.at[other, y, x], oa.at[other, y, x], ssem.at[8 + j], rsem.at[8 + j], xs[j])
        for j in range(3)
    ]
    zb.wait_recv()
    next_b = [
        send(ob.at[other, y, x], ob.at[other, y, x], ssem.at[11 + j], rsem.at[11 + j], ys[j])
        for j in range(3)
    ]
    mine_a.wait()
    mine_b.wait()
    last = []
    for step, (level, copies_a, copies_b) in enumerate(((z, first_a, first_b), (other, next_a, next_b))):
        for copy in copies_a:
            copy.wait_recv()
        for j in range(3):
            k = 14 + 6 * step + j
            last.append(send(oa.at[level, y], oa.at[level, y], ssem.at[k], rsem.at[k], ys[j]))
        for copy in copies_b:
            copy.wait_recv()
        for j in range(3):
            k = 17 + 6 * step + j
            last.append(send(ob.at[level, :, x], ob.at[level, :, x], ssem.at[k], rsem.at[k], xs[j]))
    for copy in last:
        copy.wait_recv()
    for copy in done + first_a + first_b + next_a + next_b + last:
        copy.wait_send()


def gather(a, b):
    return pl.pallas_call(
        gather_kernel,
        out_shape=(
            jax.ShapeDtypeStruct((2, 4, 4) + a.shape, a.dtype),
            jax.ShapeDtypeStruct((2, 4, 4) + b.shape, b.dtype),
        ),
        in_specs=[whole(), whole()],
        out_specs=(whole(), whole()),
        scratch_shapes=[
            pltpu.SemaphoreType.DMA((2,)),
            pltpu.SemaphoreType.DMA((26,)),
            pltpu.SemaphoreType.DMA((26,)),
        ],
        compiler_params=params(1, 30),
    )(a, b)


PIECES = 4


def total_kernel(kinds, *refs):
    n = len(kinds)
    p_ref, extras = refs[0], refs[1 : 1 + n]
    o_ref, lands = refs[1 + n], refs[2 + n : 2 + 2 * n]
    r1, h, r2, lsem, ssem, rsem = refs[2 + 2 * n :]
    x, y, z, zh, c = place_of()
    peers = {
        "x": [((x + j) % 4, device_at((x + j) % 4, y, z, zh, c)) for j in (1, 2, 3)],
        "y": [((y + j) % 4, device_at(x, (y + j) % 4, z, zh, c)) for j in (1, 2, 3)],
    }
    mine = {"x": x, "y": y}
    mate = device_at(x, y, z, zh, 1 - c)
    far = device_at(x, y, z, 1 - zh, c)
    axes = sorted({axis for _, axis in kinds})
    greet([mate, far] + [device for axis in axes for _, device in peers[axis]])
    size = p_ref.shape[1] // PIECES
    rows = [pl.ds(k * size, size) for k in range(PIECES)]
    one = [
        send(p_ref.at[1 - c, rows[k]], r1.at[rows[k]], ssem.at[k], rsem.at[k], mate)
        for k in range(PIECES)
    ]
    carried, kept = [], []
    for e, (kind, axis) in enumerate(kinds):
        band = pl.ds(pl.multiple_of(mine[axis] * 256, 256), 256)
        land = lands[e].at[:, band] if kind == "swap" else lands[e].at[band]
        for j, (place, device) in enumerate(peers[axis]):
            i = 3 * PIECES + 3 * e + j
            src = extras[e].at[place] if kind == "swap" else extras[e]
            carried.append(send(src, land, ssem.at[i], rsem.at[i], device))
        own = extras[e].at[mine[axis]] if kind == "swap" else extras[e]
        copy = pltpu.make_async_copy(own, land, lsem.at[e])
        copy.start()
        kept.append(copy)
    two, three = [], []
    for k in range(PIECES):
        one[k].wait_recv()
        h[rows[k]] = (p_ref[c, rows[k]].astype(F32) + r1[rows[k]].astype(F32)).astype(BF)
        i = PIECES + k
        two.append(send(h.at[rows[k]], r2.at[rows[k]], ssem.at[i], rsem.at[i], far))
    for k in range(PIECES):
        two[k].wait_recv()
        o_ref[c, rows[k]] = (h[rows[k]].astype(F32) + r2[rows[k]].astype(F32)).astype(BF)
        i = 2 * PIECES + k
        three.append(send(o_ref.at[c, rows[k]], o_ref.at[c, rows[k]], ssem.at[i], rsem.at[i], mate))
    for copy in three + carried:
        copy.wait_recv()
    for copy in one + two + three + carried:
        copy.wait_send()
    for copy in kept:
        copy.wait()


def total(p, collective_id, carry=()):
    half = p.shape[1:]
    kinds = tuple((kind, axis) for kind, axis, _ in carry)
    extras = [array for _, _, array in carry]
    lands = [
        jax.ShapeDtypeStruct((PART, 1024) if kind == "swap" else (1024, array.shape[1]), BF)
        for kind, _, array in carry
    ]
    sems = 3 * PIECES + 3 * len(carry)
    out = pl.pallas_call(
        functools.partial(total_kernel, kinds),
        out_shape=[jax.ShapeDtypeStruct(p.shape, BF)] + lands,
        in_specs=[whole()] + [whole(pl.ANY)] * len(carry),
        out_specs=[whole()] + [whole(pl.ANY)] * len(carry),
        scratch_shapes=[
            VMEM(half, BF),
            VMEM(half, BF),
            VMEM(half, BF),
            pltpu.SemaphoreType.DMA((max(1, len(carry)),)),
            pltpu.SemaphoreType.DMA((sems,)),
            pltpu.SemaphoreType.DMA((sems,)),
        ],
        compiler_params=params(collective_id, 30),
        cost_estimate=pl.CostEstimate(flops=1000, bytes_accessed=1000, transcendentals=0),
    )(p, *extras)
    return out[0], out[1:]


CHUNK = 4
KEYS = CHUNK * ROWS


def nt(left, right):
    return lax.dot_general(left, right, (((1,), (1,)), ((), ())), preferred_element_type=F32)


def tn(left, right):
    return lax.dot_general(left, right, (((0,), (0,)), ((), ())), preferred_element_type=F32)


def nn(left, right):
    return jnp.dot(left, right, preferred_element_type=F32)


def load_chunk(k_ref, v_ref, step, m):
    blocks = pl.ds(step * CHUNK, CHUNK)
    keys = k_ref[blocks, m * ROWS : (m + 1) * ROWS, :].reshape(KEYS, HD)
    values = v_ref[blocks, m * ROWS : (m + 1) * ROWS, :].reshape(KEYS, HD)
    tags = k_ref[blocks, TAGROW : TAGROW + 16, m * ROWS : (m + 1) * ROWS].astype(F32)
    tag_row = jnp.concatenate([tags[i, 0:1, :] for i in range(CHUNK)], axis=1)
    return keys, values, tag_row


def allowed(step, tag_row, query_tag, query_place):
    key_place = step * KEYS + lax.broadcasted_iota(jnp.int32, (2 * ROWS, KEYS), 1)
    ok = (key_place <= query_place) & (tag_row == query_tag)
    return ok | (key_place == query_place)


def query_places():
    row = lax.broadcasted_iota(jnp.int32, (2 * ROWS, 1), 0)
    return lax.axis_index("blk") * ROWS + row % ROWS


def attend_kernel(q_ref, t_ref, k_ref, v_ref, o_ref, lse_ref):
    limit = lax.axis_index("blk") // CHUNK + 1
    where = query_places()
    for m in range(2):
        q = q_ref[m]
        tag = t_ref[m]

        def step(i, carry):
            acc, mass = carry
            keys, values, tag_row = load_chunk(k_ref, v_ref, i, m)
            bent = jnp.tanh(nt(q, keys) * (HD ** (-0.5) / CAP))
            e = jnp.where(allowed(i, tag_row, tag, where), jnp.exp(CAP * bent), 0.0)
            mass = mass + jnp.sum(e, axis=-1, keepdims=True)
            return acc + nn(e.astype(BF), values), mass

        acc, mass = lax.fori_loop(
            0, limit, step, (jnp.zeros((2 * ROWS, HD), F32), jnp.zeros((2 * ROWS, 1), F32))
        )
        o_ref[m] = acc / mass
        lse_ref[m] = jnp.log(mass)


def attend(q, tag, k, v):
    return pl.pallas_call(
        attend_kernel,
        out_shape=(
            jax.ShapeDtypeStruct((2, 2 * ROWS, HD), F32),
            jax.ShapeDtypeStruct((2, 2 * ROWS, 1), F32),
        ),
        in_specs=[whole()] * 4,
        out_specs=(whole(), whole()),
        compiler_params=params(None, 40),
    )(q, tag, k, v)


FTILE = 256
ROOT = (2.0 / 3.141592653589793) ** 0.5
CUBE = 0.044715


def narrow(codes):
    level = codes * BF(1.0 / 16.0) + BF(1.0 / 32.0)
    level = (level + BF(192.0)) - BF(192.0)
    return jnp.minimum(level, BF(7.0)) * BF(16.0)


def ffn_kernel(x_ref, wg_ref, wu_ref, wd_ref, gate_ref, up_ref, hid_ref, down_ref, acc, scale_in, scale_out):
    i = pl.program_id(0)

    @pl.when(i == 0)
    def _():
        acc[...] = jnp.zeros_like(acc)

    for m in range(2):
        wg, wu, wd = wg_ref[...], wu_ref[...], wd_ref[...]
        if m == 1:
            wg, wu, wd = narrow(wg), narrow(wu), narrow(wd)
        gate = nn(x_ref[m], wg) * scale_in
        up = nn(x_ref[m], wu) * scale_in
        gate_ref[m] = gate
        up_ref[m] = up
        bent = jnp.tanh(ROOT * (gate + CUBE * gate * gate * gate))
        hidden = (0.5 * gate * (1.0 + bent) * up).astype(BF)
        hid_ref[m] = hidden
        acc[m] += nn(hidden, wd)

    @pl.when(i == pl.num_programs(0) - 1)
    def _():
        down_ref[...] = (acc[...] * scale_out).astype(BF)


def ffn(x, wg, wu, wd, scale_in, scale_out):
    def kernel(x_ref, wg_ref, wu_ref, wd_ref, gate_ref, up_ref, hid_ref, down_ref, acc):
        ffn_kernel(x_ref, wg_ref, wu_ref, wd_ref, gate_ref, up_ref, hid_ref, down_ref, acc, scale_in, scale_out)

    full = pl.BlockSpec((2, ROWS, D), lambda i: (0, 0, 0))
    wide = pl.BlockSpec((2, ROWS, FTILE), lambda i: (0, 0, i))
    width = wg.shape[1]
    return pl.pallas_call(
        kernel,
        grid=(width // FTILE,),
        out_shape=(
            jax.ShapeDtypeStruct((2, ROWS, width), F32),
            jax.ShapeDtypeStruct((2, ROWS, width), F32),
            jax.ShapeDtypeStruct((2, ROWS, width), BF),
            jax.ShapeDtypeStruct((2, ROWS, D), BF),
        ),
        in_specs=[
            full,
            pl.BlockSpec((D, FTILE), lambda i: (0, i)),
            pl.BlockSpec((D, FTILE), lambda i: (0, i)),
            pl.BlockSpec((FTILE, D), lambda i: (i, 0)),
        ],
        out_specs=(wide, wide, wide, full),
        scratch_shapes=[VMEM((2, ROWS, D), F32)],
        compiler_params=params(None, 40),
        cost_estimate=pl.CostEstimate(flops=1000, bytes_accessed=1000, transcendentals=0),
    )(x, wg, wu, wd)


def ffn_back(g, gate, up, wg, wu, wd, scale_in, scale_out):
    def kernel(g_ref, gate_ref, up_ref, wg_ref, wu_ref, wd_ref, dgate_ref, dup_ref, dx_ref, acc):
        i = pl.program_id(0)

        @pl.when(i == 0)
        def _():
            acc[...] = jnp.zeros_like(acc)

        for m in range(2):
            wg, wu, wd = wg_ref[...], wu_ref[...], wd_ref[...]
            if m == 1:
                wg, wu, wd = narrow(wg), narrow(wu), narrow(wd)
            grad = nt(g_ref[m], wd) * scale_out
            v, u = gate_ref[m], up_ref[m]
            bent = jnp.tanh(ROOT * (v + CUBE * v * v * v))
            half = 0.5 * (1.0 + bent)
            slope = half + 0.5 * v * (1.0 - bent * bent) * (ROOT * (1.0 + 3.0 * CUBE * v * v))
            dgate = (grad * u * slope).astype(BF)
            dup = (grad * (v * half)).astype(BF)
            dgate_ref[m] = dgate
            dup_ref[m] = dup
            acc[m] += nt(dgate, wg) + nt(dup, wu)

        @pl.when(i == pl.num_programs(0) - 1)
        def _():
            dx_ref[...] = (acc[...] * scale_in).astype(BF)

    full = pl.BlockSpec((2, ROWS, D), lambda i: (0, 0, 0))
    wide = pl.BlockSpec((2, ROWS, FTILE), lambda i: (0, 0, i))
    width = wg.shape[1]
    return pl.pallas_call(
        kernel,
        grid=(width // FTILE,),
        out_shape=(
            jax.ShapeDtypeStruct((2, ROWS, width), BF),
            jax.ShapeDtypeStruct((2, ROWS, width), BF),
            jax.ShapeDtypeStruct((2, ROWS, D), BF),
        ),
        in_specs=[
            full,
            wide,
            wide,
            pl.BlockSpec((D, FTILE), lambda i: (0, i)),
            pl.BlockSpec((D, FTILE), lambda i: (0, i)),
            pl.BlockSpec((FTILE, D), lambda i: (i, 0)),
        ],
        out_specs=(wide, wide, full),
        scratch_shapes=[VMEM((2, ROWS, D), F32)],
        compiler_params=params(None, 40),
        cost_estimate=pl.CostEstimate(flops=1000, bytes_accessed=1000, transcendentals=0),
    )(g, gate, up, wg, wu, wd)


PART = 576
SHARE = 72


def poster(ssem, rsem, copies):
    def post(src, dst, peer):
        k = len(copies)
        copies.append(send(src, dst, ssem.at[k], rsem.at[k], peer))
        return copies[k]

    return post


def total_start(post, p_ref, r1, rows, c, mate):
    return [post(p_ref.at[1 - c, r], r1.at[r], mate) for r in rows]


def total_across(post, p_ref, r1, h, r2, rows, c, far, one):
    two = []
    for k, r in enumerate(rows):
        one[k].wait_recv()
        h[r] = (p_ref[c, r].astype(F32) + r1[r].astype(F32)).astype(BF)
        two.append(post(h.at[r], r2.at[r], far))
    return two


def total_end(post, o_ref, h, r2, rows, c, mate, two):
    three = []
    for k, r in enumerate(rows):
        two[k].wait_recv()
        o_ref[c, r] = (h[r].astype(F32) + r2[r].astype(F32)).astype(BF)
        three.append(post(o_ref.at[c, r], o_ref.at[c, r], mate))
    for copy in three:
        copy.wait_recv()


def piece_rows():
    size = ROWS // PIECES
    return [pl.ds(k * size, size) for k in range(PIECES)]


def norm_grad(v, gain, grad):
    q = lax.rsqrt(jnp.mean(v * v, axis=-1, keepdims=True) + EPS)
    lifted = grad * gain
    back = q * lifted - v * (q * q * q * jnp.mean(lifted * v, axis=-1, keepdims=True))
    return back, jnp.sum(grad * v * q, axis=0, keepdims=True)


def mid_kernel(
    part, gain_mid, gain_out, q_ref, lse_ref, tag_ref, att_ref,
    middle_in, branch_in, up_in, wo_in, k_in, v_in, cg_own, cu_own, ch_own, da, dd,
    key_out, value_out, dq_ref, mgrad, bt, gains, cg, cu, ch, dg_land, dd_land,
    middle, branch, upstream, wo, k_ref, v_ref, blow, g_ref, dk, dv,
    t1, th, t2, total_ref, r1a, r1b, s1a, s1b, r2a, r2b, s2a, s2b, r3a, r3b,
    lsem, ssem, rsem,
    scale,
):
    x, y, z, zh, c = place_of()
    xi = [(x + j) % 4 for j in (1, 2, 3)]
    yi = [(y + j) % 4 for j in (1, 2, 3)]
    xs = [device_at(i, y, z, zh, c) for i in xi]
    ys = [device_at(x, i, z, zh, c) for i in yi]
    zp = device_at(x, y, 1 - z, zh, c)
    mate = device_at(x, y, z, zh, 1 - c)
    far = device_at(x, y, z, 1 - zh, c)
    copies, local = [], []
    post = poster(ssem, rsem, copies)

    def load(src, dst):
        copy = pltpu.make_async_copy(src, dst, lsem.at[len(local)])
        copy.start()
        local.append(copy)
        return copy

    loads = [
        load(*pair)
        for pair in (
            (middle_in, middle), (branch_in, branch), (up_in, upstream), (wo_in, wo), (k_in, k_ref), (v_in, v_ref),
        )
    ]
    greet(xs + ys + [zp, mate, far])
    rows = piece_rows()
    one = total_start(post, part, t1, rows, c, mate)
    band_x = pl.ds(pl.multiple_of(x * 256, 256), 256)
    band_y = pl.ds(pl.multiple_of(y * 256, 256), 256)
    for j in (0, 2, 1):
        post(da.at[xi[j]], dg_land.at[:, band_x], xs[j])
        post(dd.at[yi[j]], dd_land.at[:, band_y], ys[j])
    for j in (0, 2, 1):
        post(cg_own, cg.at[band_x], xs[j])
        post(ch_own, ch.at[band_y], ys[j])
    for j in (0, 2, 1):
        post(cu_own, cu.at[band_x], xs[j])
    carried = copies[len(one) :]
    for pair in (
        (da.at[x], dg_land.at[:, band_x]), (dd.at[y], dd_land.at[:, band_y]),
        (cg_own, cg.at[band_x]), (cu_own, cu.at[band_x]), (ch_own, ch.at[band_y]),
    ):
        load(*pair)
    two = total_across(post, part, t1, th, t2, rows, c, far, one)
    total_end(post, total_ref, th, t2, rows, c, mate, two)
    for copy in loads[:4]:
        copy.wait()

    zero = jnp.zeros((1, D), F32)
    for m in range(2):

        def slab(i, carry):
            sum_mid, sum_out = carry
            r = pl.ds(pl.multiple_of(i * 16, 16), 16)
            back, more = norm_grad(middle[m, r], gain_mid[...], total_ref[m, r].astype(F32))
            grad = upstream[m, r].astype(F32) + back
            mgrad[m, r] = grad
            back, most = norm_grad(branch[m, r].astype(F32), gain_out[...], grad)
            blow[m, r] = back.astype(BF)
            return sum_mid + more, sum_out + most

        sums = lax.fori_loop(0, ROWS // 16, slab, (zero, zero) if m == 0 else sums)
    gains[0:1] = sums[1]
    gains[1:2] = sums[0]
    for m in range(2):
        weight = wo[...] if m == 0 else narrow(wo[...])
        wide = (nt(blow[m], weight) * scale).astype(BF)
        g_ref[m, :ROWS] = wide[:, :HD]
        g_ref[m, ROWS:] = wide[:, HD:]
        turned = blow[m].T
        for zi in range(2):
            for k in range(4):
                at = (zi * 4 + k) * 288
                bt[zi, k, :, m * ROWS : (m + 1) * ROWS] = turned[at : at + 288]

    loads[4].wait()
    loads[5].wait()
    limit = lax.axis_index("blk") // CHUNK + 1
    where = query_places()
    for m in range(2):
        q = q_ref[m]
        g = g_ref[m]
        tag = tag_ref[m]
        lse = lse_ref[m]
        off = jnp.sum(g.astype(F32) * att_ref[m], axis=-1, keepdims=True)
        span = slice(m * ROWS, (m + 1) * ROWS)

        def step(i, dq):
            keys, values, tag_row = load_chunk(k_ref, v_ref, i, m)
            bent = jnp.tanh(nt(q, keys) * (HD ** (-0.5) / CAP))
            p = jnp.where(allowed(i, tag_row, tag, where), jnp.exp(CAP * bent - lse), 0.0)
            dp = nt(g, values)
            ds = (p * (dp - off) * (1.0 - bent * bent) * HD ** (-0.5)).astype(BF)
            dk[i // 4, i % 4, :, span, :] = tn(ds, q).astype(BF).reshape(CHUNK, ROWS, HD)
            dv[i // 4, i % 4, :, span, :] = tn(p.astype(BF), g).astype(BF).reshape(CHUNK, ROWS, HD)
            return dq + nn(ds, keys)

        dq_ref[m] = lax.fori_loop(0, limit, step, jnp.zeros((2 * ROWS, HD), F32))

        def blank(i, carry):
            dk[i // 4, i % 4, :, span, :] = jnp.zeros((CHUNK, ROWS, HD), BF)
            dv[i // 4, i % 4, :, span, :] = jnp.zeros((CHUNK, ROWS, HD), BF)
            return carry

        lax.fori_loop(limit, SEQ // KEYS, blank, 0)

    one_a = [post(dk.at[:, :, xi[j]], r1a.at[j], xs[j]) for j in range(3)]
    one_b = [post(dv.at[:, yi[j]], r1b.at[j], ys[j]) for j in range(3)]
    for copy in one_a:
        copy.wait_recv()

    def add_a(i, carry):
        zi, k = i // 4, i % 4
        out = dk[zi, k, x].astype(F32)
        for j in range(3):
            out = out + r1a[j, zi, k].astype(F32)
        s1a[zi, k] = out.astype(BF)
        return carry

    lax.fori_loop(0, 8, add_a, 0)
    two_a = [post(s1a.at[:, yi[j]], r2a.at[j], ys[j]) for j in range(3)]
    for copy in one_b:
        copy.wait_recv()

    def add_b(i, carry):
        zi, k = i // 4, i % 4
        out = dv[zi, y, k].astype(F32)
        for j in range(3):
            out = out + r1b[j, zi, k].astype(F32)
        s1b[zi, k] = out.astype(BF)
        return carry

    lax.fori_loop(0, 8, add_b, 0)
    two_b = [post(s1b.at[:, xi[j]], r2b.at[j], xs[j]) for j in range(3)]

    def second(arrivals, own, mine, land, half):
        for copy in arrivals:
            copy.wait_recv()
        for zi in range(2):
            out = own[zi, mine].astype(F32)
            for j in range(3):
                out = out + land[j, zi].astype(F32)
            half[zi] = out.astype(BF)

    second(two_a, s1a, y, r2a, s2a)
    three_a = post(s2a.at[1 - z], r3a, zp)
    second(two_b, s1b, x, r2b, s2b)
    three_b = post(s2b.at[1 - z], r3b, zp)
    three_a.wait_recv()
    key_out[...] = s2a[z].astype(F32) + r3a[...].astype(F32)
    three_b.wait_recv()
    value_out[...] = s2b[z].astype(F32) + r3b[...].astype(F32)
    for copy in carried:
        copy.wait_recv()
    for copy in local[6:]:
        copy.wait()
    for copy in copies:
        copy.wait_send()


def mid(part, gain_mid, gain_out, q, lse, tag, att, middle, branch, up, wo, k, v, cg, cu, ch, da, dd, scale):
    def kernel(*refs):
        mid_kernel(*refs, scale)

    any_ = whole(pl.ANY)
    tile = (2 * ROWS, HD)
    wide = (4 * 2 * ROWS, D)
    sems = 4 + 15 + 4 + 4 + 6 + 6 + 2
    return pl.pallas_call(
        kernel,
        out_shape=[
            jax.ShapeDtypeStruct(tile, F32),
            jax.ShapeDtypeStruct(tile, F32),
            jax.ShapeDtypeStruct((2,) + tile, F32),
            jax.ShapeDtypeStruct((2, ROWS, D), F32),
            jax.ShapeDtypeStruct((2, 4, 288, 2 * ROWS), BF),
            jax.ShapeDtypeStruct((2, D), F32),
            jax.ShapeDtypeStruct(wide, BF),
            jax.ShapeDtypeStruct(wide, BF),
            jax.ShapeDtypeStruct(wide, BF),
            jax.ShapeDtypeStruct((PART, 1024), BF),
            jax.ShapeDtypeStruct((PART, 1024), BF),
        ],
        in_specs=[whole()] * 7 + [any_] * 11,
        out_specs=[whole()] * 6 + [any_] * 5,
        scratch_shapes=[
            VMEM(middle.shape, F32),
            VMEM(branch.shape, BF),
            VMEM(up.shape, BF),
            VMEM(wo.shape, BF),
            VMEM(k.shape, BF),
            VMEM(v.shape, BF),
            VMEM((2, ROWS, D), BF),
            VMEM((2,) + tile, BF),
            VMEM((2, 4, 4) + tile, BF),
            VMEM((2, 4, 4) + tile, BF),
            VMEM((ROWS, D), BF),
            VMEM((ROWS, D), BF),
            VMEM((ROWS, D), BF),
            VMEM((2, ROWS, D), BF),
            VMEM((3, 2, 4) + tile, BF),
            VMEM((3, 2, 4) + tile, BF),
            VMEM((2, 4) + tile, BF),
            VMEM((2, 4) + tile, BF),
            VMEM((3, 2) + tile, BF),
            VMEM((3, 2) + tile, BF),
            VMEM((2,) + tile, BF),
            VMEM((2,) + tile, BF),
            VMEM(tile, BF),
            VMEM(tile, BF),
            pltpu.SemaphoreType.DMA((11,)),
            pltpu.SemaphoreType.DMA((sems,)),
            pltpu.SemaphoreType.DMA((sems,)),
        ],
        compiler_params=params(2, 62),
    )(part, gain_mid, gain_out, q, lse, tag, att, middle, branch, up, wo, k, v, cg, cu, ch, da, dd)


def turn(values, cosine, sine):
    half = HD // 2
    first, second = values[:, :half], values[:, half:]
    return jnp.concatenate([first * cosine - second * sine, second * cosine + first * sine], axis=1)


def end_kernel(
    key_ref, value_ref, dq_ref, cos_ref, sin_ref, gain_in, gains_in,
    bt, wq_in, wk_in, wv_in, tok_in, mgrad_in, dg_in, cg_in, dd_in, ch_in, cu_in, dn_in, ca_in,
    igrad, og, ou, od, oq, on,
    wq, wk, wv, tok, mgrad, dg, c0, dd, c1, dn, ca, db, cq,
    part, t1, th, t2, total_ref, gpad, gb, rgb,
    pg, pu, pd, pq, pn, rg, ru, rd, rq, rn, sg, su, sd, sq, sn, zg, zu, zd, zq, zn,
    lsem, ssem, rsem,
    scale,
):
    x, y, z, zh, c = place_of()
    xi = [(x + j) % 4 for j in (1, 2, 3)]
    yi = [(y + j) % 4 for j in (1, 2, 3)]
    xs = [device_at(i, y, z, zh, c) for i in xi]
    ys = [device_at(x, i, z, zh, c) for i in yi]
    zp = device_at(x, y, 1 - z, zh, c)
    mate = device_at(x, y, z, zh, 1 - c)
    far = device_at(x, y, z, 1 - zh, c)
    copies, local = [], []
    post = poster(ssem, rsem, copies)

    def load(src, dst):
        copy = pltpu.make_async_copy(src, dst, lsem.at[len(local)])
        copy.start()
        local.append(copy)
        return copy

    band_y = pl.ds(pl.multiple_of(y * 256, 256), 256)
    weights = [load(*pair) for pair in ((wq_in, wq), (wk_in, wk), (wv_in, wv))]
    got_g = [load(dg_in, dg), load(cg_in, c0)]
    got_d = [load(dd_in, dd), load(ch_in, c1)]
    got_t = [load(tok_in, tok), load(mgrad_in, mgrad)]
    got_q = [load(dn_in, dn), load(ca_in, ca), load(bt.at[:, y], db.at[:, :, band_y])]
    greet(xs + ys + [zp, mate, far])
    got_q_far = [post(bt.at[:, yi[j]], db.at[:, :, band_y], ys[j]) for j in range(3)]

    for m in range(2):
        r = slice(m * ROWS, (m + 1) * ROWS)
        own = pl.ds(pl.multiple_of(y * 256, 256) + m * ROWS, ROWS)
        cosine, sine = cos_ref[...], -sin_ref[...]
        for h in range(2):
            turned = turn(dq_ref[m, h * ROWS : (h + 1) * ROWS], cosine, sine)
            cq[own, h * HD : (h + 1) * HD] = turned.astype(BF)
        cq[own, 2 * HD : 3 * HD] = turn(key_ref[r], cosine, sine).astype(BF)
        cq[own, 3 * HD :] = value_ref[r].astype(BF)
    got_q_far += [post(cq.at[band_y], cq.at[band_y], ys[j]) for j in range(3)]
    for copy in weights:
        copy.wait()
    for m in range(2):
        own = pl.ds(pl.multiple_of(y * 256, 256) + m * ROWS, ROWS)
        a, b, v = wq[...], wk[...], wv[...]
        if m == 1:
            a, b, v = narrow(a), narrow(b), narrow(v)
        out = nt(cq[own, : 2 * HD], a) + nt(cq[own, 2 * HD : 3 * HD], b) + nt(cq[own, 3 * HD :], v)
        part[m] = (out * scale).astype(BF)
    rows = piece_rows()
    one = total_start(post, part, t1, rows, c, mate)
    two = total_across(post, part, t1, th, t2, rows, c, far, one)

    def multiply(left, right, out_ref, width, base, tile):
        def body(t, carry):
            cols = pl.ds(pl.multiple_of(t * tile, tile), tile)
            outs = pl.ds(pl.multiple_of(base + t * tile, 256), tile)
            out = nn(left[...].reshape(PART, 1024), right[:, cols])
            out_ref[:, :, :, outs] = out.reshape(2, 4, SHARE, tile).astype(BF)
            return carry

        lax.fori_loop(0, width // tile, body, 0)

    def spread(p, land, along):
        if along == "y":
            return [post(p.at[:, yi[j]], land.at[j], ys[j]) for j in range(3)]
        return [post(p.at[:, xi[j]], land.at[j], xs[j]) for j in range(3)]

    def reduce(p, land, half, own, arrivals, across):
        for copy in arrivals:
            copy.wait_recv()

        def body(t, carry):
            cols = pl.ds(pl.multiple_of(t * 128, 128), 128)
            for zi in range(2):
                out = p[zi, own, :, cols].astype(F32)
                for j in range(3):
                    out = out + land[j, zi, :, cols].astype(F32)
                half[zi, :, cols] = out.astype(BF)
            return carry

        lax.fori_loop(0, half.shape[-1] // 128, body, 0)
        return post(half.at[1 - z], across, zp)

    def finish(copy, half, across, out):
        copy.wait_recv()
        out[...] = half[z].astype(F32) + across[...].astype(F32)

    for copy in got_g:
        copy.wait()
    multiply(dg, c0, pg, D, 0, 768)
    two_g = spread(pg, rg, "y")
    got_u = load(cu_in, c0)
    for copy in got_d:
        copy.wait()
    multiply(dd, c1, pd, D, 0, 768)
    two_d = spread(pd, rd, "x")
    total_end(post, total_ref, th, t2, rows, c, mate, two)

    for copy in got_t:
        copy.wait()
    sums = jnp.zeros((1, D), F32)
    for m in range(2):

        def slab(i, carry):
            r = pl.ds(pl.multiple_of(i * 16, 16), 16)
            back, more = norm_grad(tok[m, r].astype(F32), gain_in[...], total_ref[m, r].astype(F32))
            igrad[m, r] = (mgrad[m, r] + back).astype(BF)
            return carry + more

        sums = lax.fori_loop(0, ROWS // 16, slab, sums)
    gpad[...] = jnp.zeros_like(gpad)
    gpad[0:1] = sums
    gpad[1:4] = gains_in[...]
    turned = gpad[...].T.astype(BF)
    for zi in range(2):
        for k in range(4):
            at = (zi * 4 + k) * 288
            gb[zi, k] = turned[at : at + 288]
    gains_far = [post(gb.at[:, yi[j]], rgb.at[j], ys[j]) for j in range(3)]

    got_u.wait()
    multiply(dg, c0, pu, D, 0, 768)
    two_u = spread(pu, ru, "y")
    for copy in got_q:
        copy.wait()
    for copy in got_q_far:
        copy.wait_recv()
    multiply(dn, cq, pq, 1024, 0, 512)
    multiply(db, ca, pq, 512, 1024, 512)
    two_q = spread(pq, rq, "x")
    out = gb[:, y].astype(F32)
    for j in range(3):
        gains_far[j].wait_recv()
        out = out + rgb[j].astype(F32)
    pn[...] = out.reshape(2, 4, SHARE, 128).astype(BF)
    two_n = spread(pn, rn, "x")
    three_g = reduce(pg, rg, sg, y, two_g, zg)
    three_d = reduce(pd, rd, sd, x, two_d, zd)
    finish(three_g, sg, zg, og)
    finish(three_d, sd, zd, od)
    three_u = reduce(pu, ru, su, y, two_u, zu)
    three_q = reduce(pq, rq, sq, x, two_q, zq)
    three_n = reduce(pn, rn, sn, x, two_n, zn)
    finish(three_u, su, zu, ou)
    finish(three_q, sq, zq, oq)
    finish(three_n, sn, zn, on)
    for copy in copies:
        copy.wait_send()


def end(key, value, dq, cosine, sine, gain_in, gains, bt, wq, wk, wv, tok, mgrad, dg, cg, dd, ch, cu, dn, ca, scale):
    def kernel(*refs):
        end_kernel(*refs, scale)

    widths = (D, D, D, 1536, 128)
    sems = 6 + 12 + 3 + 15 + 5
    return pl.pallas_call(
        kernel,
        out_shape=[jax.ShapeDtypeStruct((2, ROWS, D), BF)]
        + [jax.ShapeDtypeStruct((SHARE, w), F32) for w in widths],
        in_specs=[whole()] * 7 + [whole(pl.ANY)] * 13,
        out_specs=[whole()] * 6,
        scratch_shapes=[
            VMEM(wq.shape, BF),
            VMEM(wk.shape, BF),
            VMEM(wv.shape, BF),
            VMEM(tok.shape, BF),
            VMEM(mgrad.shape, F32),
            VMEM(dg.shape, BF),
            VMEM(cg.shape, BF),
            VMEM(dd.shape, BF),
            VMEM(ch.shape, BF),
            VMEM(dn.shape, BF),
            VMEM(ca.shape, BF),
            VMEM((2, 288, 1024), BF),
            VMEM((1024, 1024), BF),
            VMEM((2, ROWS, D), BF),
            VMEM((ROWS, D), BF),
            VMEM((ROWS, D), BF),
            VMEM((ROWS, D), BF),
            VMEM((2, ROWS, D), BF),
            VMEM((128, D), F32),
            VMEM((2, 4, 288, 128), BF),
            VMEM((3, 2, 288, 128), BF),
        ]
        + [VMEM((2, 4, SHARE, w), BF) for w in widths]
        + [VMEM((3, 2, SHARE, w), BF) for w in widths]
        + [VMEM((2, SHARE, w), BF) for w in widths]
        + [VMEM((SHARE, w), BF) for w in widths]
        + [
            pltpu.SemaphoreType.DMA((13,)),
            pltpu.SemaphoreType.DMA((sems,)),
            pltpu.SemaphoreType.DMA((sems,)),
        ],
        compiler_params=params(3, 63),
    )(key, value, dq, cosine, sine, gain_in, gains, bt, wq, wk, wv, tok, mgrad, dg, cg, dd, ch, cu, dn, ca)


def rows_for_x(left):
    t = left.T.reshape(2, 4, 4, SHARE, left.shape[0])
    return t.transpose(2, 0, 1, 3, 4).reshape(4, PART, left.shape[0])


def rows_for_y(left):
    t = left.T.reshape(2, 4, 4, SHARE, left.shape[0])
    return t.transpose(1, 0, 2, 3, 4).reshape(4, PART, left.shape[0])


def sliced(codes, bits):
    if bits == 8:
        return codes
    spacing = 2.0 ** (8 - bits)
    upper = 2.0 ** (bits - 1)
    wide = codes.astype(F32)
    return (jnp.clip(jnp.floor(wide / spacing + 0.5), -upper, upper - 1.0) * spacing).astype(BF)


def norm_rows(values, gain):
    return values * lax.rsqrt(jnp.mean(values * values, axis=-1, keepdims=True) + EPS) * gain


def norm_back(values, gain, grad):
    q = lax.rsqrt(jnp.mean(values * values, axis=-1, keepdims=True) + EPS)
    lifted = grad * gain
    back = q * lifted - values * (q * q * q) * jnp.mean(lifted * values, axis=-1, keepdims=True)
    return back, jnp.sum(grad * values * q, axis=(0, 1))


def rotate(values, cosine, sine):
    half = values.shape[-1] // 2
    first = values[..., :half]
    second = values[..., half:]
    return jnp.concatenate(
        [first * cosine - second * sine, second * cosine + first * sine], axis=-1
    )


def shards(
    inputs,
    out_grad,
    segment_ids,
    keep_mask,
    query_codes,
    key_codes,
    value_codes,
    output_codes,
    gate_codes,
    up_codes,
    down_codes,
    norm_attn_in,
    norm_attn_out,
    norm_ffn_in,
    norm_ffn_out,
):
    rows = inputs.shape[1]
    place = lax.axis_index("blk") * rows + jnp.arange(rows, dtype=jnp.int32)
    freqs = 10000.0 ** (-jnp.arange(HD // 2, dtype=F32) * 2.0 / HD)
    angles = place.astype(F32)[:, None] * freqs[None, :]
    cosine = jnp.cos(angles)
    sine = jnp.sin(angles)
    in_scale = LEVEL_SCALE * D ** (-0.5)
    mid_scale = LEVEL_SCALE * (HEADS * HD) ** (-0.5)
    ff_scale = LEVEL_SCALE * FF ** (-0.5)

    def by_batch(left, codes, scale, back=False):
        parts = []
        for m in range(2):
            weight = sliced(codes, WIDTHS[m])
            parts.append((nt if back else nn)(left[m], weight) * scale)
        return jnp.stack(parts)

    tokens = inputs.astype(F32)
    normed = norm_rows(tokens, norm_attn_in).astype(BF)
    q_raw = by_batch(normed, query_codes, in_scale).reshape(2, rows, 2, HD).transpose(0, 2, 1, 3)
    queries = rotate(q_raw, cosine, sine).astype(BF).reshape(2, 2 * rows, HD)
    key_own = rotate(by_batch(normed, key_codes, in_scale), cosine, sine).astype(BF)
    value_own = by_batch(normed, value_codes, in_scale).astype(BF)
    key_tag = jnp.where(keep_mask == 1, segment_ids, -1).astype(BF).reshape(1, 2 * rows)
    packed = jnp.concatenate(
        [key_own.reshape(2 * rows, HD), jnp.broadcast_to(key_tag, (16, 2 * rows))], axis=0
    )
    keys, values = gather(packed, value_own.reshape(2 * rows, HD))
    keys = keys.reshape(32, 2 * rows + 16, HD)
    values = values.reshape(32, 2 * rows, HD)
    tag = segment_ids.astype(F32)
    tag = jnp.concatenate([tag, tag], axis=1)[:, :, None]
    attended, lse = attend(queries, tag, keys, values)

    def flat(heads):
        return heads.reshape(2, 2, rows, HD).transpose(0, 2, 1, 3).reshape(2, rows, 2 * HD)

    def both(left):
        return left.reshape(2 * rows, left.shape[-1])

    attended_flat = flat(attended).astype(BF)
    branch, (d_normed,) = total(
        by_batch(attended_flat, output_codes, mid_scale).astype(BF),
        4,
        [("swap", "y", rows_for_y(both(normed)))],
    )
    branch_low = branch
    branch = branch.astype(F32)
    middle = tokens + norm_rows(branch, norm_attn_out)
    ffn_in = norm_rows(middle, norm_ffn_in).astype(BF)
    gate, upper, hidden, down_part = ffn(
        ffn_in, gate_codes, up_codes, down_codes, in_scale, ff_scale
    )
    down, (all_attended,) = total(down_part, 5, [("copy", "y", both(attended_flat))])
    down = down.astype(F32)
    out_rows = (middle + norm_rows(down, norm_ffn_out)).astype(BF)

    upstream = out_grad.astype(F32)
    down_grad, gain_ffn_out = norm_back(down, norm_ffn_out, upstream)
    down_low = down_grad.astype(BF)
    gate_low, up_low, ffn_part = ffn_back(
        down_low, gate, upper, gate_codes, up_codes, down_codes, in_scale, ff_scale
    )
    key_rot, value_grad, query_rot, middle_grad, d_branch, gains, cg, cu, ch, d_ffn_in, d_down = mid(
        ffn_part, norm_ffn_in[None], norm_attn_out[None], queries, lse, tag, attended,
        middle, branch_low, out_grad, output_codes, keys, values,
        both(gate_low), both(up_low), both(hidden),
        rows_for_x(both(ffn_in)), rows_for_y(both(down_low)), mid_scale,
    )
    gains = jnp.concatenate([gains, gain_ffn_out[None]])
    input_grad, g_gate, g_up, g_down, g_rest, g_gains = end(
        key_rot, value_grad, query_rot, cosine, sine, norm_attn_in[None], gains,
        d_branch, query_codes, key_codes, value_codes, inputs, middle_grad,
        d_ffn_in, cg, d_down, ch, cu, d_normed, all_attended, in_scale,
    )
    return (
        out_rows,
        input_grad,
        g_rest[:, :512] * in_scale,
        g_rest[:, 512:768] * in_scale,
        g_rest[:, 768:1024] * in_scale,
        g_rest[:, 1024:1536].T * mid_scale,
        g_gate * in_scale,
        g_up * in_scale,
        g_down.T * ff_scale,
        g_gains[:, 0],
        g_gains[:, 1],
        g_gains[:, 2],
        g_gains[:, 3],
    )


def solution(mesh):
    placed = (
        P(None, "blk", None),
        P(None, "blk", None),
        P(None, "blk"),
        P(None, "blk"),
        P(None, "tensor"),
        P(None, "tensor"),
        P(None, "tensor"),
        P("tensor", None),
        P(None, "tensor"),
        P(None, "tensor"),
        P("tensor", None),
        P(),
        P(),
        P(),
        P(),
    )
    return jax.shard_map(
        shards,
        mesh=mesh,
        in_specs=placed,
        out_specs=(
            P(None, "blk", None),
            P(None, "blk", None),
            P("blk", "tensor"),
            P("blk", "tensor"),
            P("blk", "tensor"),
            P("tensor", "blk"),
            P("blk", "tensor"),
            P("blk", "tensor"),
            P("tensor", "blk"),
            P("blk"),
            P("blk"),
            P("blk"),
            P("blk"),
        ),
        check_vma=False,
    )
```

```python
import functools

import jax
import jax.numpy as jnp
from jax import lax
from jax.experimental import pallas as pl
from jax.experimental.pallas import tpu as pltpu
from jax.sharding import PartitionSpec as P

D = 2304
HEADS = 8
HD = 256
FF = 9216

CAP = 50.0
EPS = 1e-06
LEVEL_SCALE = 1.0 / 74.0
WIDTHS = (8, 4, 2)

MESH = pl.DeviceIdType.MESH
VMEM = pltpu.VMEM
BF = jnp.bfloat16
F32 = jnp.float32
SEQ = 4096
ROWS = 128
TAGROW = 256
MASKED = -2.0


def place_of():
    b = lax.axis_index("blk")
    t = lax.axis_index("tensor")
    return b % 4, (b // 4) % 4, b // 16, t // 2, t % 2


def device_at(x, y, z, zh, c):
    return ((z * 4 + y) * 4 + x, zh * 2 + c)


def greet(peers):
    barrier = pltpu.get_barrier_semaphore()
    for peer in peers:
        pl.semaphore_signal(barrier, inc=1, device_id=peer, device_id_type=MESH)
    pl.semaphore_wait(barrier, len(peers))


def send(src, dst, ssem, rsem, peer):
    copy = pltpu.make_async_remote_copy(
        src_ref=src, dst_ref=dst, send_sem=ssem, recv_sem=rsem, device_id=peer, device_id_type=MESH
    )
    copy.start()
    return copy


def params(collective_id=None, limit=60):
    if collective_id is None:
        return pltpu.CompilerParams(vmem_limit_bytes=limit << 20)
    return pltpu.CompilerParams(
        vmem_limit_bytes=limit << 20, collective_id=collective_id, has_side_effects=True
    )


def whole(space=VMEM):
    return pl.BlockSpec(memory_space=space)


CHUNK = 4
KEYS = CHUNK * ROWS


def nt(left, right):
    return lax.dot_general(left, right, (((1,), (1,)), ((), ())), preferred_element_type=F32)


def tn(left, right):
    return lax.dot_general(left, right, (((0,), (0,)), ((), ())), preferred_element_type=F32)


def nn(left, right):
    return jnp.dot(left, right, preferred_element_type=F32)


def load_chunk(ref, step):
    zi, k = step // 4, step % 4
    keys = ref[zi, k, :, :ROWS, :].reshape(KEYS, HD)
    values = ref[zi, k, :, ROWS : 2 * ROWS, :].reshape(KEYS, HD)
    tags = ref[zi, k, :, TAGROW : TAGROW + 16, :ROWS].astype(F32)
    tag_row = jnp.concatenate([tags[i, 0:1, :] for i in range(CHUNK)], axis=1)
    return keys, values, tag_row


def allowed(key_place, tag_row, query_tag, query_place):
    ok = (key_place <= query_place) & (tag_row == query_tag)
    return ok | (key_place == query_place)


def query_places():
    row = lax.broadcasted_iota(jnp.int32, (2 * ROWS, 1), 0)
    return lax.axis_index("blk") * ROWS + row % ROWS


def poster(ssem, rsem, copies):
    def post(src, dst, peer):
        k = len(copies)
        copies.append(send(src, dst, ssem.at[k], rsem.at[k], peer))
        return copies[k]

    return post


def loader(sem, copies):
    def load(src, dst):
        copy = pltpu.make_async_copy(src, dst, sem.at[len(copies)])
        copy.start()
        copies.append(copy)
        return copy

    return load


def arrive(copies):
    for copy in copies:
        copy.wait_recv()


def turn(values, cosine, sine):
    half = HD // 2
    first, second = values[:, :half], values[:, half:]
    return jnp.concatenate([first * cosine - second * sine, second * cosine + first * sine], axis=1)


def fill_turned(dst, value, m):
    turned = value.T
    for zi in range(2):
        for k in range(4):
            at = (zi * 4 + k) * 288
            dst[zi, k, :, m * ROWS : (m + 1) * ROWS] = turned[at : at + 288]


HALF = ROWS // 2
STEP_ROWS = 32


class Summed:
    def __init__(self, post, part, t1, th, t2, c, mate, far):
        self.post, self.part, self.t1, self.th, self.t2 = post, part, t1, th, t2
        self.c, self.mate, self.far = c, mate, far
        self.pieces = [pl.ds(k * STEP_ROWS, STEP_ROWS) for k in range(HALF // STEP_ROWS)]

    def rows(self, core, k):
        return pl.ds(pl.multiple_of(core * HALF + k * STEP_ROWS, STEP_ROWS), STEP_ROWS)

    def start(self, i):
        other = 1 - self.c
        return [
            self.post(self.part.at[i, self.rows(other, k)], self.t1.at[i, r], self.mate)
            for k, r in enumerate(self.pieces)
        ]

    def across(self, i, one):
        sent = []
        for k, r in enumerate(self.pieces):
            one[k].wait_recv()
            own = self.part[i, self.rows(self.c, k)].astype(F32)
            self.th[i, r] = (own + self.t1[i, r].astype(F32)).astype(BF)
            sent.append(self.post(self.th.at[i, r], self.t2.at[i, r], self.far))
        return sent

    def back(self, i, two, dst, m):
        sent = []
        for k, r in enumerate(self.pieces):
            two[k].wait_recv()
            rows = self.rows(self.c, k)
            dst[m, rows] = (self.th[i, r].astype(F32) + self.t2[i, r].astype(F32)).astype(BF)
            sent.append(self.post(dst.at[m, rows], dst.at[m, rows], self.mate))
        return sent


CUT = 144


def front_kernel(
    gain_in, gain_out, gain_ffn, cos_ref, sin_ref, tags, tag_ref,
    tok_in, wq_in, wk_in, wv_in, wo_in,
    middle, branch, ffn_in, q_ref, att, lse_ref, ft, all_a, all_b, dn_land, ca_land,
    tok, wq, wk, wv, wo, normed, dn, flat, ga, gb, acc, mass, part, t1, th, t2,
    lsem, ssem, rsem,
    scale_in, scale_mid,
):
    x, y, z, zh, c = place_of()
    block = lax.axis_index("blk")
    xi = [(x + j) % 4 for j in (1, 2, 3)]
    yi = [(y + j) % 4 for j in (1, 2, 3)]
    xs = [device_at(i, y, z, zh, c) for i in xi]
    ys = [device_at(x, i, z, zh, c) for i in yi]
    zp = device_at(x, y, 1 - z, zh, c)
    mate = device_at(x, y, z, zh, 1 - c)
    far = device_at(x, y, z, 1 - zh, c)
    copies, local = [], []
    post = poster(ssem, rsem, copies)
    load = loader(lsem, local)
    loads = [
        load(*pair)
        for pair in ((tok_in, tok), (wk_in, wk), (wv_in, wv), (wq_in, wq), (wo_in, wo))
    ]
    greet(xs + ys + [zp, mate, far])

    loads[0].wait()
    for m in range(2):

        def slab(i, carry):
            r = pl.ds(pl.multiple_of(i * 16, 16), 16)
            v = tok[m, r].astype(F32)
            q = lax.rsqrt(jnp.mean(v * v, axis=-1, keepdims=True) + EPS)
            normed[m, r] = (v * q * gain_in[...]).astype(BF)
            return carry

        lax.fori_loop(0, ROWS // 16, slab, 0)
    loads[1].wait()
    loads[2].wait()
    cosine, sine = cos_ref[...], sin_ref[...]
    for m, held in ((0, ga), (1, gb)):
        a, b = wk[...], wv[...]
        if m == 1:
            a, b = narrow(a), narrow(b)
        held[z, y, x, :ROWS] = turn(nn(normed[m], a) * scale_in, cosine, sine).astype(BF)
        held[z, y, x, ROWS : 2 * ROWS] = (nn(normed[m], b) * scale_in).astype(BF)
        held[z, y, x, TAGROW:] = tags[m]

    levels = (z, 1 - z)

    def at_a(level, along_x, along_y, part=None):
        ref = ga.at[level, along_y, along_x]
        return ref if part is None else ref.at[part]

    def at_b(level, along_y, along_x, part=None):
        ref = gb.at[level, along_y, along_x]
        return ref if part is None else ref.at[part]

    first_half, last_half = pl.ds(0, CUT), pl.ds(CUT, TAGROW + 16 - CUT)
    sides = (
        (at_a, x, xi, xs, y, yi, ys),
        (at_b, y, yi, ys, x, xi, xs),
    )

    def line(side, level, second, pair=None):
        if side == 0:
            return ga.at[level, second] if pair is None else ga.at[level, second, pair]
        return gb.at[level, :, second] if pair is None else gb.at[level, pair, second]

    across = []
    for at, one, places, devices, two, _, _ in sides:
        own = at(z, one, two)
        across.append(post(own, own, zp))
    near = {}

    def send_near(side, k):
        at, one, places, devices, two, _, _ = sides[side]
        own = at(levels[k], one, two)
        near[side, k] = [post(own, own, devices[j]) for j in (0, 2)]

    relays = {}

    def relay_near(side, k):
        at, one, places, devices, two, _, _ = sides[side]
        sent = near[side, k]
        sent[0].wait_recv()
        piece = at(levels[k], places[2], two, first_half)
        relays[side, k] = [post(piece, piece, devices[0])]
        sent[1].wait_recv()
        piece = at(levels[k], places[0], two, last_half)
        relays[side, k].append(post(piece, piece, devices[2]))

    lines = {}

    def send_line(side, k):
        _, _, _, _, two, _, devices = sides[side]
        arrive(relays[side, k])
        own = line(side, levels[k], two)
        lines[side, k] = [post(own, own, devices[j]) for j in (0, 2)]

    passed = {}

    def relay_line(side, k):
        _, _, _, _, _, places, devices = sides[side]
        sent = lines[side, k]
        sent[0].wait_recv()
        piece = line(side, levels[k], places[2], pl.ds(0, 2))
        passed[side, k] = [post(piece, piece, devices[0])]
        sent[1].wait_recv()
        piece = line(side, levels[k], places[0], pl.ds(2, 2))
        passed[side, k].append(post(piece, piece, devices[2]))

    both = (0, 1)
    for side in both:
        send_near(side, 0)
    loads[3].wait()
    for m in range(2):
        a = wq[...] if m == 0 else narrow(wq[...])
        wide = nn(normed[m], a) * scale_in
        for h in range(2):
            turned = turn(wide[:, h * HD : (h + 1) * HD], cosine, sine)
            q_ref[m, h * ROWS : (h + 1) * ROWS] = turned.astype(BF)
        fill_turned(dn, normed[m], m)
    arrive(across)
    for side in both:
        send_near(side, 1)
    for k in both:
        for side in both:
            relay_near(side, k)

    acc[...] = jnp.zeros_like(acc)
    mass[...] = jnp.zeros_like(mass)
    where = query_places()
    lane = lax.broadcasted_iota(jnp.int32, (2 * ROWS, KEYS), 1)

    def attend(side, k, second):
        level = levels[k]
        if side == 0:
            held, begin, key_place = ga.at[level, second], level * 16 + second * 4, lane
            stride = 1
        else:
            held, begin, key_place = gb.at[level, :, second], level * 16 + second, lane % ROWS + lane // ROWS * (4 * ROWS)
            stride = 4

        @pl.when(begin <= block)
        def _():
            keys = held[:, :ROWS, :].reshape(KEYS, HD)
            values = held[:, ROWS : 2 * ROWS, :].reshape(KEYS, HD)
            tag = held[:, TAGROW : TAGROW + 16, :ROWS].astype(F32)
            tag_row = jnp.concatenate([tag[i, 0:1, :] for i in range(CHUNK)], axis=1)
            bent = jnp.tanh(nt(q_ref[side], keys) * (HD ** (-0.5) / CAP))
            ok = allowed(key_place + begin * ROWS, tag_row, tag_ref[side], where)
            e = jnp.where(ok, jnp.exp(CAP * bent), 0.0)
            mass[side] += jnp.sum(e, axis=-1, keepdims=True)
            acc[side] += nn(e.astype(BF), values)

    for k in both:
        for side in both:
            send_line(side, k)
    for k in both:
        for side in both:
            attend(side, k, sides[side][4])
    for k in both:
        for side in both:
            relay_line(side, k)
    for k in both:
        for side in both:
            attend(side, k, sides[side][5][0])
            attend(side, k, sides[side][5][2])
    for side in both:
        for k in both:
            arrive(passed[side, k])
            attend(side, k, sides[side][5][1])
    load(ga, all_a)
    load(gb, all_b)

    band_y = pl.ds(pl.multiple_of(y * 256, 256), 256)
    sums = Summed(post, part, t1, th, t2, c, mate, far)
    carried = []
    loads[4].wait()

    def project(m):
        out = acc[m] / mass[m]
        att[m] = out
        lse_ref[m] = jnp.log(mass[m])
        low = out.astype(BF)
        flat[m] = jnp.concatenate([low[:ROWS], low[ROWS:]], axis=1)
        a = wo[...] if m == 0 else narrow(wo[...])
        part[m] = (nn(flat[m], a) * scale_mid).astype(BF)

    def spread(m):
        rows = pl.ds(pl.multiple_of(y * 256, 256) + m * ROWS, ROWS)
        load(flat.at[m], ca_land.at[rows])
        return [post(flat.at[m], ca_land.at[rows], ys[j]) for j in range(3)]

    def norms(m):
        def slab(i, carry):
            r = pl.ds(pl.multiple_of(i * 16, 16), 16)
            v = branch[m, r].astype(F32)
            q = lax.rsqrt(jnp.mean(v * v, axis=-1, keepdims=True) + EPS)
            mid = tok[m, r].astype(F32) + v * q * gain_out[...]
            middle[m, r] = mid
            q = lax.rsqrt(jnp.mean(mid * mid, axis=-1, keepdims=True) + EPS)
            ffn_in[m, r] = (mid * q * gain_ffn[...]).astype(BF)
            return carry

        lax.fori_loop(0, ROWS // 16, slab, 0)
        fill_turned(ft, ffn_in[m], m)

    project(0)
    one = sums.start(0)
    carried += [post(dn.at[:, yi[j]], dn_land.at[:, :, band_y], ys[j]) for j in range(3)]
    load(dn.at[:, y], dn_land.at[:, :, band_y])
    two0 = sums.across(0, one)
    project(1)
    one = sums.start(1)
    two1 = sums.across(1, one)
    carried += spread(0)
    carried += spread(1)
    three = sums.back(0, two0, branch, 0)
    arrive(three)
    norms(0)
    three = sums.back(1, two1, branch, 1)
    arrive(three)
    norms(1)
    arrive(carried)
    for copy in local[5:]:
        copy.wait()
    for copy in copies:
        copy.wait_send()


def front(gain_in, gain_out, gain_ffn, cosine, sine, tags, tag, tok, wq, wk, wv, wo, scale_in, scale_mid):
    def kernel(*refs):
        front_kernel(*refs, scale_in, scale_mid)

    any_ = whole(pl.ANY)
    both = (2, ROWS, D)
    heads = (2, 2 * ROWS, HD)
    kv = (2, 4, 4, TAGROW + 16, HD)
    turned = (2, 4, 288, 2 * ROWS)
    sems = 34 + 2 * 3 * (HALF // STEP_ROWS) + 9
    return pl.pallas_call(
        kernel,
        out_shape=[
            jax.ShapeDtypeStruct(both, F32),
            jax.ShapeDtypeStruct(both, BF),
            jax.ShapeDtypeStruct(both, BF),
            jax.ShapeDtypeStruct(heads, BF),
            jax.ShapeDtypeStruct(heads, F32),
            jax.ShapeDtypeStruct((2, 2 * ROWS, 1), F32),
            jax.ShapeDtypeStruct(turned, BF),
            jax.ShapeDtypeStruct(kv, BF),
            jax.ShapeDtypeStruct(kv, BF),
            jax.ShapeDtypeStruct((2, 288, 1024), BF),
            jax.ShapeDtypeStruct((1024, 2 * HD), BF),
        ],
        in_specs=[whole()] * 7 + [any_] * 5,
        out_specs=[whole()] * 7 + [any_] * 4,
        scratch_shapes=[
            VMEM(both, BF),
            VMEM(wq.shape, BF),
            VMEM(wk.shape, BF),
            VMEM(wv.shape, BF),
            VMEM(wo.shape, BF),
            VMEM(both, BF),
            VMEM(turned, BF),
            VMEM((2, ROWS, 2 * HD), BF),
            VMEM(kv, BF),
            VMEM(kv, BF),
            VMEM(heads, F32),
            VMEM((2, 2 * ROWS, 1), F32),
            VMEM(both, BF),
            VMEM((2, HALF, D), BF),
            VMEM((2, HALF, D), BF),
            VMEM((2, HALF, D), BF),
            pltpu.SemaphoreType.DMA((10,)),
            pltpu.SemaphoreType.DMA((sems,)),
            pltpu.SemaphoreType.DMA((sems,)),
        ],
        compiler_params=params(1, 60),
    )(gain_in, gain_out, gain_ffn, cosine, sine, tags, tag, tok, wq, wk, wv, wo)


FTILE = 256
ROOT = (2.0 / 3.141592653589793) ** 0.5
CUBE = 0.044715


def narrow(codes):
    level = codes * BF(1.0 / 16.0) + BF(1.0 / 32.0)
    level = (level + BF(192.0)) - BF(192.0)
    return jnp.minimum(level, BF(7.0)) * BF(16.0)


def ffn_kernel(
    x_ref, gain_ref, wg_in, wu_in, wd_in, middle_in, up_in, dg_own,
    out_ref, dgate_ref, dup_ref, total_ref, gains, ch, dd_land, dg_land,
    wg, wu, wd, middle, upstream, gate_s, up_s, hid, acc, part, low, dd,
    t1, th, t2, down_sum,
    wsem, lsem, ssem, rsem,
    scale_in, scale_out,
):
    x, y, z, zh, c = place_of()
    xi = [(x + j) % 4 for j in (1, 2, 3)]
    yi = [(y + j) % 4 for j in (1, 2, 3)]
    xs = [device_at(i, y, z, zh, c) for i in xi]
    ys = [device_at(x, i, z, zh, c) for i in yi]
    mate = device_at(x, y, z, zh, 1 - c)
    far = device_at(x, y, z, 1 - zh, c)
    tiles = wg.shape[1] // FTILE
    copies, local = [], []
    post = poster(ssem, rsem, copies)

    def load(src, dst):
        copy = pltpu.make_async_copy(src, dst, lsem.at[len(local)])
        copy.start()
        local.append(copy)
        return copy

    def weight_copies(t):
        span = pl.ds(pl.multiple_of(t * FTILE, FTILE), FTILE)
        return (
            pltpu.make_async_copy(wg_in.at[:, span], wg.at[:, span], wsem.at[0, t]),
            pltpu.make_async_copy(wu_in.at[:, span], wu.at[:, span], wsem.at[1, t]),
            pltpu.make_async_copy(wd_in.at[span], wd.at[span], wsem.at[2, t]),
        )

    def start_weights(t, carry):
        for copy in weight_copies(t):
            copy.start()
        return carry

    lax.fori_loop(0, tiles, start_weights, 0)
    loads = [load(middle_in, middle), load(up_in, upstream)]
    greet(xs + ys + [mate, far])
    band_x = pl.ds(pl.multiple_of(x * 256, 256), 256)
    band_y = pl.ds(pl.multiple_of(y * 256, 256), 256)
    carried = [post(dg_own.at[xi[j]], dg_land.at[:, band_x], xs[j]) for j in range(3)]
    load(dg_own.at[x], dg_land.at[:, band_x])

    def forward(m, first, last, wait=False):
        def body(t, carry):
            span = pl.ds(pl.multiple_of(t * FTILE, FTILE), FTILE)
            if wait:
                for copy in weight_copies(t):
                    copy.wait()
            a, b, d = wg[:, span], wu[:, span], wd[span]
            if m == 1:
                a, b, d = narrow(a), narrow(b), narrow(d)
            gate = nn(x_ref[m], a) * scale_in
            up = nn(x_ref[m], b) * scale_in
            gate_s[m, :, span] = gate
            up_s[m, :, span] = up
            bent = jnp.tanh(ROOT * (gate + CUBE * gate * gate * gate))
            hidden = (0.5 * gate * (1.0 + bent) * up).astype(BF)
            hid[m, :, span] = hidden
            acc[...] += nn(hidden, d)
            return carry

        lax.fori_loop(first, last, body, 0)

    def backward(m, first, last):
        def body(t, carry):
            span = pl.ds(pl.multiple_of(t * FTILE, FTILE), FTILE)
            a, b, d = wg[:, span], wu[:, span], wd[span]
            if m == 1:
                a, b, d = narrow(a), narrow(b), narrow(d)
            grad = nt(low[m], d) * scale_out
            v, u = gate_s[m, :, span], up_s[m, :, span]
            bent = jnp.tanh(ROOT * (v + CUBE * v * v * v))
            half = 0.5 * (1.0 + bent)
            slope = half + 0.5 * v * (1.0 - bent * bent) * (ROOT * (1.0 + 3.0 * CUBE * v * v))
            dgate = (grad * u * slope).astype(BF)
            dup = (grad * (v * half)).astype(BF)
            dgate_ref[m, :, span] = dgate
            dup_ref[m, :, span] = dup
            acc[...] += nt(dgate, a) + nt(dup, b)
            return carry

        lax.fori_loop(first, last, body, 0)

    pieces = [pl.ds(k * STEP_ROWS, STEP_ROWS) for k in range(HALF // STEP_ROWS)]

    def at_rows(core, k):
        return pl.ds(pl.multiple_of(core * HALF + k * STEP_ROWS, STEP_ROWS), STEP_ROWS)

    def sum_start(i, m):
        return [post(part.at[i, at_rows(1 - c, k)], t1.at[i, r], mate) for k, r in enumerate(pieces)]

    def sum_across(i, one):
        sent = []
        for k, r in enumerate(pieces):
            one[k].wait_recv()
            th[i, r] = (part[i, at_rows(c, k)].astype(F32) + t1[i, r].astype(F32)).astype(BF)
            sent.append(post(th.at[i, r], t2.at[i, r], far))
        return sent

    def sum_back(i, two, dst, m):
        sent = []
        for k, r in enumerate(pieces):
            two[k].wait_recv()
            dst[m, at_rows(c, k)] = (th[i, r].astype(F32) + t2[i, r].astype(F32)).astype(BF)
            sent.append(post(dst.at[m, at_rows(c, k)], dst.at[m, at_rows(c, k)], mate))
        return sent

    def arrive(sent):
        for copy in sent:
            copy.wait_recv()

    def spread_hidden(m):
        rows = pl.ds(pl.multiple_of(y * 256, 256) + m * ROWS, ROWS)
        load(hid.at[m], ch.at[rows])
        return [post(hid.at[m], ch.at[rows], ys[j]) for j in (0, 2)]

    def relay_hidden(m, sent):
        for j, copy in zip((0, 2), sent):
            copy.wait_recv()
            source = yi[2] if j == 0 else yi[0]
            begin = pl.multiple_of(source * 256, 256) + m * ROWS + (0 if j == 0 else HALF)
            rows = pl.ds(begin, HALF)
            carried.append(post(ch.at[rows], ch.at[rows], ys[j]))

    def norm(m, sums):
        def slab(i, carry):
            r = pl.ds(pl.multiple_of(i * 16, 16), 16)
            v = down_sum[m, r].astype(F32)
            du = upstream[m, r].astype(F32)
            q = lax.rsqrt(jnp.mean(v * v, axis=-1, keepdims=True) + EPS)
            gain = gain_ref[...]
            out_ref[m, r] = (middle[m, r] + v * q * gain).astype(BF)
            lifted = du * gain
            back = q * lifted - v * (q * q * q * jnp.mean(lifted * v, axis=-1, keepdims=True))
            low[m, r] = back.astype(BF)
            return carry + jnp.sum(du * v * q, axis=0, keepdims=True)

        return lax.fori_loop(0, ROWS // 16, slab, sums)

    def turn_down(m):
        turned = low[m].T
        for zi in range(2):
            for k in range(4):
                at = (zi * 4 + k) * 288
                dd[zi, k, :, m * ROWS : (m + 1) * ROWS] = turned[at : at + 288]

    acc[...] = jnp.zeros_like(acc)
    forward(0, 0, tiles, True)
    part[0] = (acc[...] * scale_out).astype(BF)
    one = sum_start(0, 0)
    hidden0 = spread_hidden(0)
    acc[...] = jnp.zeros_like(acc)
    forward(1, 0, 2)
    two = sum_across(0, one)
    forward(1, 2, tiles)
    part[1] = (acc[...] * scale_out).astype(BF)
    one = sum_start(1, 1)
    hidden1 = spread_hidden(1)
    three = sum_back(0, two, down_sum, 0)
    two = sum_across(1, one)
    arrive(three)
    for copy in loads:
        copy.wait()
    sums = norm(0, jnp.zeros((1, D), F32))
    relay_hidden(0, hidden0)
    acc[...] = jnp.zeros_like(acc)
    backward(0, 0, tiles)
    part[2] = (acc[...] * scale_in).astype(BF)
    one = sum_start(2, 0)
    three = sum_back(1, two, down_sum, 1)
    two = sum_across(2, one)
    arrive(three)
    gains[...] = norm(1, sums)
    relay_hidden(1, hidden1)
    turn_down(0)
    turn_down(1)
    carried += [post(dd.at[:, yi[j]], dd_land.at[:, :, band_y], ys[j]) for j in range(3)]
    load(dd.at[:, y], dd_land.at[:, :, band_y])
    acc[...] = jnp.zeros_like(acc)
    backward(1, 0, tiles)
    part[3] = (acc[...] * scale_in).astype(BF)
    one = sum_start(3, 1)
    three = sum_back(2, two, total_ref, 0)
    two = sum_across(3, one)
    arrive(three)
    three = sum_back(3, two, total_ref, 1)
    arrive(three)
    arrive(carried)
    for copy in local[2:]:
        copy.wait()
    for copy in copies:
        copy.wait_send()


def ffn(x, gain, wg, wu, wd, middle, up, dg, scale_in, scale_out):
    def kernel(*refs):
        ffn_kernel(*refs, scale_in, scale_out)

    any_ = whole(pl.ANY)
    both = (2, ROWS, D)
    tiles = wg.shape[1] // FTILE
    sems = 3 + 4 * 3 * (HALF // STEP_ROWS) + 8 + 3
    return pl.pallas_call(
        kernel,
        out_shape=[
            jax.ShapeDtypeStruct(both, BF),
            jax.ShapeDtypeStruct(both, BF),
            jax.ShapeDtypeStruct(both, BF),
            jax.ShapeDtypeStruct(both, BF),
            jax.ShapeDtypeStruct((1, D), F32),
            jax.ShapeDtypeStruct((1024, D), BF),
            jax.ShapeDtypeStruct((2, 288, 1024), BF),
            jax.ShapeDtypeStruct((PART, 1024), BF),
        ],
        in_specs=[whole()] * 2 + [any_] * 6,
        out_specs=[whole()] * 5 + [any_] * 3,
        scratch_shapes=[
            VMEM(wg.shape, BF),
            VMEM(wu.shape, BF),
            VMEM(wd.shape, BF),
            VMEM(both, F32),
            VMEM(both, BF),
            VMEM(both, F32),
            VMEM(both, F32),
            VMEM(both, BF),
            VMEM((ROWS, D), F32),
            VMEM((4, ROWS, D), BF),
            VMEM(both, BF),
            VMEM((2, 4, 288, 2 * ROWS), BF),
            VMEM((4, HALF, D), BF),
            VMEM((4, HALF, D), BF),
            VMEM((4, HALF, D), BF),
            VMEM(both, BF),
            pltpu.SemaphoreType.DMA((3, tiles)),
            pltpu.SemaphoreType.DMA((6,)),
            pltpu.SemaphoreType.DMA((sems,)),
            pltpu.SemaphoreType.DMA((sems,)),
        ],
        compiler_params=params(5, 63),
    )(x, gain, wg, wu, wd, middle, up, dg)


PART = 576
SHARE = 72


PIECES = 4


def total_start(post, p_ref, r1, rows, c, mate):
    return [post(p_ref.at[1 - c, r], r1.at[r], mate) for r in rows]


def total_across(post, p_ref, r1, h, r2, rows, c, far, one):
    two = []
    for k, r in enumerate(rows):
        one[k].wait_recv()
        h[r] = (p_ref[c, r].astype(F32) + r1[r].astype(F32)).astype(BF)
        two.append(post(h.at[r], r2.at[r], far))
    return two


def total_end(post, o_ref, h, r2, rows, c, mate, two):
    three = []
    for k, r in enumerate(rows):
        two[k].wait_recv()
        o_ref[c, r] = (h[r].astype(F32) + r2[r].astype(F32)).astype(BF)
        three.append(post(o_ref.at[c, r], o_ref.at[c, r], mate))
    for copy in three:
        copy.wait_recv()


def piece_rows():
    size = ROWS // PIECES
    return [pl.ds(k * size, size) for k in range(PIECES)]


def norm_grad(v, gain, grad):
    q = lax.rsqrt(jnp.mean(v * v, axis=-1, keepdims=True) + EPS)
    lifted = grad * gain
    back = q * lifted - v * (q * q * q * jnp.mean(lifted * v, axis=-1, keepdims=True))
    return back, jnp.sum(grad * v * q, axis=0, keepdims=True)


def mid_kernel(
    total_ref, gain_mid, gain_out, q_ref, lse_ref, tag_ref, att_ref,
    middle_in, branch_in, up_in, wo_in, k_in, v_in, cg_own, cu_own, du,
    key_out, value_out, dq_ref, mgrad, bt, gains, cg, cu, du_land,
    middle, branch, upstream, wo, k_ref, v_ref, blow, g_ref, dk, dv,
    r1a, r1b, s1a, s1b, r2a, r2b, s2a, s2b, r3a, r3b,
    lsem, ssem, rsem,
    scale,
):
    x, y, z, zh, c = place_of()
    xi = [(x + j) % 4 for j in (1, 2, 3)]
    yi = [(y + j) % 4 for j in (1, 2, 3)]
    xs = [device_at(i, y, z, zh, c) for i in xi]
    ys = [device_at(x, i, z, zh, c) for i in yi]
    zp = device_at(x, y, 1 - z, zh, c)
    copies, local = [], []
    post = poster(ssem, rsem, copies)

    def load(src, dst):
        copy = pltpu.make_async_copy(src, dst, lsem.at[len(local)])
        copy.start()
        local.append(copy)
        return copy

    loads = [
        load(*pair)
        for pair in (
            (middle_in, middle), (branch_in, branch), (up_in, upstream), (wo_in, wo), (k_in, k_ref), (v_in, v_ref),
        )
    ]
    greet(xs + ys + [zp])
    band_x = pl.ds(pl.multiple_of(x * 256, 256), 256)
    band_y = pl.ds(pl.multiple_of(y * 256, 256), 256)
    gate_sent = [post(cg_own, cg.at[band_x], xs[j]) for j in (0, 2)]
    up_sent = [post(cu_own, cu.at[band_y], ys[j]) for j in (0, 2)]
    carried = [post(du.at[:, yi[j]], du_land.at[:, :, band_y], ys[j]) for j in range(3)]
    for pair in (
        (du.at[:, y], du_land.at[:, :, band_y]), (cg_own, cg.at[band_x]), (cu_own, cu.at[band_y]),
    ):
        load(*pair)
    for copy in loads[:4]:
        copy.wait()

    zero = jnp.zeros((1, D), F32)
    for m in range(2):

        def slab(i, carry):
            sum_mid, sum_out = carry
            r = pl.ds(pl.multiple_of(i * 16, 16), 16)
            back, more = norm_grad(middle[m, r], gain_mid[...], total_ref[m, r].astype(F32))
            grad = upstream[m, r].astype(F32) + back
            mgrad[m, r] = grad
            back, most = norm_grad(branch[m, r].astype(F32), gain_out[...], grad)
            blow[m, r] = back.astype(BF)
            return sum_mid + more, sum_out + most

        sums = lax.fori_loop(0, ROWS // 16, slab, (zero, zero) if m == 0 else sums)
    gains[0:1] = sums[1]
    gains[1:2] = sums[0]
    for m in range(2):
        weight = wo[...] if m == 0 else narrow(wo[...])
        wide = (nt(blow[m], weight) * scale).astype(BF)
        g_ref[m, :ROWS] = wide[:, :HD]
        g_ref[m, ROWS:] = wide[:, HD:]
        turned = blow[m].T
        for zi in range(2):
            for k in range(4):
                at = (zi * 4 + k) * 288
                bt[zi, k, :, m * ROWS : (m + 1) * ROWS] = turned[at : at + 288]

    for j, k in ((0, 0), (2, 1)):
        for sent, land, places, devices in ((gate_sent, cg, xi, xs), (up_sent, cu, yi, ys)):
            sent[k].wait_recv()
            begin = pl.multiple_of(places[2 - j] * 256, 256) + k * ROWS
            relayed = pl.ds(begin, ROWS)
            carried.append(post(land.at[relayed], land.at[relayed], devices[j]))

    loads[4].wait()
    loads[5].wait()
    limit = lax.axis_index("blk") // CHUNK + 1
    where = query_places()
    lane = lax.broadcasted_iota(jnp.int32, (2 * ROWS, KEYS), 1)
    for m in range(2):
        q = q_ref[m]
        g = g_ref[m]
        tag = tag_ref[m]
        lse = lse_ref[m]
        off = jnp.sum(g.astype(F32) * att_ref[m], axis=-1, keepdims=True)
        span = slice(m * ROWS, (m + 1) * ROWS)

        def step(i, dq):
            keys, values, tag_row = load_chunk(k_ref if m == 0 else v_ref, i)
            bent = jnp.tanh(nt(q, keys) * (HD ** (-0.5) / CAP))
            ok = allowed(i * KEYS + lane, tag_row, tag, where)
            p = jnp.where(ok, jnp.exp(CAP * bent - lse), 0.0)
            dp = nt(g, values)
            ds = (p * (dp - off) * (1.0 - bent * bent) * HD ** (-0.5)).astype(BF)
            dk[i // 4, i % 4, :, span, :] = tn(ds, q).astype(BF).reshape(CHUNK, ROWS, HD)
            dv[i // 4, i % 4, :, span, :] = tn(p.astype(BF), g).astype(BF).reshape(CHUNK, ROWS, HD)
            return dq + nn(ds, keys)

        dq_ref[m] = lax.fori_loop(0, limit, step, jnp.zeros((2 * ROWS, HD), F32))

        def blank(i, carry):
            dk[i // 4, i % 4, :, span, :] = jnp.zeros((CHUNK, ROWS, HD), BF)
            dv[i // 4, i % 4, :, span, :] = jnp.zeros((CHUNK, ROWS, HD), BF)
            return carry

        lax.fori_loop(limit, SEQ // KEYS, blank, 0)

    one_a = [post(dk.at[:, :, xi[j]], r1a.at[j], xs[j]) for j in range(3)]
    one_b = [post(dv.at[:, yi[j]], r1b.at[j], ys[j]) for j in range(3)]
    for copy in one_a:
        copy.wait_recv()

    def add_a(i, carry):
        zi, k = i // 4, i % 4
        out = dk[zi, k, x].astype(F32)
        for j in range(3):
            out = out + r1a[j, zi, k].astype(F32)
        s1a[zi, k] = out.astype(BF)
        return carry

    lax.fori_loop(0, 8, add_a, 0)
    two_a = [post(s1a.at[:, yi[j]], r2a.at[j], ys[j]) for j in range(3)]
    for copy in one_b:
        copy.wait_recv()

    def add_b(i, carry):
        zi, k = i // 4, i % 4
        out = dv[zi, y, k].astype(F32)
        for j in range(3):
            out = out + r1b[j, zi, k].astype(F32)
        s1b[zi, k] = out.astype(BF)
        return carry

    lax.fori_loop(0, 8, add_b, 0)
    two_b = [post(s1b.at[:, xi[j]], r2b.at[j], xs[j]) for j in range(3)]

    def second(arrivals, own, mine, land, half):
        for copy in arrivals:
            copy.wait_recv()
        for zi in range(2):
            out = own[zi, mine].astype(F32)
            for j in range(3):
                out = out + land[j, zi].astype(F32)
            half[zi] = out.astype(BF)

    second(two_a, s1a, y, r2a, s2a)
    three_a = post(s2a.at[1 - z], r3a, zp)
    second(two_b, s1b, x, r2b, s2b)
    three_b = post(s2b.at[1 - z], r3b, zp)
    three_a.wait_recv()
    key_out[...] = s2a[z].astype(F32) + r3a[...].astype(F32)
    three_b.wait_recv()
    value_out[...] = s2b[z].astype(F32) + r3b[...].astype(F32)
    for copy in carried:
        copy.wait_recv()
    for copy in local[6:]:
        copy.wait()
    for copy in copies:
        copy.wait_send()


def mid(total_in, gain_mid, gain_out, q, lse, tag, att, middle, branch, up, wo, k, v, cg, cu, du, scale):
    def kernel(*refs):
        mid_kernel(*refs, scale)

    any_ = whole(pl.ANY)
    tile = (2 * ROWS, HD)
    wide = (4 * 2 * ROWS, D)
    sems = 4 + 3 + 4 + 6 + 6 + 2
    return pl.pallas_call(
        kernel,
        out_shape=[
            jax.ShapeDtypeStruct(tile, F32),
            jax.ShapeDtypeStruct(tile, F32),
            jax.ShapeDtypeStruct((2,) + tile, F32),
            jax.ShapeDtypeStruct((2, ROWS, D), F32),
            jax.ShapeDtypeStruct((2, 4, 288, 2 * ROWS), BF),
            jax.ShapeDtypeStruct((2, D), F32),
            jax.ShapeDtypeStruct(wide, BF),
            jax.ShapeDtypeStruct(wide, BF),
            jax.ShapeDtypeStruct((2, 288, 1024), BF),
        ],
        in_specs=[whole()] * 7 + [any_] * 9,
        out_specs=[whole()] * 6 + [any_] * 3,
        scratch_shapes=[
            VMEM(middle.shape, F32),
            VMEM(branch.shape, BF),
            VMEM(up.shape, BF),
            VMEM(wo.shape, BF),
            VMEM(k.shape, BF),
            VMEM(v.shape, BF),
            VMEM((2, ROWS, D), BF),
            VMEM((2,) + tile, BF),
            VMEM((2, 4, 4) + tile, BF),
            VMEM((2, 4, 4) + tile, BF),
            VMEM((3, 2, 4) + tile, BF),
            VMEM((3, 2, 4) + tile, BF),
            VMEM((2, 4) + tile, BF),
            VMEM((2, 4) + tile, BF),
            VMEM((3, 2) + tile, BF),
            VMEM((3, 2) + tile, BF),
            VMEM((2,) + tile, BF),
            VMEM((2,) + tile, BF),
            VMEM(tile, BF),
            VMEM(tile, BF),
            pltpu.SemaphoreType.DMA((9,)),
            pltpu.SemaphoreType.DMA((sems,)),
            pltpu.SemaphoreType.DMA((sems,)),
        ],
        compiler_params=params(2, 62),
    )(total_in, gain_mid, gain_out, q, lse, tag, att, middle, branch, up, wo, k, v, cg, cu, du)


def end_kernel(
    key_ref, value_ref, dq_ref, cos_ref, sin_ref, gain_in, gains_in,
    bt, wq_in, wk_in, wv_in, tok_in, mgrad_in, dg_in, cg_in, du_in, cu_in, dd_in, ch_in, dn_in, ca_in,
    igrad, og, ou, od, oq, on,
    wq, wk, wv, tok, mgrad, dg, c0, dd, c1, dn, ca, db, cq,
    part, t1, th, t2, total_ref, gpad, gb, rgb,
    pg, pu, pd, pq, pn, rg, ru, rd, rq, rn, sg, su, sd, sq, sn, zg, zu, zd, zq, zn,
    lsem, ssem, rsem,
    scale,
):
    x, y, z, zh, c = place_of()
    xi = [(x + j) % 4 for j in (1, 2, 3)]
    yi = [(y + j) % 4 for j in (1, 2, 3)]
    xs = [device_at(i, y, z, zh, c) for i in xi]
    ys = [device_at(x, i, z, zh, c) for i in yi]
    zp = device_at(x, y, 1 - z, zh, c)
    mate = device_at(x, y, z, zh, 1 - c)
    far = device_at(x, y, z, 1 - zh, c)
    copies, local = [], []
    post = poster(ssem, rsem, copies)

    def load(src, dst):
        copy = pltpu.make_async_copy(src, dst, lsem.at[len(local)])
        copy.start()
        local.append(copy)
        return copy

    band_y = pl.ds(pl.multiple_of(y * 256, 256), 256)
    weights = [load(*pair) for pair in ((wq_in, wq), (wk_in, wk), (wv_in, wv))]
    got_g = [load(dg_in, dg), load(cg_in, c0)]
    got_u = [load(du_in, dd), load(cu_in, c1)]
    got_t = [load(tok_in, tok), load(mgrad_in, mgrad)]
    got_q = [load(dn_in, dn), load(ca_in, ca), load(bt.at[:, y], db.at[:, :, band_y])]
    greet(xs + ys + [zp, mate, far])
    got_q_far = [post(bt.at[:, yi[j]], db.at[:, :, band_y], ys[j]) for j in range(3)]

    for m in range(2):
        r = slice(m * ROWS, (m + 1) * ROWS)
        own = pl.ds(pl.multiple_of(y * 256, 256) + m * ROWS, ROWS)
        cosine, sine = cos_ref[...], -sin_ref[...]
        for h in range(2):
            turned = turn(dq_ref[m, h * ROWS : (h + 1) * ROWS], cosine, sine)
            cq[own, h * HD : (h + 1) * HD] = turned.astype(BF)
        cq[own, 2 * HD : 3 * HD] = turn(key_ref[r], cosine, sine).astype(BF)
        cq[own, 3 * HD :] = value_ref[r].astype(BF)
    got_q_far += [post(cq.at[band_y], cq.at[band_y], ys[j]) for j in range(3)]
    for copy in weights:
        copy.wait()
    for m in range(2):
        own = pl.ds(pl.multiple_of(y * 256, 256) + m * ROWS, ROWS)
        a, b, v = wq[...], wk[...], wv[...]
        if m == 1:
            a, b, v = narrow(a), narrow(b), narrow(v)
        out = nt(cq[own, : 2 * HD], a) + nt(cq[own, 2 * HD : 3 * HD], b) + nt(cq[own, 3 * HD :], v)
        part[m] = (out * scale).astype(BF)
    rows = piece_rows()
    one = total_start(post, part, t1, rows, c, mate)
    two = total_across(post, part, t1, th, t2, rows, c, far, one)

    def multiply(left, right, out_ref, width, base, tile):
        def body(t, carry):
            cols = pl.ds(pl.multiple_of(t * tile, tile), tile)
            outs = pl.ds(pl.multiple_of(base + t * tile, 256), tile)
            out = nn(left[...].reshape(PART, 1024), right[:, cols])
            out_ref[:, :, :, outs] = out.reshape(2, 4, SHARE, tile).astype(BF)
            return carry

        lax.fori_loop(0, width // tile, body, 0)

    def spread(p, land, along):
        if along == "y":
            return [post(p.at[:, yi[j]], land.at[j], ys[j]) for j in range(3)]
        return [post(p.at[:, xi[j]], land.at[j], xs[j]) for j in range(3)]

    def reduce(p, land, half, own, arrivals, across):
        for copy in arrivals:
            copy.wait_recv()

        def body(t, carry):
            cols = pl.ds(pl.multiple_of(t * 128, 128), 128)
            for zi in range(2):
                out = p[zi, own, :, cols].astype(F32)
                for j in range(3):
                    out = out + land[j, zi, :, cols].astype(F32)
                half[zi, :, cols] = out.astype(BF)
            return carry

        lax.fori_loop(0, half.shape[-1] // 128, body, 0)
        return post(half.at[1 - z], across, zp)

    def finish(copy, half, across, out):
        copy.wait_recv()
        out[...] = half[z].astype(F32) + across[...].astype(F32)

    for copy in got_g:
        copy.wait()
    multiply(dg, c0, pg, D, 0, 768)
    two_g = spread(pg, rg, "y")
    got_d = [load(ch_in, c0)]
    for copy in got_u:
        copy.wait()
    multiply(dd, c1, pu, D, 0, 768)
    two_u = spread(pu, ru, "x")
    got_d.append(load(dd_in, dd))
    total_end(post, total_ref, th, t2, rows, c, mate, two)

    for copy in got_t:
        copy.wait()
    sums = jnp.zeros((1, D), F32)
    for m in range(2):

        def slab(i, carry):
            r = pl.ds(pl.multiple_of(i * 16, 16), 16)
            back, more = norm_grad(tok[m, r].astype(F32), gain_in[...], total_ref[m, r].astype(F32))
            igrad[m, r] = (mgrad[m, r] + back).astype(BF)
            return carry + more

        sums = lax.fori_loop(0, ROWS // 16, slab, sums)
    gpad[...] = jnp.zeros_like(gpad)
    gpad[0:1] = sums
    gpad[1:4] = gains_in[...]
    turned = gpad[...].T.astype(BF)
    for zi in range(2):
        for k in range(4):
            at = (zi * 4 + k) * 288
            gb[zi, k] = turned[at : at + 288]
    gains_far = [post(gb.at[:, yi[j]], rgb.at[j], ys[j]) for j in range(3)]

    for copy in got_d:
        copy.wait()
    multiply(dd, c0, pd, D, 0, 768)
    two_d = spread(pd, rd, "x")
    for copy in got_q:
        copy.wait()
    for copy in got_q_far:
        copy.wait_recv()
    multiply(dn, cq, pq, 1024, 0, 512)
    multiply(db, ca, pq, 512, 1024, 512)
    two_q = spread(pq, rq, "x")
    out = gb[:, y].astype(F32)
    for j in range(3):
        gains_far[j].wait_recv()
        out = out + rgb[j].astype(F32)
    pn[...] = out.reshape(2, 4, SHARE, 128).astype(BF)
    two_n = spread(pn, rn, "x")
    three_g = reduce(pg, rg, sg, y, two_g, zg)
    three_u = reduce(pu, ru, su, x, two_u, zu)
    finish(three_g, sg, zg, og)
    finish(three_u, su, zu, ou)
    three_d = reduce(pd, rd, sd, x, two_d, zd)
    three_q = reduce(pq, rq, sq, x, two_q, zq)
    three_n = reduce(pn, rn, sn, x, two_n, zn)
    finish(three_d, sd, zd, od)
    finish(three_q, sq, zq, oq)
    finish(three_n, sn, zn, on)
    for copy in copies:
        copy.wait_send()


def end(key, value, dq, cosine, sine, gain_in, gains, bt, wq, wk, wv, tok, mgrad, dg, cg, du, cu, dd, ch, dn, ca, scale):
    def kernel(*refs):
        end_kernel(*refs, scale)

    widths = (D, D, D, 1536, 128)
    sems = 6 + 12 + 3 + 15 + 5
    return pl.pallas_call(
        kernel,
        out_shape=[jax.ShapeDtypeStruct((2, ROWS, D), BF)]
        + [jax.ShapeDtypeStruct((SHARE, w), F32) for w in widths],
        in_specs=[whole()] * 7 + [whole(pl.ANY)] * 14,
        out_specs=[whole()] * 6,
        scratch_shapes=[
            VMEM(wq.shape, BF),
            VMEM(wk.shape, BF),
            VMEM(wv.shape, BF),
            VMEM(tok.shape, BF),
            VMEM(mgrad.shape, F32),
            VMEM(dg.shape, BF),
            VMEM(cg.shape, BF),
            VMEM(dd.shape, BF),
            VMEM(ch.shape, BF),
            VMEM(dn.shape, BF),
            VMEM(ca.shape, BF),
            VMEM((2, 288, 1024), BF),
            VMEM((1024, 1024), BF),
            VMEM((2, ROWS, D), BF),
            VMEM((ROWS, D), BF),
            VMEM((ROWS, D), BF),
            VMEM((ROWS, D), BF),
            VMEM((2, ROWS, D), BF),
            VMEM((128, D), F32),
            VMEM((2, 4, 288, 128), BF),
            VMEM((3, 2, 288, 128), BF),
        ]
        + [VMEM((2, 4, SHARE, w), BF) for w in widths]
        + [VMEM((3, 2, SHARE, w), BF) for w in widths]
        + [VMEM((2, SHARE, w), BF) for w in widths]
        + [VMEM((SHARE, w), BF) for w in widths]
        + [
            pltpu.SemaphoreType.DMA((14,)),
            pltpu.SemaphoreType.DMA((sems,)),
            pltpu.SemaphoreType.DMA((sems,)),
        ],
        compiler_params=params(3, 63),
    )(key, value, dq, cosine, sine, gain_in, gains, bt, wq, wk, wv, tok, mgrad, dg, cg, du, cu, dd, ch, dn, ca)


def shards(
    inputs,
    out_grad,
    segment_ids,
    keep_mask,
    query_codes,
    key_codes,
    value_codes,
    output_codes,
    gate_codes,
    up_codes,
    down_codes,
    norm_attn_in,
    norm_attn_out,
    norm_ffn_in,
    norm_ffn_out,
):
    rows = inputs.shape[1]
    place = lax.axis_index("blk") * rows + jnp.arange(rows, dtype=jnp.int32)
    freqs = 10000.0 ** (-jnp.arange(HD // 2, dtype=F32) * 2.0 / HD)
    angles = place.astype(F32)[:, None] * freqs[None, :]
    cosine = jnp.cos(angles)
    sine = jnp.sin(angles)
    in_scale = LEVEL_SCALE * D ** (-0.5)
    mid_scale = LEVEL_SCALE * (HEADS * HD) ** (-0.5)
    ff_scale = LEVEL_SCALE * FF ** (-0.5)

    def both(left):
        return left.reshape(2 * rows, left.shape[-1])

    key_tag = jnp.where(keep_mask == 1, segment_ids, -1).astype(BF)
    key_tag = jnp.concatenate([key_tag, jnp.zeros_like(key_tag)], axis=1)
    key_tag = jnp.broadcast_to(key_tag[:, None, :], (2, 16, 2 * rows))
    tag = segment_ids.astype(F32)
    tag = jnp.concatenate([tag, tag], axis=1)[:, :, None]
    (
        middle, branch, ffn_in, queries, attended, lse, ffn_turned, blocks_a, blocks_b, d_normed, all_attended,
    ) = front(
        norm_attn_in[None], norm_attn_out[None], norm_ffn_in[None], cosine, sine, key_tag, tag,
        inputs, query_codes, key_codes, value_codes, output_codes, in_scale, mid_scale,
    )
    out_rows, gate_low, up_low, ffn_in_grad, gain_ffn_out, ch, d_down, d_gate = ffn(
        ffn_in, norm_ffn_out[None], gate_codes, up_codes, down_codes, middle, out_grad,
        ffn_turned.reshape(8, 4, SHARE, 2 * rows).transpose(1, 0, 2, 3).reshape(4, PART, 2 * rows),
        in_scale, ff_scale,
    )
    key_rot, value_grad, query_rot, middle_grad, d_branch, gains, cg, cu, d_up = mid(
        ffn_in_grad, norm_ffn_in[None], norm_attn_out[None], queries, lse, tag, attended,
        middle, branch, out_grad, output_codes, blocks_a, blocks_b,
        both(gate_low), both(up_low), ffn_turned, mid_scale,
    )
    gains = jnp.concatenate([gains, gain_ffn_out])
    input_grad, g_gate, g_up, g_down, g_rest, g_gains = end(
        key_rot, value_grad, query_rot, cosine, sine, norm_attn_in[None], gains,
        d_branch, query_codes, key_codes, value_codes, inputs, middle_grad,
        d_gate, cg, d_up, cu, d_down, ch, d_normed, all_attended, in_scale,
    )
    return (
        out_rows,
        input_grad,
        g_rest[:, :512] * in_scale,
        g_rest[:, 512:768] * in_scale,
        g_rest[:, 768:1024] * in_scale,
        g_rest[:, 1024:1536].T * mid_scale,
        g_gate * in_scale,
        g_up * in_scale,
        g_down.T * ff_scale,
        g_gains[:, 0],
        g_gains[:, 1],
        g_gains[:, 2],
        g_gains[:, 3],
    )


def solution(mesh):
    placed = (
        P(None, "blk", None),
        P(None, "blk", None),
        P(None, "blk"),
        P(None, "blk"),
        P(None, "tensor"),
        P(None, "tensor"),
        P(None, "tensor"),
        P("tensor", None),
        P(None, "tensor"),
        P(None, "tensor"),
        P("tensor", None),
        P(),
        P(),
        P(),
        P(),
    )
    return jax.shard_map(
        shards,
        mesh=mesh,
        in_specs=placed,
        out_specs=(
            P(None, "blk", None),
            P(None, "blk", None),
            P("blk", "tensor"),
            P("blk", "tensor"),
            P("blk", "tensor"),
            P("tensor", "blk"),
            P("blk", "tensor"),
            P("blk", "tensor"),
            P("tensor", "blk"),
            P("blk"),
            P("blk"),
            P("blk"),
            P("blk"),
        ),
        check_vma=False,
    )
```

```python
import functools

import jax
import jax.numpy as jnp
from jax import lax
from jax.experimental import pallas as pl
from jax.experimental.pallas import tpu as pltpu
from jax.sharding import PartitionSpec as P

D = 2304
HEADS = 8
HD = 256
FF = 9216

CAP = 50.0
EPS = 1e-06
LEVEL_SCALE = 1.0 / 74.0
WIDTHS = (8, 4, 2)

MESH = pl.DeviceIdType.MESH
VMEM = pltpu.VMEM
BF = jnp.bfloat16
F32 = jnp.float32
SEQ = 4096
ROWS = 128
TAGROW = 256
MASKED = -2.0


def place_of():
    b = lax.axis_index("blk")
    t = lax.axis_index("tensor")
    return b % 4, (b // 4) % 4, b // 16, t // 2, t % 2


def device_at(x, y, z, zh, c):
    return ((z * 4 + y) * 4 + x, zh * 2 + c)


def greet(peers):
    barrier = pltpu.get_barrier_semaphore()
    for peer in peers:
        pl.semaphore_signal(barrier, inc=1, device_id=peer, device_id_type=MESH)
    pl.semaphore_wait(barrier, len(peers))


def send(src, dst, ssem, rsem, peer):
    copy = pltpu.make_async_remote_copy(
        src_ref=src, dst_ref=dst, send_sem=ssem, recv_sem=rsem, device_id=peer, device_id_type=MESH
    )
    copy.start()
    return copy


def params(collective_id=None, limit=60):
    if collective_id is None:
        return pltpu.CompilerParams(vmem_limit_bytes=limit << 20)
    return pltpu.CompilerParams(
        vmem_limit_bytes=limit << 20, collective_id=collective_id, has_side_effects=True
    )


def whole(space=VMEM):
    return pl.BlockSpec(memory_space=space)


CHUNK = 4
KEYS = CHUNK * ROWS


def nt(left, right):
    return lax.dot_general(left, right, (((1,), (1,)), ((), ())), preferred_element_type=F32)


def tn(left, right):
    return lax.dot_general(left, right, (((0,), (0,)), ((), ())), preferred_element_type=F32)


def nn(left, right):
    return jnp.dot(left, right, preferred_element_type=F32)


def allowed(key_place, tag_row, query_tag, query_place):
    ok = (key_place <= query_place) & (tag_row == query_tag)
    return ok | (key_place == query_place)


def query_places():
    row = lax.broadcasted_iota(jnp.int32, (2 * ROWS, 1), 0)
    return lax.axis_index("blk") * ROWS + row % ROWS


def poster(ssem, rsem, copies):
    def post(src, dst, peer):
        k = len(copies)
        copies.append(send(src, dst, ssem.at[k], rsem.at[k], peer))
        return copies[k]

    return post


def loader(sem, copies):
    def load(src, dst):
        copy = pltpu.make_async_copy(src, dst, sem.at[len(copies)])
        copy.start()
        copies.append(copy)
        return copy

    return load


def arrive(copies):
    for copy in copies:
        copy.wait_recv()


def turn(values, cosine, sine):
    half = HD // 2
    first, second = values[:, :half], values[:, half:]
    return jnp.concatenate([first * cosine - second * sine, second * cosine + first * sine], axis=1)


def fill_turned(dst, value, m):
    turned = value.T
    for zi in range(2):
        for k in range(4):
            at = (zi * 4 + k) * 288
            dst[zi, k, :, m * ROWS : (m + 1) * ROWS] = turned[at : at + 288]


HALF = ROWS // 2
STEP_ROWS = 32


class Summed:
    def __init__(self, post, part, t1, th, t2, c, mate, far):
        self.post, self.part, self.t1, self.th, self.t2 = post, part, t1, th, t2
        self.c, self.mate, self.far = c, mate, far
        self.pieces = [pl.ds(k * STEP_ROWS, STEP_ROWS) for k in range(HALF // STEP_ROWS)]

    def rows(self, core, k):
        return pl.ds(pl.multiple_of(core * HALF + k * STEP_ROWS, STEP_ROWS), STEP_ROWS)

    def start(self, i):
        other = 1 - self.c
        return [
            self.post(self.part.at[i, self.rows(other, k)], self.t1.at[i, r], self.mate)
            for k, r in enumerate(self.pieces)
        ]

    def across(self, i, one):
        sent = []
        for k, r in enumerate(self.pieces):
            one[k].wait_recv()
            own = self.part[i, self.rows(self.c, k)].astype(F32)
            self.th[i, r] = (own + self.t1[i, r].astype(F32)).astype(BF)
            sent.append(self.post(self.th.at[i, r], self.t2.at[i, r], self.far))
        return sent

    def back(self, i, two, dst, m):
        sent = []
        for k, r in enumerate(self.pieces):
            two[k].wait_recv()
            rows = self.rows(self.c, k)
            dst[m, rows] = (self.th[i, r].astype(F32) + self.t2[i, r].astype(F32)).astype(BF)
            sent.append(self.post(dst.at[m, rows], dst.at[m, rows], self.mate))
        return sent


def relay(post, sent, land, places, devices):
    out = []
    size = land.shape[1] // 2
    for k, j in ((0, 0), (1, 2)):
        sent[k].wait_recv()
        half = land.at[places[2 - j], pl.ds(k * size, size)]
        out.append(post(half, half, devices[j]))
    return out


def share(post, sent, land, places, width, c, mate):
    out = []
    for j, copy in enumerate(sent):
        copy.wait_recv()
        begin = pl.multiple_of(places[2 - j] * (2 * width), 2 * width) + c * width
        band = land.at[:, :, pl.ds(pl.multiple_of(begin, width), width)]
        out.append(post(band, band, mate))
    return out


class Ring:
    def __init__(self, post, held, land, mine, places, devices, add):
        self.post, self.land, self.mine, self.places, self.devices = post, land, mine, places, devices
        self.held, self.add = held, add
        near, across, far = places
        self.order = ((0, across), (1, across), (1, near), (0, far))
        self.sent = []

    def begin(self):
        k = len(self.sent)
        self.sent.append(self.post(self.held(*self.order[k]), self.land.at[k], self.devices[0 if k % 2 == 0 else 2]))

    def begin_all(self):
        for _ in self.order:
            self.begin()
        return self

    def onward(self):
        self.passed = []
        for level, j in ((0, 0), (1, 2)):
            self.sent[level].wait_recv()
            ref = self.held(level, self.places[j])
            self.add(ref, ref, (self.land.at[level],))
            self.passed.append(self.post(ref, self.land.at[4 + level], self.devices[j]))

    def close(self, half):
        for level in range(2):
            self.sent[3 - level].wait_recv()
            self.passed[level].wait_recv()
            own = self.held(level, self.mine)
            self.add(half.at[level], own, (self.land.at[3 - level], self.land.at[4 + level]))


def add_blocks(dst, own, others):
    def body(k, carry):
        out = own[k].astype(F32)
        for other in others:
            out = out + other[k].astype(F32)
        dst[k] = out.astype(BF)
        return carry

    lax.fori_loop(0, own.shape[0], body, 0)


def add_columns(dst, own, others):
    tile = 256 if own.shape[-1] % 256 == 0 else 128

    def body(t, carry):
        cols = pl.ds(pl.multiple_of(t * tile, tile), tile)
        out = own[:, cols].astype(F32)
        for other in others:
            out = out + other[:, cols].astype(F32)
        dst[:, cols] = out.astype(BF)
        return carry

    lax.fori_loop(0, own.shape[-1] // tile, body, 0)


def multiply(left, right, out_ref, width, base, tile):
    def body(t, carry):
        cols = pl.ds(pl.multiple_of(t * tile, tile), tile)
        outs = pl.ds(pl.multiple_of(base + t * tile, 256), tile)
        out = nn(left[...].reshape(PART, 1024), right[:, :, cols].reshape(1024, tile))
        out_ref[:, :, :, outs] = out.reshape(2, 4, SHARE, tile).astype(BF)
        return carry

    lax.fori_loop(0, width // tile, body, 0)


CUT = 144


def front_kernel(
    norms_ref, cos_ref, sin_ref, tags, tag_ref,
    tok_in, wq_in, wk_in, wv_in, wo_in,
    middle, branch, ffn_in, q_ref, att, lse_ref, ft, all_a, all_b, dn_land, ca_land,
    tok, wq, wk, wv, wo, normed, dn, flat, ga, gb, acc, mass, part, t1, th, t2,
    lsem, ssem, rsem,
    scale_in, scale_mid,
):
    x, y, z, zh, c = place_of()
    block = lax.axis_index("blk")
    xi = [(x + j) % 4 for j in (1, 2, 3)]
    yi = [(y + j) % 4 for j in (1, 2, 3)]
    xs = [device_at(i, y, z, zh, c) for i in xi]
    ys = [device_at(x, i, z, zh, c) for i in yi]
    zp = device_at(x, y, 1 - z, zh, c)
    mate = device_at(x, y, z, zh, 1 - c)
    far = device_at(x, y, z, 1 - zh, c)
    copies, local = [], []
    post = poster(ssem, rsem, copies)
    load = loader(lsem, local)
    loads = [
        load(*pair)
        for pair in ((tok_in, tok), (wk_in, wk), (wv_in, wv), (wq_in, wq), (wo_in, wo))
    ]
    greet(xs + ys + [zp, mate, far])

    loads[0].wait()
    for m in range(2):

        def slab(i, carry):
            r = pl.ds(pl.multiple_of(i * 16, 16), 16)
            v = tok[m, r].astype(F32)
            q = lax.rsqrt(jnp.mean(v * v, axis=-1, keepdims=True) + EPS)
            normed[m, r] = (v * q * norms_ref[0:1]).astype(BF)
            return carry

        lax.fori_loop(0, ROWS // 16, slab, 0)
    loads[1].wait()
    loads[2].wait()
    cosine, sine = cos_ref[...], sin_ref[...]
    for m, held in ((0, ga), (1, gb)):
        a, b = wk[...], wv[...]
        if m == 1:
            a, b = narrow(a), narrow(b)
        held[z, y, x, :ROWS] = turn(nn(normed[m], a) * scale_in, cosine, sine).astype(BF)
        held[z, y, x, ROWS : 2 * ROWS] = (nn(normed[m], b) * scale_in).astype(BF)
        held[z, y, x, TAGROW:] = tags[m]

    levels = (z, 1 - z)

    def at_a(level, along_x, along_y, part=None):
        ref = ga.at[level, along_y, along_x]
        return ref if part is None else ref.at[part]

    def at_b(level, along_y, along_x, part=None):
        ref = gb.at[level, along_y, along_x]
        return ref if part is None else ref.at[part]

    first_half, last_half = pl.ds(0, CUT), pl.ds(CUT, TAGROW + 16 - CUT)
    sides = (
        (at_a, x, xi, xs, y, yi, ys),
        (at_b, y, yi, ys, x, xi, xs),
    )

    def line(side, level, second, pair=None):
        if side == 0:
            return ga.at[level, second] if pair is None else ga.at[level, second, pair]
        return gb.at[level, :, second] if pair is None else gb.at[level, pair, second]

    across = []
    for at, one, places, devices, two, _, _ in sides:
        own = at(z, one, two)
        across.append(post(own, own, zp))
    near = {}

    def send_near(side, k):
        at, one, places, devices, two, _, _ = sides[side]
        own = at(levels[k], one, two)
        near[side, k] = [post(own, own, devices[j]) for j in (0, 2)]

    relays = {}

    def relay_near(side, k):
        at, one, places, devices, two, _, _ = sides[side]
        sent = near[side, k]
        sent[0].wait_recv()
        piece = at(levels[k], places[2], two, first_half)
        relays[side, k] = [post(piece, piece, devices[0])]
        sent[1].wait_recv()
        piece = at(levels[k], places[0], two, last_half)
        relays[side, k].append(post(piece, piece, devices[2]))

    lines = {}

    def send_line(side, k):
        _, _, _, _, two, _, devices = sides[side]
        arrive(relays[side, k])
        own = line(side, levels[k], two)
        lines[side, k] = [post(own, own, devices[j]) for j in (0, 2)]

    passed = {}

    def relay_line(side, k):
        _, _, _, _, _, places, devices = sides[side]
        sent = lines[side, k]
        sent[0].wait_recv()
        piece = line(side, levels[k], places[2], pl.ds(0, 2))
        passed[side, k] = [post(piece, piece, devices[0])]
        sent[1].wait_recv()
        piece = line(side, levels[k], places[0], pl.ds(2, 2))
        passed[side, k].append(post(piece, piece, devices[2]))

    both = (0, 1)
    for side in both:
        send_near(side, 0)
    loads[3].wait()
    for m in range(2):
        a = wq[...] if m == 0 else narrow(wq[...])
        wide = nn(normed[m], a) * scale_in
        for h in range(2):
            turned = turn(wide[:, h * HD : (h + 1) * HD], cosine, sine)
            q_ref[m, h * ROWS : (h + 1) * ROWS] = turned.astype(BF)
        fill_turned(dn, normed[m], m)
    arrive(across)
    for side in both:
        send_near(side, 1)
    for k in both:
        for side in both:
            relay_near(side, k)

    acc[...] = jnp.zeros_like(acc)
    mass[...] = jnp.zeros_like(mass)
    where = query_places()
    lane = lax.broadcasted_iota(jnp.int32, (2 * ROWS, KEYS), 1)

    def attend(side, k, second):
        level = levels[k]
        if side == 0:
            held, begin, key_place = ga.at[level, second], level * 16 + second * 4, lane
            stride = 1
        else:
            held, begin, key_place = gb.at[level, :, second], level * 16 + second, lane % ROWS + lane // ROWS * (4 * ROWS)
            stride = 4

        @pl.when(begin <= block)
        def _():
            keys = held[:, :ROWS, :].reshape(KEYS, HD)
            values = held[:, ROWS : 2 * ROWS, :].reshape(KEYS, HD)
            tag = held[:, TAGROW : TAGROW + 16, :ROWS].astype(F32)
            tag_row = jnp.concatenate([tag[i, 0:1, :] for i in range(CHUNK)], axis=1)
            bent = jnp.tanh(nt(q_ref[side], keys) * (HD ** (-0.5) / CAP))
            ok = allowed(key_place + begin * ROWS, tag_row, tag_ref[side], where)
            e = jnp.where(ok, jnp.exp(CAP * bent), 0.0)
            mass[side] += jnp.sum(e, axis=-1, keepdims=True)
            acc[side] += nn(e.astype(BF), values)

    for k in both:
        for side in both:
            send_line(side, k)
    for k in both:
        for side in both:
            attend(side, k, sides[side][4])
    for k in both:
        for side in both:
            relay_line(side, k)
    for k in both:
        for side in both:
            attend(side, k, sides[side][5][0])
            attend(side, k, sides[side][5][2])
    for side in both:
        for k in both:
            arrive(passed[side, k])
            attend(side, k, sides[side][5][1])
    load(ga, all_a)
    load(gb, all_b)

    band_y = pl.ds(pl.multiple_of(y * 256, 256), 256)
    sums = Summed(post, part, t1, th, t2, c, mate, far)
    carried = []
    loads[4].wait()

    def project(m):
        out = acc[m] / mass[m]
        att[m] = out
        lse_ref[m] = jnp.log(mass[m])
        low = out.astype(BF)
        flat[m] = jnp.concatenate([low[:ROWS], low[ROWS:]], axis=1)
        a = wo[...] if m == 0 else narrow(wo[...])
        part[m] = (nn(flat[m], a) * scale_mid).astype(BF)

    def spread(m):
        land = ca_land.at[y, pl.ds(m * ROWS, ROWS)]
        load(flat.at[m], land)
        return [post(flat.at[m], land, ys[j]) for j in range(3)]

    def norms(m):
        def slab(i, carry):
            r = pl.ds(pl.multiple_of(i * 16, 16), 16)
            v = branch[m, r].astype(F32)
            q = lax.rsqrt(jnp.mean(v * v, axis=-1, keepdims=True) + EPS)
            mid = tok[m, r].astype(F32) + v * q * norms_ref[1:2]
            middle[m, r] = mid
            q = lax.rsqrt(jnp.mean(mid * mid, axis=-1, keepdims=True) + EPS)
            ffn_in[m, r] = (mid * q * norms_ref[2:3]).astype(BF)
            return carry

        lax.fori_loop(0, ROWS // 16, slab, 0)
        fill_turned(ft, ffn_in[m], m)

    project(0)
    one = sums.start(0)
    carried += [post(dn.at[:, yi[j]], dn_land.at[:, :, band_y], ys[j]) for j in range(3)]
    load(dn.at[:, y], dn_land.at[:, :, band_y])
    two0 = sums.across(0, one)
    project(1)
    one = sums.start(1)
    two1 = sums.across(1, one)
    carried += spread(0)
    carried += spread(1)
    three = sums.back(0, two0, branch, 0)
    arrive(three)
    norms(0)
    three = sums.back(1, two1, branch, 1)
    arrive(three)
    norms(1)
    arrive(carried)
    for copy in local[5:]:
        copy.wait()
    for copy in copies:
        copy.wait_send()


def front(norms, cosine, sine, tags, tag, tok, wq, wk, wv, wo, scale_in, scale_mid):
    def kernel(*refs):
        front_kernel(*refs, scale_in, scale_mid)

    any_ = whole(pl.ANY)
    both = (2, ROWS, D)
    heads = (2, 2 * ROWS, HD)
    kv = (2, 4, 4, TAGROW + 16, HD)
    turned = (2, 4, 288, 2 * ROWS)
    sems = 34 + 2 * 3 * (HALF // STEP_ROWS) + 9
    return pl.pallas_call(
        kernel,
        out_shape=[
            jax.ShapeDtypeStruct(both, F32),
            jax.ShapeDtypeStruct(both, BF),
            jax.ShapeDtypeStruct(both, BF),
            jax.ShapeDtypeStruct(heads, BF),
            jax.ShapeDtypeStruct(heads, F32),
            jax.ShapeDtypeStruct((2, 2 * ROWS, 1), F32),
            jax.ShapeDtypeStruct(turned, BF),
            jax.ShapeDtypeStruct(kv, BF),
            jax.ShapeDtypeStruct(kv, BF),
            jax.ShapeDtypeStruct((2, 288, 1024), BF),
            jax.ShapeDtypeStruct((4, 2 * ROWS, 2 * HD), BF),
        ],
        in_specs=[whole()] * 5 + [any_] * 5,
        out_specs=[whole()] * 7 + [any_] * 4,
        scratch_shapes=[
            VMEM(both, BF),
            VMEM(wq.shape, BF),
            VMEM(wk.shape, BF),
            VMEM(wv.shape, BF),
            VMEM(wo.shape, BF),
            VMEM(both, BF),
            VMEM(turned, BF),
            VMEM((2, ROWS, 2 * HD), BF),
            VMEM(kv, BF),
            VMEM(kv, BF),
            VMEM(heads, F32),
            VMEM((2, 2 * ROWS, 1), F32),
            VMEM(both, BF),
            VMEM((2, HALF, D), BF),
            VMEM((2, HALF, D), BF),
            VMEM((2, HALF, D), BF),
            pltpu.SemaphoreType.DMA((10,)),
            pltpu.SemaphoreType.DMA((sems,)),
            pltpu.SemaphoreType.DMA((sems,)),
        ],
        compiler_params=params(1, 60),
    )(norms, cosine, sine, tags, tag, tok, wq, wk, wv, wo)


LTILE = 256
FTILE = 768
ROOT = (2.0 / 3.141592653589793) ** 0.5
CUBE = 0.044715


def narrow(codes):
    level = codes * BF(1.0 / 16.0) + BF(1.0 / 32.0)
    level = (level + BF(192.0)) - BF(192.0)
    return jnp.minimum(level, BF(7.0)) * BF(16.0)


def ffn_kernel(
    x_ref, gain_ref, wg_in, wu_in, wd_in, middle_in, up_in, dg_own, du_own,
    out_ref, dup_ref, total_ref, gains, ch, dd_land, dg_land, du_land, cg, cu,
    wg, wu, wd, middle, upstream, gate_s, up_s, hid, dgate_ref, acc, part, low, dd,
    t1, th, t2, down_sum,
    wsem, lsem, ssem, rsem,
    scale_in, scale_out,
):
    x, y, z, zh, c = place_of()
    xi = [(x + j) % 4 for j in (1, 2, 3)]
    yi = [(y + j) % 4 for j in (1, 2, 3)]
    xs = [device_at(i, y, z, zh, c) for i in xi]
    ys = [device_at(x, i, z, zh, c) for i in yi]
    mate = device_at(x, y, z, zh, 1 - c)
    far = device_at(x, y, z, 1 - zh, c)
    tiles = wg.shape[1] // FTILE
    copies, local = [], []
    post = poster(ssem, rsem, copies)
    load = loader(lsem, local)

    def weight_copies(t):
        span = pl.ds(pl.multiple_of(t * LTILE, LTILE), LTILE)
        return (
            pltpu.make_async_copy(wg_in.at[:, span], wg.at[:, span], wsem.at[0, t]),
            pltpu.make_async_copy(wu_in.at[:, span], wu.at[:, span], wsem.at[1, t]),
            pltpu.make_async_copy(wd_in.at[span], wd.at[span], wsem.at[2, t]),
        )

    def start_weights(t, carry):
        for copy in weight_copies(t):
            copy.start()
        return carry

    lax.fori_loop(0, wg.shape[1] // LTILE, start_weights, 0)
    loads = [load(middle_in, middle), load(up_in, upstream)]
    greet(xs + ys + [mate, far])
    band_x = pl.ds(pl.multiple_of(x * 256, 256), 256)
    band_y = pl.ds(pl.multiple_of(y * 256, 256), 256)
    carried = [post(dg_own.at[xi[j]], dg_land.at[:, band_x], xs[j]) for j in range(3)]
    mine = pl.ds(pl.multiple_of(c * ROWS, ROWS), ROWS)
    mine_y = pl.ds(pl.multiple_of(y * 256 + c * ROWS, ROWS), ROWS)
    du_sent = [post(du_own.at[:, yi[j], :, mine], du_land.at[:, :, mine_y], ys[j]) for j in range(3)]
    load(dg_own.at[x], dg_land.at[:, band_x])
    load(du_own.at[:, y], du_land.at[:, :, band_y])

    def forward(m, first, last, wait=False):
        def body(t, carry):
            span = pl.ds(pl.multiple_of(t * FTILE, FTILE), FTILE)
            if wait:
                for k in range(FTILE // LTILE):
                    for copy in weight_copies(t * (FTILE // LTILE) + k):
                        copy.wait()
            a, b, d = wg[:, span], wu[:, span], wd[span]
            if m == 1:
                a, b, d = narrow(a), narrow(b), narrow(d)
            gate = nn(x_ref[m], a) * scale_in
            up = nn(x_ref[m], b) * scale_in
            gate_s[m, :, span] = gate
            up_s[m, :, span] = up
            bent = jnp.tanh(ROOT * (gate + CUBE * gate * gate * gate))
            hidden = (0.5 * gate * (1.0 + bent) * up).astype(BF)
            hid[m, :, span] = hidden
            acc[...] += nn(hidden, d)
            return carry

        lax.fori_loop(first, last, body, 0)

    def backward(m, first, last):
        def body(t, carry):
            span = pl.ds(pl.multiple_of(t * FTILE, FTILE), FTILE)
            a, b, d = wg[:, span], wu[:, span], wd[span]
            if m == 1:
                a, b, d = narrow(a), narrow(b), narrow(d)
            grad = nt(low[m], d) * scale_out
            v, u = gate_s[m, :, span], up_s[m, :, span]
            bent = jnp.tanh(ROOT * (v + CUBE * v * v * v))
            half = 0.5 * (1.0 + bent)
            slope = half + 0.5 * v * (1.0 - bent * bent) * (ROOT * (1.0 + 3.0 * CUBE * v * v))
            dgate = (grad * u * slope).astype(BF)
            dup = (grad * (v * half)).astype(BF)
            dgate_ref[m, :, span] = dgate
            dup_ref[m, :, span] = dup
            acc[...] += nt(dgate, a) + nt(dup, b)
            return carry

        lax.fori_loop(first, last, body, 0)

    pieces = [pl.ds(k * STEP_ROWS, STEP_ROWS) for k in range(HALF // STEP_ROWS)]

    def at_rows(core, k):
        return pl.ds(pl.multiple_of(core * HALF + k * STEP_ROWS, STEP_ROWS), STEP_ROWS)

    def sum_start(i, m):
        return [post(part.at[i, at_rows(1 - c, k)], t1.at[i, r], mate) for k, r in enumerate(pieces)]

    def sum_across(i, one):
        sent = []
        for k, r in enumerate(pieces):
            one[k].wait_recv()
            th[i, r] = (part[i, at_rows(c, k)].astype(F32) + t1[i, r].astype(F32)).astype(BF)
            sent.append(post(th.at[i, r], t2.at[i, r], far))
        return sent

    def sum_back(i, two, dst, m):
        sent = []
        for k, r in enumerate(pieces):
            two[k].wait_recv()
            dst[m, at_rows(c, k)] = (th[i, r].astype(F32) + t2[i, r].astype(F32)).astype(BF)
            sent.append(post(dst.at[m, at_rows(c, k)], dst.at[m, at_rows(c, k)], mate))
        return sent

    def arrive(sent):
        for copy in sent:
            copy.wait_recv()

    def spread_hidden(m):
        land = ch.at[y, pl.ds(m * ROWS, ROWS)]
        load(hid.at[m], land)
        return [post(hid.at[m], land, ys[j]) for j in (0, 2)]

    def spread_gate(m):
        land = cg.at[x, pl.ds(m * ROWS, ROWS)]
        load(dgate_ref.at[m], land)
        return [post(dgate_ref.at[m], land, xs[j]) for j in (0, 2)]

    def relay_rows(m, sent, land, places, devices):
        for k, j in ((0, 0), (1, 2)):
            sent[k].wait_recv()
            half = land.at[places[2 - j], pl.ds(m * ROWS + k * HALF, HALF)]
            carried.append(post(half, half, devices[j]))

    def norm(m, sums):
        def slab(i, carry):
            r = pl.ds(pl.multiple_of(i * 16, 16), 16)
            v = down_sum[m, r].astype(F32)
            du = upstream[m, r].astype(F32)
            q = lax.rsqrt(jnp.mean(v * v, axis=-1, keepdims=True) + EPS)
            gain = gain_ref[3:4]
            out_ref[m, r] = (middle[m, r] + v * q * gain).astype(BF)
            lifted = du * gain
            back = q * lifted - v * (q * q * q * jnp.mean(lifted * v, axis=-1, keepdims=True))
            low[m, r] = back.astype(BF)
            return carry + jnp.sum(du * v * q, axis=0, keepdims=True)

        return lax.fori_loop(0, ROWS // 16, slab, sums)

    def swap_down(m):
        turned = low[m].T
        for zi in range(2):
            for k in range(4):
                at = (zi * 4 + k) * 288
                dd[m, zi, k] = turned[at : at + 288]
        band = pl.ds(pl.multiple_of(y * 256, 256) + m * ROWS, ROWS)
        load(dd.at[m, :, y], dd_land.at[:, :, band])

    acc[...] = jnp.zeros_like(acc)
    forward(0, 0, tiles, True)
    part[0] = (acc[...] * scale_out).astype(BF)
    one = sum_start(0, 0)
    hidden0 = spread_hidden(0)
    acc[...] = jnp.zeros_like(acc)
    forward(1, 0, 1)
    two = sum_across(0, one)
    forward(1, 1, tiles)
    part[1] = (acc[...] * scale_out).astype(BF)
    one = sum_start(1, 1)
    hidden1 = spread_hidden(1)
    three = sum_back(0, two, down_sum, 0)
    two = sum_across(1, one)
    arrive(three)
    for copy in loads:
        copy.wait()
    sums = norm(0, jnp.zeros((1, D), F32))
    relay_rows(0, hidden0, ch, yi, ys)
    carried += share(post, du_sent, du_land, yi, ROWS, c, mate)
    swap_down(0)
    acc[...] = jnp.zeros_like(acc)
    backward(0, 0, 2)
    relay_rows(1, hidden1, ch, yi, ys)
    backward(0, 2, tiles)
    part[2] = (acc[...] * scale_in).astype(BF)
    one = sum_start(2, 0)
    gate0 = spread_gate(0)
    up_sent = [post(dup_ref.at[0], cu.at[y], ys[j]) for j in (0, 2)]
    load(dup_ref.at[0], cu.at[y])
    three = sum_back(1, two, down_sum, 1)
    two = sum_across(2, one)
    arrive(three)
    gains[...] = norm(1, sums)
    swap_down(1)
    dd_sent = [post(dd.at[c, :, yi[j]], dd_land.at[:, :, mine_y], ys[j]) for j in range(3)]
    acc[...] = jnp.zeros_like(acc)
    backward(1, 0, tiles)
    part[3] = (acc[...] * scale_in).astype(BF)
    one = sum_start(3, 1)
    gate1 = spread_gate(1)
    carried += share(post, dd_sent, dd_land, yi, ROWS, c, mate)
    relay_rows(0, gate0, cg, xi, xs)
    carried += relay(post, up_sent, cu, yi, ys)
    three = sum_back(2, two, total_ref, 0)
    two = sum_across(3, one)
    arrive(three)
    three = sum_back(3, two, total_ref, 1)
    arrive(three)
    arrive(gate1)
    arrive(carried)
    for copy in local[2:]:
        copy.wait()
    for copy in copies:
        copy.wait_send()


def ffn(x, gain, wg, wu, wd, middle, up, dg, du, scale_in, scale_out):
    def kernel(*refs):
        ffn_kernel(*refs, scale_in, scale_out)

    any_ = whole(pl.ANY)
    both = (2, ROWS, D)
    loads = wg.shape[1] // LTILE
    sems = 3 + 4 * 3 * (HALF // STEP_ROWS) + 8 + 6 + 6 + 12
    return pl.pallas_call(
        kernel,
        out_shape=[
            jax.ShapeDtypeStruct(both, BF),
            jax.ShapeDtypeStruct(both, BF),
            jax.ShapeDtypeStruct(both, BF),
            jax.ShapeDtypeStruct((1, D), F32),
            jax.ShapeDtypeStruct((4, 2 * ROWS, D), BF),
            jax.ShapeDtypeStruct((2, 288, 1024), BF),
            jax.ShapeDtypeStruct((PART, 1024), BF),
            jax.ShapeDtypeStruct((2, 288, 1024), BF),
            jax.ShapeDtypeStruct((4, 2 * ROWS, D), BF),
            jax.ShapeDtypeStruct((4, ROWS, D), BF),
        ],
        in_specs=[whole()] * 2 + [any_] * 7,
        out_specs=[whole()] * 4 + [any_] * 6,
        scratch_shapes=[
            VMEM(wg.shape, BF),
            VMEM(wu.shape, BF),
            VMEM(wd.shape, BF),
            VMEM(both, F32),
            VMEM(both, BF),
            VMEM(both, F32),
            VMEM(both, F32),
            VMEM(both, BF),
            VMEM(both, BF),
            VMEM((ROWS, D), F32),
            VMEM((4, ROWS, D), BF),
            VMEM(both, BF),
            VMEM((2, 2, 4, 288, ROWS), BF),
            VMEM((4, HALF, D), BF),
            VMEM((4, HALF, D), BF),
            VMEM((4, HALF, D), BF),
            VMEM(both, BF),
            pltpu.SemaphoreType.DMA((3, loads)),
            pltpu.SemaphoreType.DMA((11,)),
            pltpu.SemaphoreType.DMA((sems,)),
            pltpu.SemaphoreType.DMA((sems,)),
        ],
        compiler_params=params(5, 63),
    )(x, gain, wg, wu, wd, middle, up, dg, du)


PART = 576
SHARE = 72


def norm_grad(v, gain, grad):
    q = lax.rsqrt(jnp.mean(v * v, axis=-1, keepdims=True) + EPS)
    lifted = grad * gain
    back = q * lifted - v * (q * q * q * jnp.mean(lifted * v, axis=-1, keepdims=True))
    return back, jnp.sum(grad * v * q, axis=0, keepdims=True)


def mid_kernel(
    total_ref, norms_ref, q_ref, lse_ref, tag_ref, att_ref,
    middle_in, branch_in, up_in, wo_in, k_in, v_in, ch_in, dd_in, cu_own, cg_in,
    out_a, out_b, dq_ref, mgrad, gains, od, cu, db_land, cg_far,
    middle, branch, upstream, wo, k_ref, v_ref, ch, dd, bt, pd, rd, sd, zd, blow, g_ref, dk, dv,
    r1a, r1b, s1a, s1b, r2a, r2b, s2a, s2b, r3a, r3b,
    lsem, ssem, rsem,
    scale,
):
    x, y, z, zh, c = place_of()
    xi = [(x + j) % 4 for j in (1, 2, 3)]
    yi = [(y + j) % 4 for j in (1, 2, 3)]
    xs = [device_at(i, y, z, zh, c) for i in xi]
    ys = [device_at(x, i, z, zh, c) for i in yi]
    zp = device_at(x, y, 1 - z, zh, c)
    copies, local = [], []
    post = poster(ssem, rsem, copies)

    def load(src, dst):
        copy = pltpu.make_async_copy(src, dst, lsem.at[len(local)])
        copy.start()
        local.append(copy)
        return copy

    loads = [
        load(*pair)
        for pair in (
            (middle_in, middle), (branch_in, branch), (up_in, upstream), (wo_in, wo),
            (ch_in, ch), (dd_in, dd), (k_in, k_ref), (v_in, v_ref),
        )
    ]
    mate = device_at(x, y, z, zh, 1 - c)
    greet(xs + ys + [zp, mate])
    up_sent = [post(cu_own.at[1], cu.at[y], ys[j]) for j in (0, 2)]
    carried = []
    for k, j in ((0, 0), (1, 2)):
        half = pl.ds(k * HALF, HALF)
        source = cg_in.at[xi[2 - j], pl.ds(ROWS + k * HALF, HALF)]
        carried.append(post(source, cg_far.at[half], xs[j]))
    load(cu_own.at[1], cu.at[y])
    for copy in loads[:4]:
        copy.wait()

    zero = jnp.zeros((1, D), F32)
    for m in range(2):

        def slab(i, carry):
            sum_mid, sum_out = carry
            r = pl.ds(pl.multiple_of(i * 16, 16), 16)
            back, more = norm_grad(middle[m, r], norms_ref[2:3], total_ref[m, r].astype(F32))
            grad = upstream[m, r].astype(F32) + back
            mgrad[m, r] = grad
            back, most = norm_grad(branch[m, r].astype(F32), norms_ref[1:2], grad)
            blow[m, r] = back.astype(BF)
            return sum_mid + more, sum_out + most

        sums = lax.fori_loop(0, ROWS // 16, slab, (zero, zero) if m == 0 else sums)
    gains[0:1] = sums[1]
    gains[1:2] = sums[0]
    for m in range(2):
        weight = wo[...] if m == 0 else narrow(wo[...])
        wide = (nt(blow[m], weight) * scale).astype(BF)
        g_ref[m, :ROWS] = wide[:, :HD]
        g_ref[m, ROWS:] = wide[:, HD:]
        turned = blow[m].T
        for zi in range(2):
            for k in range(4):
                at = (zi * 4 + k) * 288
                bt[zi, k, :, m * ROWS : (m + 1) * ROWS] = turned[at : at + 288]

    band_y = pl.ds(pl.multiple_of(y * 256, 256), 256)
    mine = pl.ds(pl.multiple_of(c * ROWS, ROWS), ROWS)
    mine_y = pl.ds(pl.multiple_of(y * 256 + c * ROWS, ROWS), ROWS)
    db_sent = [post(bt.at[:, yi[j], :, mine], db_land.at[:, :, mine_y], ys[j]) for j in range(3)]
    load(bt.at[:, y], db_land.at[:, :, band_y])
    loads[6].wait()
    loads[7].wait()
    where = query_places()
    block = lax.axis_index("blk")
    lane = lax.broadcasted_iota(jnp.int32, (2 * ROWS, KEYS), 1)
    offsets = [jnp.sum(g_ref[m].astype(F32) * att_ref[m], axis=-1, keepdims=True) for m in range(2)]
    dq_ref[...] = jnp.zeros_like(dq_ref)

    def chunk(m, level, i):
        if m == 0:
            held, out, begin = k_ref.at[level, :, i], dk.at[level, :, i], level * 16 + i
            key_place = lane % ROWS + lane // ROWS * (4 * ROWS) + begin * ROWS
        else:
            held, out, begin = v_ref.at[level, i], dv.at[level, i], level * 16 + i * 4
            key_place = lane + begin * ROWS

        @pl.when(begin <= block)
        def _():
            q, g = q_ref[m], g_ref[m]
            keys = held[:, :ROWS, :].reshape(KEYS, HD)
            values = held[:, ROWS : 2 * ROWS, :].reshape(KEYS, HD)
            tags = held[:, TAGROW : TAGROW + 16, :ROWS].astype(F32)
            tag_row = jnp.concatenate([tags[k, 0:1, :] for k in range(CHUNK)], axis=1)
            bent = jnp.tanh(nt(q, keys) * (HD ** (-0.5) / CAP))
            ok = allowed(key_place, tag_row, tag_ref[m], where)
            p = jnp.where(ok, jnp.exp(CAP * bent - lse_ref[m]), 0.0)
            dp = nt(g, values)
            ds = (p * (dp - offsets[m]) * (1.0 - bent * bent) * HD ** (-0.5)).astype(BF)
            out[:, :ROWS, :] = tn(ds, q).astype(BF).reshape(CHUNK, ROWS, HD)
            out[:, ROWS:, :] = tn(p.astype(BF), g).astype(BF).reshape(CHUNK, ROWS, HD)
            dq_ref[m] += nn(ds, keys)

        @pl.when(begin > block)
        def _():
            out[...] = jnp.zeros(out.shape, BF)

    ring_a = Ring(post, lambda level, i: dk.at[level, :, i], r1a, x, xi, xs, add_blocks)
    ring_b = Ring(post, lambda level, i: dv.at[level, i], r1b, y, yi, ys, add_blocks)
    rings = (ring_a, ring_b)
    for k in range(4):
        for m in range(2):
            chunk(m, *rings[m].order[k])
            rings[m].begin()
        if k == 1:
            carried += relay(post, up_sent, cu, yi, ys)
    for m, places in ((0, xi), (1, yi)):
        chunk(m, 0, places[0])
        chunk(m, 1, places[2])
    for m, own in ((0, x), (1, y)):
        chunk(m, 0, own)
        chunk(m, 1, own)
    loads[4].wait()
    loads[5].wait()
    multiply(dd, ch, pd, D, 0, 768)
    carried += share(post, db_sent, db_land, yi, ROWS, c, mate)
    ring_a.onward()
    ring_b.onward()
    ring_d = Ring(post, lambda level, i: pd.at[level, i], rd, x, xi, xs, add_columns).begin_all()
    ring_a.close(s1a)
    two_a = [post(s1a.at[:, yi[j]], r2a.at[j], ys[j]) for j in range(3)]
    ring_b.close(s1b)
    two_b = [post(s1b.at[:, xi[j]], r2b.at[j], xs[j]) for j in range(3)]
    ring_d.onward()

    def second(arrivals, own, mine, land, half):
        for copy in arrivals:
            copy.wait_recv()
        for zi in range(2):
            out = own[zi, mine].astype(F32)
            for j in range(3):
                out = out + land[j, zi].astype(F32)
            half[zi] = out.astype(BF)

    second(two_a, s1a, y, r2a, s2a)
    three_a = post(s2a.at[1 - z], r3a, zp)
    second(two_b, s1b, x, r2b, s2b)
    three_b = post(s2b.at[1 - z], r3b, zp)
    ring_d.close(sd)
    three_d = post(sd.at[1 - z], zd, zp)
    three_a.wait_recv()
    out_a[...] = s2a[z].astype(F32) + r3a[...].astype(F32)
    three_b.wait_recv()
    out_b[...] = s2b[z].astype(F32) + r3b[...].astype(F32)
    three_d.wait_recv()
    od[...] = sd[z].astype(F32) + zd[...].astype(F32)
    for copy in carried:
        copy.wait_recv()
    for copy in local[8:]:
        copy.wait()
    for copy in copies:
        copy.wait_send()


def mid(total_in, norms, q, lse, tag, att, middle, branch, up, wo, k, v, ch, dd, cu, cg, scale):
    def kernel(*refs):
        mid_kernel(*refs, scale)

    any_ = whole(pl.ANY)
    tile = (2 * ROWS, HD)
    wide = (4, ROWS, D)
    sems = 4 + 2 + 12 + 6 + 2 + 6 + 7
    return pl.pallas_call(
        kernel,
        out_shape=[
            jax.ShapeDtypeStruct(tile, F32),
            jax.ShapeDtypeStruct(tile, F32),
            jax.ShapeDtypeStruct((2,) + tile, F32),
            jax.ShapeDtypeStruct((2, ROWS, D), F32),
            jax.ShapeDtypeStruct((2, D), F32),
            jax.ShapeDtypeStruct((SHARE, D), F32),
            jax.ShapeDtypeStruct(wide, BF),
            jax.ShapeDtypeStruct((2, 288, 1024), BF),
            jax.ShapeDtypeStruct((ROWS, D), BF),
        ],
        in_specs=[whole()] * 6 + [any_] * 10,
        out_specs=[whole()] * 6 + [any_] * 3,
        scratch_shapes=[
            VMEM(middle.shape, F32),
            VMEM(branch.shape, BF),
            VMEM(up.shape, BF),
            VMEM(wo.shape, BF),
            VMEM(k.shape, BF),
            VMEM(v.shape, BF),
            VMEM(ch.shape, BF),
            VMEM(dd.shape, BF),
            VMEM((2, 4, 288, 2 * ROWS), BF),
            VMEM((2, 4, SHARE, D), BF),
            VMEM((6, SHARE, D), BF),
            VMEM((2, SHARE, D), BF),
            VMEM((SHARE, D), BF),
            VMEM((2, ROWS, D), BF),
            VMEM((2,) + tile, BF),
            VMEM((2, 4, 4) + tile, BF),
            VMEM((2, 4, 4) + tile, BF),
            VMEM((6, 4) + tile, BF),
            VMEM((6, 4) + tile, BF),
            VMEM((2, 4) + tile, BF),
            VMEM((2, 4) + tile, BF),
            VMEM((3, 2) + tile, BF),
            VMEM((3, 2) + tile, BF),
            VMEM((2,) + tile, BF),
            VMEM((2,) + tile, BF),
            VMEM(tile, BF),
            VMEM(tile, BF),
            pltpu.SemaphoreType.DMA((11,)),
            pltpu.SemaphoreType.DMA((sems,)),
            pltpu.SemaphoreType.DMA((sems,)),
        ],
        compiler_params=params(2, 63),
    )(total_in, norms, q, lse, tag, att, middle, branch, up, wo, k, v, ch, dd, cu, cg)


def end_kernel(
    kv_a, kv_b, dq_ref, cos_ref, sin_ref, gain_in, gains_in,
    wq_in, wk_in, wv_in, tok_in, mgrad_in, dg_in, cg_in, cg_far, du_in, cu0_in, cu1_in, dn_in, db_in, ca_in,
    igrad, og, ou, oq, on,
    wq, wk, wv, tok, mgrad, dg, cg, du, cu, dn, db, ca, cq,
    part, t1, th, t2, total_ref, gpad, gb, rgb,
    pg, pu, pq, pn, rg, ru, rq, rn, sg, su, sq, sn, zg, zu, zq, zn,
    lsem, ssem, rsem,
    scale,
):
    x, y, z, zh, c = place_of()
    xi = [(x + j) % 4 for j in (1, 2, 3)]
    yi = [(y + j) % 4 for j in (1, 2, 3)]
    xs = [device_at(i, y, z, zh, c) for i in xi]
    ys = [device_at(x, i, z, zh, c) for i in yi]
    zp = device_at(x, y, 1 - z, zh, c)
    mate = device_at(x, y, z, zh, 1 - c)
    far = device_at(x, y, z, 1 - zh, c)
    copies, local = [], []
    post = poster(ssem, rsem, copies)
    load = loader(lsem, local)

    first, second = pl.ds(0, ROWS), pl.ds(ROWS, ROWS)
    weights = [load(*pair) for pair in ((wq_in, wq), (wk_in, wk), (wv_in, wv))]
    got_u = [load(du_in, du), load(cu0_in, cu.at[:, first]), load(cu1_in, cu.at[:, second])]
    got_g = [load(dg_in, dg), load(cg_far, cg.at[xi[1], second]), load(cg_in.at[xi[1], first], cg.at[xi[1], first])]
    got_g += [load(cg_in.at[i], cg.at[i]) for i in (x, xi[0], xi[2])]
    got_t = [load(tok_in, tok), load(mgrad_in, mgrad)]
    got_q = [load(dn_in, dn), load(ca_in, ca), load(db_in, db)]
    greet(xs + ys + [zp, mate, far])

    for m in range(2):
        r = slice(m * ROWS, (m + 1) * ROWS)
        cosine, sine = cos_ref[...], -sin_ref[...]
        for h in range(2):
            turned = turn(dq_ref[m, h * ROWS : (h + 1) * ROWS], cosine, sine)
            cq[y, r, h * HD : (h + 1) * HD] = turned.astype(BF)
        both = (kv_a, kv_b)[m]
        cq[y, r, 2 * HD : 3 * HD] = turn(both[:ROWS], cosine, sine).astype(BF)
        cq[y, r, 3 * HD :] = both[ROWS:].astype(BF)
    cq_sent = [post(cq.at[y], cq.at[y], ys[j]) for j in (0, 2)]
    for copy in weights:
        copy.wait()
    for m in range(2):
        r = slice(m * ROWS, (m + 1) * ROWS)
        a, b, v = wq[...], wk[...], wv[...]
        if m == 1:
            a, b, v = narrow(a), narrow(b), narrow(v)
        out = nt(cq[y, r, : 2 * HD], a) + nt(cq[y, r, 2 * HD : 3 * HD], b) + nt(cq[y, r, 3 * HD :], v)
        part[m] = (out * scale).astype(BF)
    sums = Summed(post, part, t1, th, t2, c, mate, far)
    ones = [sums.start(0), sums.start(1)]
    twos = [sums.across(m, ones[m]) for m in range(2)]

    def ring(p, land, along):
        if along == "x":
            return Ring(post, lambda level, i: p.at[level, i], land, x, xi, xs, add_columns).begin_all()
        return Ring(post, lambda level, i: p.at[level, i], land, y, yi, ys, add_columns).begin_all()

    def swap(done, half, across):
        done.close(half)
        return post(half.at[1 - z], across, zp)

    def finish(copy, half, across, out):
        copy.wait_recv()
        out[...] = half[z].astype(F32) + across[...].astype(F32)

    for copy in got_u:
        copy.wait()
    multiply(du, cu, pu, D, 0, 768)
    ring_u = ring(pu, ru, "x")
    cq_far = relay(post, cq_sent, cq, yi, ys)
    for copy in got_g:
        copy.wait()
    multiply(dg, cg, pg, D, 0, 768)
    ring_g = ring(pg, rg, "y")
    for copy in got_q:
        copy.wait()
    arrive(cq_far)
    multiply(dn, cq, pq, 1024, 0, 512)
    multiply(db, ca, pq, 512, 1024, 512)
    ring_q = ring(pq, rq, "x")

    threes = [sums.back(m, twos[m], total_ref, m) for m in range(2)]
    for copy in got_t:
        copy.wait()
    sums_in = jnp.zeros((1, D), F32)
    for m in range(2):
        arrive(threes[m])

        def slab(i, carry):
            r = pl.ds(pl.multiple_of(i * 16, 16), 16)
            back, more = norm_grad(tok[m, r].astype(F32), gain_in[0:1], total_ref[m, r].astype(F32))
            igrad[m, r] = (mgrad[m, r] + back).astype(BF)
            return carry + more

        sums_in = lax.fori_loop(0, ROWS // 16, slab, sums_in)
    gpad[...] = jnp.zeros_like(gpad)
    gpad[0:1] = sums_in
    gpad[1:4] = gains_in[...]
    turned = gpad[...].T.astype(BF)
    for zi in range(2):
        for k in range(4):
            at = (zi * 4 + k) * 288
            gb[zi, k] = turned[at : at + 288]
    gains_far = [post(gb.at[:, yi[j]], rgb.at[j], ys[j]) for j in range(3)]

    ring_u.onward()
    ring_g.onward()
    ring_q.onward()
    out = gb[:, y].astype(F32)
    for j in range(3):
        gains_far[j].wait_recv()
        out = out + rgb[j].astype(F32)
    pn[...] = out.reshape(2, 4, SHARE, 128).astype(BF)
    ring_n = ring(pn, rn, "x")
    three_u = swap(ring_u, su, zu)
    three_g = swap(ring_g, sg, zg)
    ring_n.onward()
    three_q = swap(ring_q, sq, zq)
    three_n = swap(ring_n, sn, zn)
    finish(three_u, su, zu, ou)
    finish(three_g, sg, zg, og)
    finish(three_q, sq, zq, oq)
    finish(three_n, sn, zn, on)
    for copy in copies:
        copy.wait_send()


def end(
    kv_a, kv_b, dq, cosine, sine, norms, gains, wq, wk, wv, tok, mgrad, dg, cg, cg_far, du, cu0, cu1, dn, db, ca, scale
):
    def kernel(*refs):
        end_kernel(*refs, scale)

    widths = (D, D, 1536, 128)
    sems = 4 + 2 * 3 * (HALF // STEP_ROWS) + 3 + 4 * 7
    both = (4, 2 * ROWS, D)
    return pl.pallas_call(
        kernel,
        out_shape=[jax.ShapeDtypeStruct((2, ROWS, D), BF)]
        + [jax.ShapeDtypeStruct((SHARE, w), F32) for w in widths],
        in_specs=[whole()] * 7 + [whole(pl.ANY)] * 14,
        out_specs=[whole()] * 5,
        scratch_shapes=[
            VMEM(wq.shape, BF),
            VMEM(wk.shape, BF),
            VMEM(wv.shape, BF),
            VMEM(tok.shape, BF),
            VMEM(mgrad.shape, F32),
            VMEM(dg.shape, BF),
            VMEM(both, BF),
            VMEM(du.shape, BF),
            VMEM(both, BF),
            VMEM(dn.shape, BF),
            VMEM(db.shape, BF),
            VMEM(ca.shape, BF),
            VMEM((4, 2 * ROWS, 1024), BF),
            VMEM((2, ROWS, D), BF),
            VMEM((2, HALF, D), BF),
            VMEM((2, HALF, D), BF),
            VMEM((2, HALF, D), BF),
            VMEM((2, ROWS, D), BF),
            VMEM((128, D), F32),
            VMEM((2, 4, 288, 128), BF),
            VMEM((3, 2, 288, 128), BF),
        ]
        + [VMEM((2, 4, SHARE, w), BF) for w in widths]
        + [VMEM((6, SHARE, w), BF) for w in widths]
        + [VMEM((2, SHARE, w), BF) for w in widths]
        + [VMEM((SHARE, w), BF) for w in widths]
        + [
            pltpu.SemaphoreType.DMA((17,)),
            pltpu.SemaphoreType.DMA((sems,)),
            pltpu.SemaphoreType.DMA((sems,)),
        ],
        compiler_params=params(3, 62),
    )(kv_a, kv_b, dq, cosine, sine, norms, gains, wq, wk, wv, tok, mgrad, dg, cg, cg_far, du, cu0, cu1, dn, db, ca)


def shards(
    inputs,
    out_grad,
    segment_ids,
    keep_mask,
    query_codes,
    key_codes,
    value_codes,
    output_codes,
    gate_codes,
    up_codes,
    down_codes,
    norm_attn_in,
    norm_attn_out,
    norm_ffn_in,
    norm_ffn_out,
):
    rows = inputs.shape[1]
    place = lax.axis_index("blk") * rows + jnp.arange(rows, dtype=jnp.int32)
    freqs = 10000.0 ** (-jnp.arange(HD // 2, dtype=F32) * 2.0 / HD)
    angles = place.astype(F32)[:, None] * freqs[None, :]
    cosine = jnp.cos(angles)
    sine = jnp.sin(angles)
    in_scale = LEVEL_SCALE * D ** (-0.5)
    mid_scale = LEVEL_SCALE * (HEADS * HD) ** (-0.5)
    ff_scale = LEVEL_SCALE * FF ** (-0.5)

    norms = jnp.stack([norm_attn_in, norm_attn_out, norm_ffn_in, norm_ffn_out])
    key_tag = jnp.where(keep_mask == 1, segment_ids, -1).astype(BF)
    key_tag = jnp.concatenate([key_tag, jnp.zeros_like(key_tag)], axis=1)
    key_tag = jnp.broadcast_to(key_tag[:, None, :], (2, 16, 2 * rows))
    tag = segment_ids.astype(F32)
    tag = jnp.concatenate([tag, tag], axis=1)[:, :, None]
    (
        middle, branch, ffn_in, queries, attended, lse, ffn_turned, blocks_a, blocks_b, d_normed, all_attended,
    ) = front(
        norms, cosine, sine, key_tag, tag,
        inputs, query_codes, key_codes, value_codes, output_codes, in_scale, mid_scale,
    )
    out_rows, up_low, ffn_in_grad, gain_ffn_out, ch, d_down, d_gate, d_up, cg, cu0 = ffn(
        ffn_in, norms, gate_codes, up_codes, down_codes, middle, out_grad,
        ffn_turned.reshape(8, 4, SHARE, 2 * rows).transpose(1, 0, 2, 3).reshape(4, PART, 2 * rows),
        ffn_turned, in_scale, ff_scale,
    )
    kv_a, kv_b, query_rot, middle_grad, gains, g_down, cu1, d_branch, cg_far = mid(
        ffn_in_grad, norms, queries, lse, tag, attended,
        middle, branch, out_grad, output_codes, blocks_a, blocks_b,
        ch, d_down, up_low, cg, mid_scale,
    )
    gains = jnp.concatenate([gains, gain_ffn_out])
    input_grad, g_gate, g_up, g_rest, g_gains = end(
        kv_a, kv_b, query_rot, cosine, sine, norms, gains,
        query_codes, key_codes, value_codes, inputs, middle_grad,
        d_gate, cg, cg_far, d_up, cu0, cu1, d_normed, d_branch, all_attended, in_scale,
    )
    return (
        out_rows,
        input_grad,
        g_rest[:, :512] * in_scale,
        g_rest[:, 512:768] * in_scale,
        g_rest[:, 768:1024] * in_scale,
        g_rest[:, 1024:1536].T * mid_scale,
        g_gate * in_scale,
        g_up * in_scale,
        g_down.T * ff_scale,
        g_gains[:, 0],
        g_gains[:, 1],
        g_gains[:, 2],
        g_gains[:, 3],
    )


def solution(mesh):
    placed = (
        P(None, "blk", None),
        P(None, "blk", None),
        P(None, "blk"),
        P(None, "blk"),
        P(None, "tensor"),
        P(None, "tensor"),
        P(None, "tensor"),
        P("tensor", None),
        P(None, "tensor"),
        P(None, "tensor"),
        P("tensor", None),
        P(),
        P(),
        P(),
        P(),
    )
    return jax.shard_map(
        shards,
        mesh=mesh,
        in_specs=placed,
        out_specs=(
            P(None, "blk", None),
            P(None, "blk", None),
            P("blk", "tensor"),
            P("blk", "tensor"),
            P("blk", "tensor"),
            P("tensor", "blk"),
            P("blk", "tensor"),
            P("blk", "tensor"),
            P("tensor", "blk"),
            P("blk"),
            P("blk"),
            P("blk"),
            P("blk"),
        ),
        check_vma=False,
    )
```

```python
import functools

import jax
import jax.numpy as jnp
from jax import lax
from jax.experimental import pallas as pl
from jax.experimental.pallas import tpu as pltpu
from jax.sharding import PartitionSpec as P

D = 2304
HEADS = 8
HD = 256
FF = 9216

CAP = 50.0
EPS = 1e-06
LEVEL_SCALE = 1.0 / 74.0
WIDTHS = (8, 4, 2)

MESH = pl.DeviceIdType.MESH
VMEM = pltpu.VMEM
BF = jnp.bfloat16
F32 = jnp.float32
SEQ = 4096
ROWS = 128
TAGROW = 256
MASKED = -2.0


def place_of():
    b = lax.axis_index("blk")
    t = lax.axis_index("tensor")
    return b % 4, (b // 4) % 4, b // 16, t // 2, t % 2


def device_at(x, y, z, zh, c):
    return ((z * 4 + y) * 4 + x, zh * 2 + c)


def greet(peers):
    barrier = pltpu.get_barrier_semaphore()
    for peer in peers:
        pl.semaphore_signal(barrier, inc=1, device_id=peer, device_id_type=MESH)
    pl.semaphore_wait(barrier, len(peers))


def send(src, dst, ssem, rsem, peer):
    copy = pltpu.make_async_remote_copy(
        src_ref=src, dst_ref=dst, send_sem=ssem, recv_sem=rsem, device_id=peer, device_id_type=MESH
    )
    copy.start()
    return copy


def params(collective_id=None, limit=60):
    if collective_id is None:
        return pltpu.CompilerParams(vmem_limit_bytes=limit << 20)
    return pltpu.CompilerParams(
        vmem_limit_bytes=limit << 20, collective_id=collective_id, has_side_effects=True
    )


def whole(space=VMEM):
    return pl.BlockSpec(memory_space=space)


CHUNK = 4
KEYS = CHUNK * ROWS


def nt(left, right):
    return lax.dot_general(left, right, (((1,), (1,)), ((), ())), preferred_element_type=F32)


def tn(left, right):
    return lax.dot_general(left, right, (((0,), (0,)), ((), ())), preferred_element_type=F32)


def nn(left, right):
    return jnp.dot(left, right, preferred_element_type=F32)


def allowed(key_place, tag_row, query_tag, query_place):
    ok = (key_place <= query_place) & (tag_row == query_tag)
    return ok | (key_place == query_place)


def query_places():
    row = lax.broadcasted_iota(jnp.int32, (2 * ROWS, 1), 0)
    return lax.axis_index("blk") * ROWS + row % ROWS


class Later:
    def __init__(self, src, dst, ssem, rsem, k, peer):
        self.src, self.dst, self.ssem, self.rsem, self.k, self.peer = src, dst, ssem, rsem, k, peer

    def describe(self):
        return pltpu.make_async_remote_copy(
            src_ref=self.src(),
            dst_ref=self.dst(),
            send_sem=self.ssem.at[self.k],
            recv_sem=self.rsem.at[self.k],
            device_id=self.peer,
            device_id_type=MESH,
        )

    def wait_recv(self):
        self.describe().wait_recv()

    def wait_send(self):
        self.describe().wait_send()


def poster(ssem, rsem, copies):
    def post(src, dst, peer, later=False):
        k = len(copies)
        if later:
            copies.append(Later(src, dst, ssem, rsem, k, peer))
            copies[k].describe().start()
        else:
            copies.append(send(src, dst, ssem.at[k], rsem.at[k], peer))
        return copies[k]

    return post


def settle(copies, later=False):
    for copy in copies:
        if isinstance(copy, Later) == later:
            copy.wait_send()


def loader(sem, copies):
    def load(src, dst):
        copy = pltpu.make_async_copy(src, dst, sem.at[len(copies)])
        copy.start()
        copies.append(copy)
        return copy

    return load


def arrive(copies):
    for copy in copies:
        copy.wait_recv()


def turn(values, cosine, sine):
    half = HD // 2
    first, second = values[:, :half], values[:, half:]
    return jnp.concatenate([first * cosine - second * sine, second * cosine + first * sine], axis=1)


def fill_turned(dst, value, m):
    turned = value.T
    for zi in range(2):
        for k in range(4):
            at = (zi * 4 + k) * 288
            dst[zi, k, :, m * ROWS : (m + 1) * ROWS] = turned[at : at + 288]


HALF = ROWS // 2
STEP_ROWS = 32


class Summed:
    def __init__(self, post, part, t1, th, t2, c, mate, far):
        self.post, self.part, self.t1, self.th, self.t2 = post, part, t1, th, t2
        self.c, self.mate, self.far = c, mate, far
        self.pieces = [pl.ds(k * STEP_ROWS, STEP_ROWS) for k in range(HALF // STEP_ROWS)]

    def rows(self, core, k):
        return pl.ds(pl.multiple_of(core * HALF + k * STEP_ROWS, STEP_ROWS), STEP_ROWS)

    @staticmethod
    def piece(ref, i, r):
        return ref.at[i, r]

    def start(self, i):
        other = 1 - self.c
        return [
            self.post(self.part.at[i, self.rows(other, k)], self.t1.at[i, r], self.mate)
            for k, r in enumerate(self.pieces)
        ]

    def across(self, i, one):
        sent = []
        for k, r in enumerate(self.pieces):
            one[k].wait_recv()
            own = self.part[i, self.rows(self.c, k)].astype(F32)
            self.th[i, r] = (own + self.t1[i, r].astype(F32)).astype(BF)
            src, dst = functools.partial(self.piece, self.th, i, r), functools.partial(self.piece, self.t2, i, r)
            sent.append(self.post(src, dst, self.far, True))
        return sent

    def back(self, i, two, dst, m):
        sent = []
        for k, r in enumerate(self.pieces):
            two[k].wait_recv()
            rows = self.rows(self.c, k)
            dst[m, rows] = (self.th[i, r].astype(F32) + self.t2[i, r].astype(F32)).astype(BF)
            sent.append(self.post(dst.at[m, rows], dst.at[m, rows], self.mate))
        return sent


def relay(post, sent, land, places, devices):
    out = []
    size = land.shape[1] // 2
    for k, j in ((0, 0), (1, 2)):
        sent[k].wait_recv()
        half = functools.partial(lambda place, k: land.at[place, pl.ds(k * size, size)], places[2 - j], k)
        out.append(post(half, half, devices[j], True))
    return out


def share(post, sent, land, places, width, c, mate):
    def band(place):
        begin = pl.multiple_of(place * (2 * width), 2 * width) + c * width
        return land.at[:, :, pl.ds(pl.multiple_of(begin, width), width)]

    out = []
    for j, copy in enumerate(sent):
        copy.wait_recv()
        own = functools.partial(band, places[2 - j])
        out.append(post(own, own, mate, True))
    return out


class Ring:
    def __init__(self, post, held, land, mine, places, devices, add):
        self.post, self.land, self.mine, self.places, self.devices = post, land, mine, places, devices
        self.held, self.add = held, add
        near, across, far = places
        self.order = ((0, across), (1, across), (1, near), (0, far))
        self.sent = []

    def begin(self):
        k = len(self.sent)
        src = functools.partial(self.held, *self.order[k])
        dst = functools.partial(self.slot, k)
        self.sent.append(self.post(src, dst, self.devices[0 if k % 2 == 0 else 2], True))

    def slot(self, k):
        return self.land.at[k]

    def begin_all(self):
        for _ in self.order:
            self.begin()
        return self

    def onward(self):
        self.passed = []
        for level, j in ((0, 0), (1, 2)):
            self.sent[level].wait_recv()
            ref = self.held(level, self.places[j])
            self.add(ref, ref, (self.land.at[level],))
            src = functools.partial(self.held, level, self.places[j])
            dst = functools.partial(self.slot, 4 + level)
            self.passed.append(self.post(src, dst, self.devices[j], True))

    def close(self):
        for level in range(2):
            self.sent[3 - level].wait_recv()
            self.passed[level].wait_recv()
            own = self.held(level, self.mine)
            self.add(own, own, (self.land.at[3 - level], self.land.at[4 + level]))


def add_blocks(dst, own, others):
    def body(k, carry):
        out = own[k].astype(F32)
        for other in others:
            out = out + other[k].astype(F32)
        dst[k] = out.astype(BF)
        return carry

    lax.fori_loop(0, own.shape[0], body, 0)


def add_columns(dst, own, others):
    tile = 256 if own.shape[-1] % 256 == 0 else 128

    def body(t, carry):
        cols = pl.ds(pl.multiple_of(t * tile, tile), tile)
        out = own[:, cols].astype(F32)
        for other in others:
            out = out + other[:, cols].astype(F32)
        dst[:, cols] = out.astype(BF)
        return carry

    lax.fori_loop(0, own.shape[-1] // tile, body, 0)


CUT = 144


def front_kernel(
    norms_ref, cos_ref, sin_ref, tags, tag_ref,
    tok_in, wq_in, wk_in, wv_in, wo_in,
    middle, branch, ffn_in, q_ref, att, lse_ref, ft, all_a, all_b, dn_land, ca_land,
    tok, wq, wk, wv, wo, normed, dn, flat, ga, gb, acc, mass, part, t1, th, t2,
    lsem, ssem, rsem,
    scale_in, scale_mid,
):
    x, y, z, zh, c = place_of()
    block = lax.axis_index("blk")
    xi = [(x + j) % 4 for j in (1, 2, 3)]
    yi = [(y + j) % 4 for j in (1, 2, 3)]
    xs = [device_at(i, y, z, zh, c) for i in xi]
    ys = [device_at(x, i, z, zh, c) for i in yi]
    zp = device_at(x, y, 1 - z, zh, c)
    mate = device_at(x, y, z, zh, 1 - c)
    far = device_at(x, y, z, 1 - zh, c)
    copies, local = [], []
    post = poster(ssem, rsem, copies)
    load = loader(lsem, local)
    loads = [
        load(*pair)
        for pair in ((tok_in, tok), (wk_in, wk), (wv_in, wv), (wq_in, wq), (wo_in, wo))
    ]
    greet(xs + ys + [zp, mate, far])

    loads[0].wait()
    for m in range(2):

        def slab(i, carry):
            r = pl.ds(pl.multiple_of(i * 16, 16), 16)
            v = tok[m, r].astype(F32)
            q = lax.rsqrt(jnp.mean(v * v, axis=-1, keepdims=True) + EPS)
            normed[m, r] = (v * q * norms_ref[0:1]).astype(BF)
            return carry

        lax.fori_loop(0, ROWS // 16, slab, 0)
    loads[1].wait()
    loads[2].wait()
    cosine, sine = cos_ref[...], sin_ref[...]
    for m, held in ((0, ga), (1, gb)):
        a, b = wk[...], wv[...]
        if m == 1:
            a, b = narrow(a), narrow(b)
        held[z, y, x, :ROWS] = turn(nn(normed[m], a) * scale_in, cosine, sine).astype(BF)
        held[z, y, x, ROWS : 2 * ROWS] = (nn(normed[m], b) * scale_in).astype(BF)
        held[z, y, x, TAGROW:] = tags[m]

    levels = (z, 1 - z)

    def at_a(level, along_x, along_y, part=None):
        ref = ga.at[level, along_y, along_x]
        return ref if part is None else ref.at[part]

    def at_b(level, along_y, along_x, part=None):
        ref = gb.at[level, along_y, along_x]
        return ref if part is None else ref.at[part]

    first_half, last_half = pl.ds(0, CUT), pl.ds(CUT, TAGROW + 16 - CUT)
    sides = (
        (at_a, x, xi, xs, y, yi, ys),
        (at_b, y, yi, ys, x, xi, xs),
    )

    def line(side, level, second, pair=None):
        if side == 0:
            return ga.at[level, second] if pair is None else ga.at[level, second, pair]
        return gb.at[level, :, second] if pair is None else gb.at[level, pair, second]

    across = []
    for at, one, places, devices, two, _, _ in sides:
        own = at(z, one, two)
        across.append(post(own, own, zp))
    near = {}

    def send_near(side, k):
        at, one, places, devices, two, _, _ = sides[side]
        own = at(levels[k], one, two)
        near[side, k] = [post(own, own, devices[j]) for j in (0, 2)]

    relays = {}

    def relay_near(side, k):
        at, one, places, devices, two, _, _ = sides[side]
        sent = near[side, k]
        sent[0].wait_recv()
        piece = at(levels[k], places[2], two, first_half)
        relays[side, k] = [post(piece, piece, devices[0])]
        sent[1].wait_recv()
        piece = at(levels[k], places[0], two, last_half)
        relays[side, k].append(post(piece, piece, devices[2]))

    lines = {}

    def send_line(side, k):
        _, _, _, _, two, _, devices = sides[side]
        arrive(relays[side, k])
        own = line(side, levels[k], two)
        lines[side, k] = [post(own, own, devices[j]) for j in (0, 2)]

    passed = {}

    def relay_line(side, k):
        _, _, _, _, _, places, devices = sides[side]
        sent = lines[side, k]
        sent[0].wait_recv()
        piece = line(side, levels[k], places[2], pl.ds(0, 2))
        passed[side, k] = [post(piece, piece, devices[0])]
        sent[1].wait_recv()
        piece = line(side, levels[k], places[0], pl.ds(2, 2))
        passed[side, k].append(post(piece, piece, devices[2]))

    both = (0, 1)
    for side in both:
        send_near(side, 0)
    loads[3].wait()
    for m in range(2):
        a = wq[...] if m == 0 else narrow(wq[...])
        wide = nn(normed[m], a) * scale_in
        for h in range(2):
            turned = turn(wide[:, h * HD : (h + 1) * HD], cosine, sine)
            q_ref[m, h * ROWS : (h + 1) * ROWS] = turned.astype(BF)
        fill_turned(dn, normed[m], m)
    arrive(across)
    for side in both:
        send_near(side, 1)
    for k in both:
        for side in both:
            relay_near(side, k)

    acc[...] = jnp.zeros_like(acc)
    mass[...] = jnp.zeros_like(mass)
    where = query_places()
    lane = lax.broadcasted_iota(jnp.int32, (2 * ROWS, KEYS), 1)

    def attend(side, k, second):
        level = levels[k]
        if side == 0:
            held, begin, key_place = ga.at[level, second], level * 16 + second * 4, lane
            stride = 1
        else:
            held, begin, key_place = gb.at[level, :, second], level * 16 + second, lane % ROWS + lane // ROWS * (4 * ROWS)
            stride = 4

        @pl.when(begin <= block)
        def _():
            keys = held[:, :ROWS, :].reshape(KEYS, HD)
            values = held[:, ROWS : 2 * ROWS, :].reshape(KEYS, HD)
            tag = held[:, TAGROW : TAGROW + 16, :ROWS].astype(F32)
            tag_row = jnp.concatenate([tag[i, 0:1, :] for i in range(CHUNK)], axis=1)
            bent = jnp.tanh(nt(q_ref[side], keys) * (HD ** (-0.5) / CAP))
            ok = allowed(key_place + begin * ROWS, tag_row, tag_ref[side], where)
            e = jnp.where(ok, jnp.exp(CAP * bent), 0.0)
            mass[side] += jnp.sum(e, axis=-1, keepdims=True)
            acc[side] += nn(e.astype(BF), values)

    for k in both:
        for side in both:
            send_line(side, k)
    for k in both:
        for side in both:
            attend(side, k, sides[side][4])
    for k in both:
        for side in both:
            relay_line(side, k)
    for k in both:
        for side in both:
            attend(side, k, sides[side][5][0])
            attend(side, k, sides[side][5][2])
    for side in both:
        for k in both:
            arrive(passed[side, k])
            attend(side, k, sides[side][5][1])
    load(ga, all_a)
    load(gb, all_b)

    band_y = pl.ds(pl.multiple_of(y * 256, 256), 256)
    sums = Summed(post, part, t1, th, t2, c, mate, far)
    carried = []
    loads[4].wait()

    def project(m):
        out = acc[m] / mass[m]
        att[m] = out
        lse_ref[m] = jnp.log(mass[m])
        low = out.astype(BF)
        flat[m] = jnp.concatenate([low[:ROWS], low[ROWS:]], axis=1)
        a = wo[...] if m == 0 else narrow(wo[...])
        part[m] = (nn(flat[m], a) * scale_mid).astype(BF)

    def spread(m):
        land = ca_land.at[y, pl.ds(m * ROWS, ROWS)]
        load(flat.at[m], land)
        return [post(flat.at[m], land, ys[j]) for j in range(3)]

    def norms(m):
        def slab(i, carry):
            r = pl.ds(pl.multiple_of(i * 16, 16), 16)
            v = branch[m, r].astype(F32)
            q = lax.rsqrt(jnp.mean(v * v, axis=-1, keepdims=True) + EPS)
            mid = tok[m, r].astype(F32) + v * q * norms_ref[1:2]
            middle[m, r] = mid
            q = lax.rsqrt(jnp.mean(mid * mid, axis=-1, keepdims=True) + EPS)
            ffn_in[m, r] = (mid * q * norms_ref[2:3]).astype(BF)
            return carry

        lax.fori_loop(0, ROWS // 16, slab, 0)
        fill_turned(ft, ffn_in[m], m)

    project(0)
    one = sums.start(0)
    carried += [post(dn.at[:, yi[j]], dn_land.at[:, :, band_y], ys[j]) for j in range(3)]
    load(dn.at[:, y], dn_land.at[:, :, band_y])
    two0 = sums.across(0, one)
    project(1)
    one = sums.start(1)
    two1 = sums.across(1, one)
    carried += spread(0)
    carried += spread(1)
    three = sums.back(0, two0, branch, 0)
    arrive(three)
    norms(0)
    three = sums.back(1, two1, branch, 1)
    arrive(three)
    norms(1)
    arrive(carried)
    for copy in local[5:]:
        copy.wait()
    for copy in copies:
        copy.wait_send()


def front(norms, cosine, sine, tags, tag, tok, wq, wk, wv, wo, scale_in, scale_mid):
    def kernel(*refs):
        front_kernel(*refs, scale_in, scale_mid)

    any_ = whole(pl.ANY)
    both = (2, ROWS, D)
    heads = (2, 2 * ROWS, HD)
    kv = (2, 4, 4, TAGROW + 16, HD)
    turned = (2, 4, 288, 2 * ROWS)
    sems = 34 + 2 * 3 * (HALF // STEP_ROWS) + 9
    return pl.pallas_call(
        kernel,
        out_shape=[
            jax.ShapeDtypeStruct(both, F32),
            jax.ShapeDtypeStruct(both, BF),
            jax.ShapeDtypeStruct(both, BF),
            jax.ShapeDtypeStruct(heads, BF),
            jax.ShapeDtypeStruct(heads, F32),
            jax.ShapeDtypeStruct((2, 2 * ROWS, 1), F32),
            jax.ShapeDtypeStruct(turned, BF),
            jax.ShapeDtypeStruct(kv, BF),
            jax.ShapeDtypeStruct(kv, BF),
            jax.ShapeDtypeStruct((2, 288, 1024), BF),
            jax.ShapeDtypeStruct((4, 2 * ROWS, 2 * HD), BF),
        ],
        in_specs=[whole()] * 5 + [any_] * 5,
        out_specs=[whole()] * 7 + [any_] * 4,
        scratch_shapes=[
            VMEM(both, BF),
            VMEM(wq.shape, BF),
            VMEM(wk.shape, BF),
            VMEM(wv.shape, BF),
            VMEM(wo.shape, BF),
            VMEM(both, BF),
            VMEM(turned, BF),
            VMEM((2, ROWS, 2 * HD), BF),
            VMEM(kv, BF),
            VMEM(kv, BF),
            VMEM(heads, F32),
            VMEM((2, 2 * ROWS, 1), F32),
            VMEM(both, BF),
            VMEM((2, HALF, D), BF),
            VMEM((2, HALF, D), BF),
            VMEM((2, HALF, D), BF),
            pltpu.SemaphoreType.DMA((10,)),
            pltpu.SemaphoreType.DMA((sems,)),
            pltpu.SemaphoreType.DMA((sems,)),
        ],
        compiler_params=params(1, 60),
    )(norms, cosine, sine, tags, tag, tok, wq, wk, wv, wo)


LTILE = 256
FTILE = 768
ROOT = (2.0 / 3.141592653589793) ** 0.5
CUBE = 0.044715


def narrow(codes):
    level = codes * BF(1.0 / 16.0) + BF(1.0 / 32.0)
    level = (level + BF(192.0)) - BF(192.0)
    return jnp.minimum(level, BF(7.0)) * BF(16.0)


def ffn_kernel(
    x_ref, gain_ref, wg_in, wu_in, wd_in, middle_in, up_in, dg_own, du_own,
    out_ref, dup_ref, total_ref, gains, ch, dd_land, dg_land, du_land, cg, cu, pd_out,
    wg, wu, wd, middle, upstream, gate_s, up_s, hid, dgate_ref, acc, part, low, dd,
    t1, th, t2, down_sum,
    wsem, lsem, ssem, rsem,
    scale_in, scale_out,
):
    x, y, z, zh, c = place_of()
    xi = [(x + j) % 4 for j in (1, 2, 3)]
    yi = [(y + j) % 4 for j in (1, 2, 3)]
    xs = [device_at(i, y, z, zh, c) for i in xi]
    ys = [device_at(x, i, z, zh, c) for i in yi]
    mate = device_at(x, y, z, zh, 1 - c)
    far = device_at(x, y, z, 1 - zh, c)
    tiles = wg.shape[1] // FTILE
    copies, local = [], []
    post = poster(ssem, rsem, copies)
    load = loader(lsem, local)

    def weight_copies(t):
        span = pl.ds(pl.multiple_of(t * LTILE, LTILE), LTILE)
        return (
            pltpu.make_async_copy(wg_in.at[:, span], wg.at[:, span], wsem.at[0, t]),
            pltpu.make_async_copy(wu_in.at[:, span], wu.at[:, span], wsem.at[1, t]),
            pltpu.make_async_copy(wd_in.at[span], wd.at[span], wsem.at[2, t]),
        )

    def start_weights(t, carry):
        for copy in weight_copies(t):
            copy.start()
        return carry

    lax.fori_loop(0, wg.shape[1] // LTILE, start_weights, 0)
    loads = [load(middle_in, middle), load(up_in, upstream)]
    greet(xs + ys + [mate, far])
    band_x = pl.ds(pl.multiple_of(x * 256, 256), 256)
    band_y = pl.ds(pl.multiple_of(y * 256, 256), 256)
    carried = []
    mine = pl.ds(pl.multiple_of(c * ROWS, ROWS), ROWS)
    mine_y = pl.ds(pl.multiple_of(y * 256 + c * ROWS, ROWS), ROWS)
    du_sent = [post(du_own.at[:, yi[j], :, mine], du_land.at[:, :, mine_y], ys[j]) for j in range(3)]
    mine_x = pl.ds(pl.multiple_of(x * 256 + c * ROWS, ROWS), ROWS)
    dg_sent = [post(dg_own.at[xi[j], :, :, mine], dg_land.at[:, :, mine_x], xs[j]) for j in range(3)]
    load(dg_own.at[x], dg_land.at[:, :, band_x])
    load(du_own.at[:, y], du_land.at[:, :, band_y])

    def forward(m, first, last, wait=False):
        def body(t, carry):
            span = pl.ds(pl.multiple_of(t * FTILE, FTILE), FTILE)
            if wait:
                for k in range(FTILE // LTILE):
                    for copy in weight_copies(t * (FTILE // LTILE) + k):
                        copy.wait()
            a, b, d = wg[:, span], wu[:, span], wd[span]
            if m == 1:
                a, b, d = narrow(a), narrow(b), narrow(d)
            gate = nn(x_ref[m], a) * scale_in
            up = nn(x_ref[m], b) * scale_in
            gate_s[m, :, span] = gate
            up_s[m, :, span] = up
            bent = jnp.tanh(ROOT * (gate + CUBE * gate * gate * gate))
            hidden = (0.5 * gate * (1.0 + bent) * up).astype(BF)
            hid[m, :, span] = hidden
            acc[...] += nn(hidden, d)
            return carry

        lax.fori_loop(first, last, body, 0)

    def backward(m):
        def body(t, carry):
            span = pl.ds(pl.multiple_of(t * FTILE, FTILE), FTILE)
            d = wd[span] if m == 0 else narrow(wd[span])
            grad = nt(low[m], d) * scale_out
            v, u = gate_s[m, :, span], up_s[m, :, span]
            bent = jnp.tanh(ROOT * (v + CUBE * v * v * v))
            half = 0.5 * (1.0 + bent)
            slope = half + 0.5 * v * (1.0 - bent * bent) * (ROOT * (1.0 + 3.0 * CUBE * v * v))
            dgate_ref[m, :, span] = (grad * u * slope).astype(BF)
            dup_ref[m, :, span] = (grad * (v * half)).astype(BF)
            return carry

        lax.fori_loop(0, tiles, body, 0)

    def through(m, first, last):
        def body(t, carry):
            span = pl.ds(pl.multiple_of(t * FTILE, FTILE), FTILE)
            a, b = wg[:, span], wu[:, span]
            if m == 1:
                a, b = narrow(a), narrow(b)
            acc[...] += nt(dgate_ref[m, :, span], a) + nt(dup_ref[m, :, span], b)
            return carry

        lax.fori_loop(first, last, body, 0)

    pieces = [pl.ds(k * STEP_ROWS, STEP_ROWS) for k in range(HALF // STEP_ROWS)]

    def at_rows(core, k):
        return pl.ds(pl.multiple_of(core * HALF + k * STEP_ROWS, STEP_ROWS), STEP_ROWS)

    def sum_start(i, m):
        return [post(part.at[i, at_rows(1 - c, k)], t1.at[i, r], mate) for k, r in enumerate(pieces)]

    def sum_across(i, one):
        sent = []
        for k, r in enumerate(pieces):
            one[k].wait_recv()
            th[i, r] = (part[i, at_rows(c, k)].astype(F32) + t1[i, r].astype(F32)).astype(BF)
            sent.append(post(th.at[i, r], t2.at[i, r], far))
        return sent

    def sum_back(i, two, dst, m):
        sent = []
        for k, r in enumerate(pieces):
            two[k].wait_recv()
            dst[m, at_rows(c, k)] = (th[i, r].astype(F32) + t2[i, r].astype(F32)).astype(BF)
            sent.append(post(dst.at[m, at_rows(c, k)], dst.at[m, at_rows(c, k)], mate))
        return sent

    def arrive(sent):
        for copy in sent:
            copy.wait_recv()

    def spread_hidden(m):
        land = ch.at[y, pl.ds(m * ROWS, ROWS)]
        load(hid.at[m], land)
        return [post(hid.at[m], land, ys[j]) for j in (0, 2)]

    def spread_gate(m):
        land = cg.at[x, pl.ds(m * ROWS, ROWS)]
        load(dgate_ref.at[m], land)
        return [post(dgate_ref.at[m], land, xs[j]) for j in (0, 2)]

    def relay_rows(m, sent, land, places, devices):
        for k, j in ((0, 0), (1, 2)):
            sent[k].wait_recv()
            half = land.at[places[2 - j], pl.ds(m * ROWS + k * HALF, HALF)]
            carried.append(post(half, half, devices[j]))

    def norm(m, sums):
        def slab(i, carry):
            r = pl.ds(pl.multiple_of(i * 16, 16), 16)
            v = down_sum[m, r].astype(F32)
            du = upstream[m, r].astype(F32)
            q = lax.rsqrt(jnp.mean(v * v, axis=-1, keepdims=True) + EPS)
            gain = gain_ref[3:4]
            out_ref[m, r] = (middle[m, r] + v * q * gain).astype(BF)
            lifted = du * gain
            back = q * lifted - v * (q * q * q * jnp.mean(lifted * v, axis=-1, keepdims=True))
            low[m, r] = back.astype(BF)
            return carry + jnp.sum(du * v * q, axis=0, keepdims=True)

        return lax.fori_loop(0, ROWS // 16, slab, sums)

    def swap_down(m):
        turned = low[m].T
        for zi in range(2):
            for k in range(4):
                at = (zi * 4 + k) * 288
                dd[m, zi, k] = turned[at : at + 288]
        band = pl.ds(pl.multiple_of(y * 256, 256) + m * ROWS, ROWS)
        load(dd.at[m, :, y], dd_land.at[:, :, band])

    acc[...] = jnp.zeros_like(acc)
    forward(0, 0, tiles, True)
    part[0] = (acc[...] * scale_out).astype(BF)
    one = sum_start(0, 0)
    hidden0 = spread_hidden(0)
    acc[...] = jnp.zeros_like(acc)
    forward(1, 0, 1)
    two = sum_across(0, one)
    forward(1, 1, tiles)
    part[1] = (acc[...] * scale_out).astype(BF)
    one = sum_start(1, 1)
    hidden1 = spread_hidden(1)
    three = sum_back(0, two, down_sum, 0)
    two = sum_across(1, one)
    arrive(three)
    for copy in loads:
        copy.wait()
    sums = norm(0, jnp.zeros((1, D), F32))
    relay_rows(0, hidden0, ch, yi, ys)
    carried += share(post, du_sent, du_land, yi, ROWS, c, mate)
    carried += share(post, dg_sent, dg_land, xi, ROWS, c, mate)
    swap_down(0)
    acc[...] = jnp.zeros_like(acc)
    backward(0)
    gate0 = spread_gate(0)
    up_sent = [post(dup_ref.at[0], cu.at[y], ys[j]) for j in (0, 2)]
    load(dup_ref.at[0], cu.at[y])
    relay_rows(1, hidden1, ch, yi, ys)
    through(0, 0, tiles)
    part[2] = (acc[...] * scale_in).astype(BF)
    one = sum_start(2, 0)
    three = sum_back(1, two, down_sum, 1)
    two = sum_across(2, one)
    arrive(three)
    gains[...] = norm(1, sums)
    swap_down(1)
    dd_sent = [post(dd.at[c, :, yi[j]], dd_land.at[:, :, mine_y], ys[j]) for j in range(3)]
    acc[...] = jnp.zeros_like(acc)
    backward(1)
    gate1 = spread_gate(1)
    through(1, 0, 2)
    relay_rows(0, gate0, cg, xi, xs)
    carried += relay(post, up_sent, cu, yi, ys)
    carried += share(post, dd_sent, dd_land, yi, ROWS, c, mate)
    through(1, 2, tiles)
    part[3] = (acc[...] * scale_in).astype(BF)
    one = sum_start(3, 1)
    three = sum_back(2, two, total_ref, 0)
    two = sum_across(3, one)
    arrive(carried)
    for copy in local[2:]:
        copy.wait()
    done = len(local)
    width = 4 * 2 * ROWS
    parts = [load(ch.at[i], wg.at[pl.ds(i * 2 * ROWS, 2 * ROWS)]) for i in range(4)]
    parts += [load(dd_land.at[i], wd.at[pl.ds(i * 288, 288), pl.ds(0, width)]) for i in range(2)]
    for copy in parts:
        copy.wait()

    def down_product(t, carry):
        span = pl.ds(pl.multiple_of(t * FTILE, FTILE), FTILE)
        out = nn(wd[:PART, :width], wg[:width, span]).reshape(8, SHARE, FTILE)
        for k in range(8):
            wu[k * 80 : k * 80 + SHARE, span] = out[k].astype(BF)
        return carry

    lax.fori_loop(0, D // FTILE, down_product, 0)
    for k in range(8):
        load(wu.at[pl.ds(k * 80, SHARE)], pd_out.at[k // 4, k % 4])
    arrive(three)
    three = sum_back(3, two, total_ref, 1)
    arrive(three)
    arrive(gate1)
    for copy in local[done + 6 :]:
        copy.wait()
    for copy in copies:
        copy.wait_send()


def ffn(x, gain, wg, wu, wd, middle, up, dg, du, scale_in, scale_out):
    def kernel(*refs):
        ffn_kernel(*refs, scale_in, scale_out)

    any_ = whole(pl.ANY)
    both = (2, ROWS, D)
    loads = wg.shape[1] // LTILE
    sems = 6 + 4 * 3 * (HALF // STEP_ROWS) + 8 + 6 + 6 + 12
    return pl.pallas_call(
        kernel,
        out_shape=[
            jax.ShapeDtypeStruct(both, BF),
            jax.ShapeDtypeStruct(both, BF),
            jax.ShapeDtypeStruct(both, BF),
            jax.ShapeDtypeStruct((1, D), F32),
            jax.ShapeDtypeStruct((4, 2 * ROWS, D), BF),
            jax.ShapeDtypeStruct((2, 288, 1024), BF),
            jax.ShapeDtypeStruct((2, 288, 1024), BF),
            jax.ShapeDtypeStruct((2, 288, 1024), BF),
            jax.ShapeDtypeStruct((4, 2 * ROWS, D), BF),
            jax.ShapeDtypeStruct((4, ROWS, D), BF),
            jax.ShapeDtypeStruct((2, 4, SHARE, D), BF),
        ],
        in_specs=[whole()] * 2 + [any_] * 7,
        out_specs=[whole()] * 4 + [any_] * 7,
        scratch_shapes=[
            VMEM(wg.shape, BF),
            VMEM(wu.shape, BF),
            VMEM(wd.shape, BF),
            VMEM(both, F32),
            VMEM(both, BF),
            VMEM(both, F32),
            VMEM(both, F32),
            VMEM(both, BF),
            VMEM(both, BF),
            VMEM((ROWS, D), F32),
            VMEM((4, ROWS, D), BF),
            VMEM(both, BF),
            VMEM((2, 2, 4, 288, ROWS), BF),
            VMEM((4, HALF, D), BF),
            VMEM((4, HALF, D), BF),
            VMEM((4, HALF, D), BF),
            VMEM(both, BF),
            pltpu.SemaphoreType.DMA((3, loads)),
            pltpu.SemaphoreType.DMA((32,)),
            pltpu.SemaphoreType.DMA((sems,)),
            pltpu.SemaphoreType.DMA((sems,)),
        ],
        compiler_params=params(5, 63),
    )(x, gain, wg, wu, wd, middle, up, dg, du)


PART = 576
SHARE = 72


def norm_grad(v, gain, grad):
    q = lax.rsqrt(jnp.mean(v * v, axis=-1, keepdims=True) + EPS)
    lifted = grad * gain
    back = q * lifted - v * (q * q * q * jnp.mean(lifted * v, axis=-1, keepdims=True))
    return back, jnp.sum(grad * v * q, axis=0, keepdims=True)


CTILE = 768


def back_kernel(
    norms_ref, q_ref, lse_ref, tag_ref, att_ref, cos_ref, sin_ref, gain_ref,
    total_in, middle_in, branch_in, up_in, wo_in, k_in, v_in, pd_in, du_in, cu0_in, cu_own, dg_in, cg_in,
    wq_in, wk_in, wv_in, tok_in, dn_in, ca_in,
    on, igrad, og, ou, od, oq, mgrad_out, cu1, cg_far, db_land,
    dk, dv, dq, gsum, bt, pd, r1a, r1b, r2a, r2b, s2a, s2b, r3a, r3b, cq, part, t1, th, t2, total_ref, gb, rgb, pn,
    rd, ru, rg, rq, rn, zd, zu, zg, zq, zn, stage,
    lsem, csem, ssem, rsem,
    scale_mid, scale_in,
):
    x, y, z, zh, c = place_of()
    xi = [(x + j) % 4 for j in (1, 2, 3)]
    yi = [(y + j) % 4 for j in (1, 2, 3)]
    xs = [device_at(i, y, z, zh, c) for i in xi]
    ys = [device_at(x, i, z, zh, c) for i in yi]
    zp = device_at(x, y, 1 - z, zh, c)
    mate = device_at(x, y, z, zh, 1 - c)
    far = device_at(x, y, z, 1 - zh, c)
    copies, local = [], []
    post = poster(ssem, rsem, copies)
    load = loader(lsem, local)
    mine = pl.ds(pl.multiple_of(c * ROWS, ROWS), ROWS)
    mine_y = pl.ds(pl.multiple_of(y * 256 + c * ROWS, ROWS), ROWS)
    band_y = pl.ds(pl.multiple_of(y * 256, 256), 256)
    where = query_places()
    block = lax.axis_index("blk")
    lane = lax.broadcasted_iota(jnp.int32, (2 * ROWS, KEYS), 1)
    ring_a = Ring(post, lambda level, i: dk.at[level, :, i], r1a, x, xi, xs, add_blocks)
    ring_b = Ring(post, lambda level, i: dv.at[level, i], r1b, y, yi, ys, add_blocks)
    rings = (ring_a, ring_b)

    carried, up_sent, up_far = [], [], []

    ring_d = Ring(post, lambda level, i: pd.at[level, i], rd, x, xi, xs, add_columns)

    def first(k_ref, v_ref, wo, middle, branch, upstream, total, blow, g_ref):
        got_d = load(pd_in, pd)
        loads = [
            load(*pair)
            for pair in (
                (middle_in, middle), (branch_in, branch), (up_in, upstream), (total_in, total), (wo_in, wo),
                (k_in, k_ref), (v_in, v_ref),
            )
        ]
        greet(xs + ys + [zp, mate, far])
        got_d.wait()
        ring_d.begin_all()
        up_sent.extend(post(lambda: cu_own.at[1], lambda: cu1.at[y], ys[j], True) for j in (0, 2))
        own_up = load(cu_own.at[1], cu1.at[y])
        for k, j in ((0, 0), (1, 2)):
            src = functools.partial(lambda j, k: cg_in.at[xi[2 - j], pl.ds(ROWS + k * HALF, HALF)], j, k)
            dst = functools.partial(lambda k: cg_far.at[pl.ds(k * HALF, HALF)], k)
            carried.append(post(src, dst, xs[j], True))
        for copy in loads[:4]:
            copy.wait()

        sums = (jnp.zeros((1, D), F32), jnp.zeros((1, D), F32))
        for m in range(2):

            def slab(i, carry):
                r = pl.ds(pl.multiple_of(i * 16, 16), 16)
                back, more = norm_grad(middle[m, r], norms_ref[2:3], total[m, r].astype(F32))
                grad = upstream[m, r].astype(F32) + back
                middle[m, r] = grad
                back, most = norm_grad(branch[m, r].astype(F32), norms_ref[1:2], grad)
                blow[m, r] = back.astype(BF)
                return carry[0] + most, carry[1] + more

            sums = lax.fori_loop(0, ROWS // 16, slab, sums)
        gsum[1:2] = sums[0]
        gsum[2:3] = sums[1]
        gsum[3:4] = gain_ref[...]
        keep = load(middle, mgrad_out)
        loads[4].wait()
        for m in range(2):
            weight = wo[...] if m == 0 else narrow(wo[...])
            wide = (nt(blow[m], weight) * scale_mid).astype(BF)
            g_ref[m, :ROWS] = wide[:, :HD]
            g_ref[m, ROWS:] = wide[:, HD:]
        offsets = [jnp.sum(g_ref[m].astype(F32) * att_ref[m], axis=-1, keepdims=True) for m in range(2)]

        loads[5].wait()
        loads[6].wait()
        dq[...] = jnp.zeros_like(dq)

        def chunk(m, level, i):
            if m == 0:
                held, out, begin = k_ref.at[level, :, i], dk.at[level, :, i], level * 16 + i
                key_place = lane % ROWS + lane // ROWS * (4 * ROWS) + begin * ROWS
            else:
                held, out, begin = v_ref.at[level, i], dv.at[level, i], level * 16 + i * 4
                key_place = lane + begin * ROWS

            @pl.when(begin <= block)
            def _():
                q, g = q_ref[m], g_ref[m]
                keys = held[:, :ROWS, :].reshape(KEYS, HD)
                values = held[:, ROWS : 2 * ROWS, :].reshape(KEYS, HD)
                tags = held[:, TAGROW : TAGROW + 16, :ROWS].astype(F32)
                tag_row = jnp.concatenate([tags[k, 0:1, :] for k in range(CHUNK)], axis=1)
                bent = jnp.tanh(nt(q, keys) * (HD ** (-0.5) / CAP))
                ok = allowed(key_place, tag_row, tag_ref[m], where)
                p = jnp.where(ok, jnp.exp(CAP * bent - lse_ref[m]), 0.0)
                dp = nt(g, values)
                ds = (p * (dp - offsets[m]) * (1.0 - bent * bent) * HD ** (-0.5)).astype(BF)
                out[:, :ROWS, :] = tn(ds, q).astype(BF).reshape(CHUNK, ROWS, HD)
                out[:, ROWS:, :] = tn(p.astype(BF), g).astype(BF).reshape(CHUNK, ROWS, HD)
                dq[m] += nn(ds, keys)

            @pl.when(begin > block)
            def _():
                out[...] = jnp.zeros(out.shape, BF)

        for k in range(4):
            for m in range(2):
                chunk(m, *rings[m].order[k])
                rings[m].begin()
            if k == 1:
                up_far.extend(relay(post, up_sent, cu1, yi, ys))
                ring_d.onward()
        for m, places in ((0, xi), (1, yi)):
            chunk(m, 0, places[0])
            chunk(m, 1, places[2])
        for m in range(2):
            fill_turned(bt, blow[m], m)
        own = load(bt.at[:, y], db_land.at[:, :, band_y])
        for m, place in ((0, x), (1, y)):
            chunk(m, 0, place)
            chunk(m, 1, place)
        for copy in (own, keep, own_up):
            copy.wait()

    both = (2, ROWS, D)
    kv = (2, 4, 4, TAGROW + 16, HD)
    pl.run_scoped(
        first,
        VMEM(kv, BF), VMEM(kv, BF), VMEM(wo_in.shape, BF), VMEM(both, F32), VMEM(both, BF), VMEM(both, BF),
        VMEM(both, BF), VMEM(both, BF), VMEM((2, 2 * ROWS, HD), BF),
    )

    def second(pu, pg, pq, cbuf, left):
        begun = len(copies)
        used = [0]

        def fetch(sources, slot):
            out = []
            for src, dst in sources:
                copy = pltpu.make_async_copy(src, cbuf.at[(slot,) + dst], csem.at[used[0]])
                copy.start()
                used[0] += 1
                out.append(copy)
            return out

        rows_0, rows_1 = pl.ds(0, ROWS), pl.ds(ROWS, ROWS)
        everything = slice(None)

        def sources_u(cols):
            return [
                (cu0_in.at[:, :, cols], (everything, rows_0)),
                (cu1.at[:, :, cols], (everything, rows_1)),
            ]

        def sources_g(cols):
            out = [(cg_in.at[i, :, cols], (i,)) for i in (x, xi[0], xi[2])]
            out.append((cg_in.at[xi[1], rows_0, cols], (xi[1], rows_0)))
            out.append((cg_far.at[:, cols], (xi[1], rows_1)))
            return out

        tiles = [pl.ds(t * CTILE, CTILE) for t in range(D // CTILE)]
        flight = {}

        def ahead(name, sources, t, slot):
            flight[name, t] = (fetch(sources(tiles[t]), slot), slot)

        def product(name, t, weights, out):
            pending, slot = flight.pop((name, t))
            for copy in pending:
                copy.wait()
            done = nn(weights[...].reshape(PART, 1024), cbuf[slot].reshape(1024, CTILE))
            out[:, :, :, tiles[t]] = done.reshape(2, 4, SHARE, CTILE).astype(BF)

        def column_ring(p, land, along):
            held = lambda level, i: p.at[level, i]
            if along == "x":
                return Ring(post, held, land, x, xi, xs, add_columns).begin_all()
            return Ring(post, held, land, y, yi, ys, add_columns).begin_all()

        def across(ring, p, land, own):
            ring.close()
            return post(p.at[1 - z, own], land, zp)

        out_copies = {}

        def finish(copy, p, land, own, slot, width, dst):
            copy.wait_recv()
            if slot in out_copies:
                out_copies[slot].wait()
            stage[slot, :, :width] = p[z, own].astype(F32) + land[...].astype(F32)
            out_copies[slot] = load(stage.at[slot, :, pl.ds(0, width)], dst)

        left_g = load(dg_in, left.at[0])
        left_u = load(du_in, left.at[1])
        arrive(carried)
        ahead("g", sources_g, 0, 0)
        ahead("g", sources_g, 1, 1)
        ring_a.onward()
        ring_b.onward()
        left_g.wait()
        product("g", 0, left.at[0], pg)
        ahead("g", sources_g, 2, 0)
        product("g", 1, left.at[0], pg)
        product("g", 2, left.at[0], pg)
        ring_a.close()
        two_a = [post(dk.at[:, yi[j], x], r2a.at[j], ys[j]) for j in range(3)]
        ring_b.close()
        two_b = [post(dv.at[:, y, xi[j]], r2b.at[j], xs[j]) for j in range(3)]
        db_sent = [post(bt.at[:, yi[j], :, mine], db_land.at[:, :, mine_y], ys[j]) for j in range(3)]
        three_d = across(ring_d, pd, zd, x)
        arrive(up_far)
        ahead("u", sources_u, 0, 0)
        ahead("u", sources_u, 1, 1)
        left_u.wait()
        product("u", 0, left.at[1], pu)
        ahead("u", sources_u, 2, 0)
        product("u", 1, left.at[1], pu)
        product("u", 2, left.at[1], pu)
        left_n = load(dn_in, left.at[1])
        got_c = fetch([(ca_in, (everything, everything, pl.ds(0, 2 * HD)))], 1)

        def sum_two(arrivals, own, land, half):
            arrive(arrivals)
            for zi in range(2):
                out = own(zi).astype(F32)
                for j in range(3):
                    out = out + land[j, zi].astype(F32)
                half[zi] = out.astype(BF)

        def project(wq, wk, wv):
            begun = len(copies)
            weights = [load(*pair) for pair in ((wq_in, wq), (wk_in, wk), (wv_in, wv))]
            sum_two(two_a, lambda zi: dk[zi, y, x], r2a, s2a)
            three_a = post(s2a.at[1 - z], r3a, zp)
            sum_two(two_b, lambda zi: dv[zi, y, x], r2b, s2b)
            three_b = post(s2b.at[1 - z], r3b, zp)
            ring_u = column_ring(pu, ru, "x")
            carried.extend(share(post, db_sent, db_land, yi, ROWS, c, mate))
            cosine, sine = cos_ref[...], -sin_ref[...]
            for m in range(2):
                r = slice(m * ROWS, (m + 1) * ROWS)
                for h in range(2):
                    turned = turn(dq[m, h * ROWS : (h + 1) * ROWS], cosine, sine)
                    cq[y, r, h * HD : (h + 1) * HD] = turned.astype(BF)
            for m, (copy, half, land) in enumerate(((three_a, s2a, r3a), (three_b, s2b, r3b))):
                r = slice(m * ROWS, (m + 1) * ROWS)
                copy.wait_recv()
                pair = half[z].astype(F32) + land[...].astype(F32)
                cq[y, r, 2 * HD : 3 * HD] = turn(pair[:ROWS], cosine, sine).astype(BF)
                cq[y, r, 3 * HD :] = pair[ROWS:].astype(BF)
            own = lambda: cq.at[y]
            cq_sent = [post(own, own, ys[j], True) for j in (0, 2)]
            for copy in weights:
                copy.wait()
            sums = Summed(post, part, t1, th, t2, c, mate, far)
            ones = []
            for m in range(2):
                r = slice(m * ROWS, (m + 1) * ROWS)
                a, b, v = wq[...], wk[...], wv[...]
                if m == 1:
                    a, b, v = narrow(a), narrow(b), narrow(v)
                out = nt(cq[y, r, : 2 * HD], a) + nt(cq[y, r, 2 * HD : 3 * HD], b) + nt(cq[y, r, 3 * HD :], v)
                part[m] = (out * scale_in).astype(BF)
                ones.append(sums.start(m))
            twos = [sums.across(m, ones[m]) for m in range(2)]
            settle(copies[begun:])
            return ring_u, cq_sent, sums, twos

        between = len(copies)
        state = []
        pl.run_scoped(
            lambda *refs: state.append(project(*refs)),
            VMEM(wq_in.shape, BF), VMEM(wk_in.shape, BF), VMEM(wv_in.shape, BF),
        )
        ring_u, cq_sent, sums, twos = state[0]
        arrive(carried[2:])
        left_b = load(db_land, left.at[0])
        cq_far = relay(post, cq_sent, cq, yi, ys)
        ring_g = column_ring(pg, rg, "y")
        ring_u.onward()
        left_b.wait()
        for copy in got_c:
            copy.wait()
        out = nn(left[0].reshape(PART, 1024), cbuf[1, :, :, : 2 * HD].reshape(1024, 512))
        pq[:, :, :, 1024:] = out.reshape(2, 4, SHARE, 512).astype(BF)
        settle(copies[begun:between])
        left_n.wait()
        arrive(cq_far)
        for t in range(2):
            cols = pl.ds(t * 512, 512)
            out = nn(left[1].reshape(PART, 1024), cq[:, :, cols].reshape(1024, 512))
            pq[:, :, :, cols] = out.reshape(2, 4, SHARE, 512).astype(BF)
        ring_q = column_ring(pq, rq, "x")

        def last(tok, mgrad, gpad):
            begun = len(copies)
            got = [load(tok_in, tok), load(mgrad_out, mgrad)]
            threes = [sums.back(m, twos[m], total_ref, m) for m in range(2)]
            for copy in got:
                copy.wait()
            gain = jnp.zeros((1, D), F32)
            for m in range(2):
                arrive(threes[m])

                def slab(i, carry):
                    r = pl.ds(pl.multiple_of(i * 16, 16), 16)
                    back, more = norm_grad(tok[m, r].astype(F32), norms_ref[0:1], total_ref[m, r].astype(F32))
                    part[m, r] = (mgrad[m, r] + back).astype(BF)
                    return carry + more

                gain = lax.fori_loop(0, ROWS // 16, slab, gain)
            out_grad = load(part, igrad)
            gpad[...] = jnp.zeros_like(gpad)
            gpad[0:1] = gain
            gpad[1:4] = gsum[1:4]
            turned = gpad[...].T.astype(BF)
            for zi in range(2):
                for k in range(4):
                    at = (zi * 4 + k) * 288
                    gb[zi, k] = turned[at : at + 288]
            gains_far = [post(gb.at[:, yi[j]], rgb.at[j], ys[j]) for j in range(3)]
            finish(three_d, pd, zd, x, 0, D, od)
            three_u = across(ring_u, pu, zu, x)
            out = gb[:, y].astype(F32)
            for j in range(3):
                gains_far[j].wait_recv()
                out = out + rgb[j].astype(F32)
            pn[...] = out.reshape(2, 4, SHARE, 128).astype(BF)
            ring_n = column_ring(pn, rn, "x")
            ring_g.onward()
            ring_q.onward()
            finish(three_u, pu, zu, x, 1, D, ou)
            ring_n.onward()
            three_g = across(ring_g, pg, zg, y)
            three_q = across(ring_q, pq, zq, x)
            three_n = across(ring_n, pn, zn, x)
            finish(three_g, pg, zg, y, 0, D, og)
            finish(three_q, pq, zq, x, 1, 1536, oq)
            three_n.wait_recv()
            on[...] = pn[z, x].astype(F32) + zn[...].astype(F32)
            out_grad.wait()
            for copy in out_copies.values():
                copy.wait()
            settle(copies[begun:])

        pl.run_scoped(last, VMEM(both, BF), VMEM(both, F32), VMEM((128, D), F32))
        settle(copies, True)

    wide = (2, 4, SHARE, D)
    pl.run_scoped(
        second,
        VMEM(wide, BF), VMEM(wide, BF), VMEM((2, 4, SHARE, 1536), BF),
        VMEM((2, 4, 2 * ROWS, CTILE), BF), VMEM((2, 2, 288, 1024), BF),
    )


def back(inputs, scale_mid, scale_in):
    def kernel(*refs):
        back_kernel(*refs, scale_mid, scale_in)

    any_ = whole(pl.ANY)
    tile = (2 * ROWS, HD)
    both = (2, ROWS, D)
    sems = 4 + 6 + 12 + 6 + 2 + 6 + 4 * 7 + 7 + 4 + 2 * 3 * (HALF // STEP_ROWS) + 3
    return pl.pallas_call(
        kernel,
        out_shape=[
            jax.ShapeDtypeStruct((SHARE, 128), F32),
            jax.ShapeDtypeStruct(both, BF),
            jax.ShapeDtypeStruct((SHARE, D), F32),
            jax.ShapeDtypeStruct((SHARE, D), F32),
            jax.ShapeDtypeStruct((SHARE, D), F32),
            jax.ShapeDtypeStruct((SHARE, 1536), F32),
            jax.ShapeDtypeStruct(both, F32),
            jax.ShapeDtypeStruct((4, ROWS, D), BF),
            jax.ShapeDtypeStruct((ROWS, D), BF),
            jax.ShapeDtypeStruct((2, 288, 1024), BF),
        ],
        in_specs=[whole()] * 8 + [any_] * 19,
        out_specs=[whole()] + [any_] * 9,
        scratch_shapes=[
            VMEM((2, 4, 4) + tile, BF),
            VMEM((2, 4, 4) + tile, BF),
            VMEM((2,) + tile, F32),
            VMEM((8, D), F32),
            VMEM((2, 4, 288, 2 * ROWS), BF),
            VMEM((2, 4, SHARE, D), BF),
            VMEM((6, 4) + tile, BF),
            VMEM((6, 4) + tile, BF),
            VMEM((3, 2) + tile, BF),
            VMEM((3, 2) + tile, BF),
            VMEM((2,) + tile, BF),
            VMEM((2,) + tile, BF),
            VMEM(tile, BF),
            VMEM(tile, BF),
            VMEM((4, 2 * ROWS, 1024), BF),
            VMEM(both, BF),
            VMEM((2, HALF, D), BF),
            VMEM((2, HALF, D), BF),
            VMEM((2, HALF, D), BF),
            VMEM(both, BF),
            VMEM((2, 4, 288, 128), BF),
            VMEM((3, 2, 288, 128), BF),
            VMEM((2, 4, SHARE, 128), BF),
        ]
        + [VMEM((6, SHARE, w), BF) for w in (D, D, D, 1536, 128)]
        + [VMEM((SHARE, w), BF) for w in (D, D, D, 1536, 128)]
        + [
            VMEM((2, SHARE, D), F32),
            pltpu.SemaphoreType.DMA((32,)),
            pltpu.SemaphoreType.DMA((32,)),
            pltpu.SemaphoreType.DMA((sems,)),
            pltpu.SemaphoreType.DMA((sems,)),
        ],
        compiler_params=params(2, 63),
    )(*inputs)


def shards(
    inputs,
    out_grad,
    segment_ids,
    keep_mask,
    query_codes,
    key_codes,
    value_codes,
    output_codes,
    gate_codes,
    up_codes,
    down_codes,
    norm_attn_in,
    norm_attn_out,
    norm_ffn_in,
    norm_ffn_out,
):
    rows = inputs.shape[1]
    place = lax.axis_index("blk") * rows + jnp.arange(rows, dtype=jnp.int32)
    freqs = 10000.0 ** (-jnp.arange(HD // 2, dtype=F32) * 2.0 / HD)
    angles = place.astype(F32)[:, None] * freqs[None, :]
    cosine = jnp.cos(angles)
    sine = jnp.sin(angles)
    in_scale = LEVEL_SCALE * D ** (-0.5)
    mid_scale = LEVEL_SCALE * (HEADS * HD) ** (-0.5)
    ff_scale = LEVEL_SCALE * FF ** (-0.5)

    norms = jnp.stack([norm_attn_in, norm_attn_out, norm_ffn_in, norm_ffn_out])
    key_tag = jnp.where(keep_mask == 1, segment_ids, -1).astype(BF)
    key_tag = jnp.concatenate([key_tag, jnp.zeros_like(key_tag)], axis=1)
    key_tag = jnp.broadcast_to(key_tag[:, None, :], (2, 16, 2 * rows))
    tag = segment_ids.astype(F32)
    tag = jnp.concatenate([tag, tag], axis=1)[:, :, None]
    (
        middle, branch, ffn_in, queries, attended, lse, ffn_turned, blocks_a, blocks_b, d_normed, all_attended,
    ) = front(
        norms, cosine, sine, key_tag, tag,
        inputs, query_codes, key_codes, value_codes, output_codes, in_scale, mid_scale,
    )
    out_rows, up_low, ffn_in_grad, gain_ffn_out, _, _, d_gate, d_up, cg, cu0, p_down = ffn(
        ffn_in, norms, gate_codes, up_codes, down_codes, middle, out_grad,
        ffn_turned.reshape(8, 4, SHARE, 2 * rows).transpose(1, 0, 2, 3).reshape(4, 2, 288, 2 * rows),
        ffn_turned, in_scale, ff_scale,
    )
    g_gains, input_grad, g_gate, g_up, g_down, g_rest = back(
        (
            norms, queries, lse, tag, attended, cosine, sine, gain_ffn_out,
            ffn_in_grad, middle, branch, out_grad, output_codes, blocks_a, blocks_b,
            p_down, d_up, cu0, up_low, d_gate, cg,
            query_codes, key_codes, value_codes, inputs, d_normed, all_attended,
        ),
        mid_scale,
        in_scale,
    )[:6]
    return (
        out_rows,
        input_grad,
        g_rest[:, :512] * in_scale,
        g_rest[:, 512:768] * in_scale,
        g_rest[:, 768:1024] * in_scale,
        g_rest[:, 1024:1536].T * mid_scale,
        g_gate * in_scale,
        g_up * in_scale,
        g_down.T * ff_scale,
        g_gains[:, 0],
        g_gains[:, 1],
        g_gains[:, 2],
        g_gains[:, 3],
    )


def solution(mesh):
    placed = (
        P(None, "blk", None),
        P(None, "blk", None),
        P(None, "blk"),
        P(None, "blk"),
        P(None, "tensor"),
        P(None, "tensor"),
        P(None, "tensor"),
        P("tensor", None),
        P(None, "tensor"),
        P(None, "tensor"),
        P("tensor", None),
        P(),
        P(),
        P(),
        P(),
    )
    return jax.shard_map(
        shards,
        mesh=mesh,
        in_specs=placed,
        out_specs=(
            P(None, "blk", None),
            P(None, "blk", None),
            P("blk", "tensor"),
            P("blk", "tensor"),
            P("blk", "tensor"),
            P("tensor", "blk"),
            P("blk", "tensor"),
            P("blk", "tensor"),
            P("tensor", "blk"),
            P("blk"),
            P("blk"),
            P("blk"),
            P("blk"),
        ),
        check_vma=False,
    )
```

```python
import functools

import jax
import jax.numpy as jnp
from jax import lax
from jax.experimental import pallas as pl
from jax.experimental.pallas import tpu as pltpu
from jax.sharding import PartitionSpec as P

D = 2304
HEADS = 8
HD = 256
FF = 9216

CAP = 50.0
EPS = 1e-06
LEVEL_SCALE = 1.0 / 74.0
WIDTHS = (8, 4, 2)

MESH = pl.DeviceIdType.MESH
VMEM = pltpu.VMEM
BF = jnp.bfloat16
F32 = jnp.float32
SEQ = 4096
ROWS = 128
TAGROW = 256
MASKED = -2.0


def place_of():
    b = lax.axis_index("blk")
    t = lax.axis_index("tensor")
    return b % 4, (b // 4) % 4, b // 16, t // 2, t % 2


def device_at(x, y, z, zh, c):
    return ((z * 4 + y) * 4 + x, zh * 2 + c)


def greet(peers):
    barrier = pltpu.get_barrier_semaphore()
    for peer in peers:
        pl.semaphore_signal(barrier, inc=1, device_id=peer, device_id_type=MESH)
    pl.semaphore_wait(barrier, len(peers))


def send(src, dst, ssem, rsem, peer):
    copy = pltpu.make_async_remote_copy(
        src_ref=src, dst_ref=dst, send_sem=ssem, recv_sem=rsem, device_id=peer, device_id_type=MESH
    )
    copy.start()
    return copy


def params(collective_id=None, limit=60):
    if collective_id is None:
        return pltpu.CompilerParams(vmem_limit_bytes=limit << 20)
    return pltpu.CompilerParams(
        vmem_limit_bytes=limit << 20, collective_id=collective_id, has_side_effects=True
    )


def whole(space=VMEM):
    return pl.BlockSpec(memory_space=space)


CHUNK = 4
KEYS = CHUNK * ROWS


def nt(left, right):
    return lax.dot_general(left, right, (((1,), (1,)), ((), ())), preferred_element_type=F32)


def tn(left, right):
    return lax.dot_general(left, right, (((0,), (0,)), ((), ())), preferred_element_type=F32)


def nn(left, right):
    return jnp.dot(left, right, preferred_element_type=F32)


def allowed(key_place, tag_row, query_tag, query_place):
    ok = (key_place <= query_place) & (tag_row == query_tag)
    return ok | (key_place == query_place)


def query_places():
    row = lax.broadcasted_iota(jnp.int32, (2 * ROWS, 1), 0)
    return lax.axis_index("blk") * ROWS + row % ROWS


class Later:
    def __init__(self, src, dst, ssem, rsem, k, peer):
        self.src, self.dst, self.ssem, self.rsem, self.k, self.peer = src, dst, ssem, rsem, k, peer

    def describe(self):
        return pltpu.make_async_remote_copy(
            src_ref=self.src(),
            dst_ref=self.dst(),
            send_sem=self.ssem.at[self.k],
            recv_sem=self.rsem.at[self.k],
            device_id=self.peer,
            device_id_type=MESH,
        )

    def wait_recv(self):
        self.describe().wait_recv()

    def wait_send(self):
        self.describe().wait_send()


def poster(ssem, rsem, copies):
    def post(src, dst, peer, later=False):
        k = len(copies)
        if later:
            copies.append(Later(src, dst, ssem, rsem, k, peer))
            copies[k].describe().start()
        else:
            copies.append(send(src, dst, ssem.at[k], rsem.at[k], peer))
        return copies[k]

    return post


def settle(copies, later=False):
    for copy in copies:
        if isinstance(copy, Later) == later:
            copy.wait_send()


def loader(sem, copies):
    def load(src, dst):
        copy = pltpu.make_async_copy(src, dst, sem.at[len(copies)])
        copy.start()
        copies.append(copy)
        return copy

    return load


def arrive(copies):
    for copy in copies:
        copy.wait_recv()


def turn(values, cosine, sine):
    half = HD // 2
    first, second = values[:, :half], values[:, half:]
    return jnp.concatenate([first * cosine - second * sine, second * cosine + first * sine], axis=1)


def fill_turned(dst, value, m):
    turned = value.T
    for zi in range(2):
        for k in range(4):
            at = (zi * 4 + k) * 288
            dst[zi, k, :, m * ROWS : (m + 1) * ROWS] = turned[at : at + 288]


HALF = ROWS // 2
STEP_ROWS = 32


class Summed:
    def __init__(self, post, part, t1, th, t2, c, mate, far):
        self.post, self.part, self.t1, self.th, self.t2 = post, part, t1, th, t2
        self.c, self.mate, self.far = c, mate, far
        self.pieces = [pl.ds(k * STEP_ROWS, STEP_ROWS) for k in range(HALF // STEP_ROWS)]

    def rows(self, core, k):
        return pl.ds(pl.multiple_of(core * HALF + k * STEP_ROWS, STEP_ROWS), STEP_ROWS)

    @staticmethod
    def piece(ref, i, r):
        return ref.at[i, r]

    def start(self, i):
        other = 1 - self.c
        return [
            self.post(self.part.at[i, self.rows(other, k)], self.t1.at[i, r], self.mate)
            for k, r in enumerate(self.pieces)
        ]

    def across(self, i, one):
        sent = []
        for k, r in enumerate(self.pieces):
            one[k].wait_recv()
            own = self.part[i, self.rows(self.c, k)].astype(F32)
            self.th[i, r] = (own + self.t1[i, r].astype(F32)).astype(BF)
            src, dst = functools.partial(self.piece, self.th, i, r), functools.partial(self.piece, self.t2, i, r)
            sent.append(self.post(src, dst, self.far, True))
        return sent

    def back(self, i, two, dst, m):
        sent = []
        for k, r in enumerate(self.pieces):
            two[k].wait_recv()
            rows = self.rows(self.c, k)
            dst[m, rows] = (self.th[i, r].astype(F32) + self.t2[i, r].astype(F32)).astype(BF)
            sent.append(self.post(dst.at[m, rows], dst.at[m, rows], self.mate))
        return sent


def relay(post, sent, land, places, devices):
    out = []
    size = land.shape[1] // 2
    for k, j in ((0, 0), (1, 2)):
        sent[k].wait_recv()
        half = functools.partial(lambda place, k: land.at[place, pl.ds(k * size, size)], places[2 - j], k)
        out.append(post(half, half, devices[j], True))
    return out


def share(post, sent, land, places, width, c, mate):
    def band(place):
        begin = pl.multiple_of(place * (2 * width), 2 * width) + c * width
        return land.at[:, :, pl.ds(pl.multiple_of(begin, width), width)]

    out = []
    for j, copy in enumerate(sent):
        copy.wait_recv()
        own = functools.partial(band, places[2 - j])
        out.append(post(own, own, mate, True))
    return out


class Ring:
    def __init__(self, post, held, land, mine, places, devices, add):
        self.post, self.land, self.mine, self.places, self.devices = post, land, mine, places, devices
        self.held, self.add = held, add
        near, across, far = places
        self.order = ((0, across), (1, across), (1, near), (0, far))
        self.sent = []

    def begin(self):
        k = len(self.sent)
        src = functools.partial(self.held, *self.order[k])
        dst = functools.partial(self.slot, k)
        self.sent.append(self.post(src, dst, self.devices[0 if k % 2 == 0 else 2], True))

    def slot(self, k):
        return self.land.at[k]

    def begin_all(self):
        for _ in self.order:
            self.begin()
        return self

    def onward(self):
        self.passed = []
        for level, j in ((0, 0), (1, 2)):
            self.sent[level].wait_recv()
            ref = self.held(level, self.places[j])
            self.add(ref, ref, (self.land.at[level],))
            src = functools.partial(self.held, level, self.places[j])
            dst = functools.partial(self.slot, 4 + level)
            self.passed.append(self.post(src, dst, self.devices[j], True))

    def close(self):
        for level in range(2):
            self.sent[3 - level].wait_recv()
            self.passed[level].wait_recv()
            own = self.held(level, self.mine)
            self.add(own, own, (self.land.at[3 - level], self.land.at[4 + level]))


def add_blocks(dst, own, others):
    def body(k, carry):
        out = own[k].astype(F32)
        for other in others:
            out = out + other[k].astype(F32)
        dst[k] = out.astype(BF)
        return carry

    lax.fori_loop(0, own.shape[0], body, 0)


def add_columns(dst, own, others):
    tile = 256 if own.shape[-1] % 256 == 0 else 128

    def body(t, carry):
        cols = pl.ds(pl.multiple_of(t * tile, tile), tile)
        out = own[:, cols].astype(F32)
        for other in others:
            out = out + other[:, cols].astype(F32)
        dst[:, cols] = out.astype(BF)
        return carry

    lax.fori_loop(0, own.shape[-1] // tile, body, 0)


CUT = 144


def front_kernel(
    norms_ref, cos_ref, sin_ref, tags, tag_ref,
    tok_in, wq_in, wk_in, wv_in, wo_in,
    middle, branch, ffn_in, q_ref, att, lse_ref, ft, all_a, all_b, dn_land, ca_land,
    tok, wq, wk, wv, wo, normed, dn, flat, ga, gb, acc, mass, part, t1, th, t2,
    lsem, ssem, rsem,
    scale_in, scale_mid,
):
    x, y, z, zh, c = place_of()
    block = lax.axis_index("blk")
    xi = [(x + j) % 4 for j in (1, 2, 3)]
    yi = [(y + j) % 4 for j in (1, 2, 3)]
    xs = [device_at(i, y, z, zh, c) for i in xi]
    ys = [device_at(x, i, z, zh, c) for i in yi]
    zp = device_at(x, y, 1 - z, zh, c)
    mate = device_at(x, y, z, zh, 1 - c)
    far = device_at(x, y, z, 1 - zh, c)
    copies, local = [], []
    post = poster(ssem, rsem, copies)
    load = loader(lsem, local)
    loads = [
        load(*pair)
        for pair in ((tok_in, tok), (wk_in, wk), (wv_in, wv), (wq_in, wq), (wo_in, wo))
    ]
    greet(xs + ys + [zp, mate, far])

    loads[0].wait()
    for m in range(2):

        def slab(i, carry):
            r = pl.ds(pl.multiple_of(i * 16, 16), 16)
            v = tok[m, r].astype(F32)
            q = lax.rsqrt(jnp.mean(v * v, axis=-1, keepdims=True) + EPS)
            normed[m, r] = (v * q * norms_ref[0:1]).astype(BF)
            return carry

        lax.fori_loop(0, ROWS // 16, slab, 0)
    loads[1].wait()
    loads[2].wait()
    cosine, sine = cos_ref[...], sin_ref[...]
    for m, held in ((0, ga), (1, gb)):
        a, b = wk[...], wv[...]
        if m == 1:
            a, b = narrow(a), narrow(b)
        held[z, y, x, :ROWS] = turn(nn(normed[m], a) * scale_in, cosine, sine).astype(BF)
        held[z, y, x, ROWS : 2 * ROWS] = (nn(normed[m], b) * scale_in).astype(BF)
        held[z, y, x, TAGROW:] = tags[m]

    levels = (z, 1 - z)

    def at_a(level, along_x, along_y, part=None):
        ref = ga.at[level, along_y, along_x]
        return ref if part is None else ref.at[part]

    def at_b(level, along_y, along_x, part=None):
        ref = gb.at[level, along_y, along_x]
        return ref if part is None else ref.at[part]

    first_half, last_half = pl.ds(0, CUT), pl.ds(CUT, TAGROW + 16 - CUT)
    sides = (
        (at_a, x, xi, xs, y, yi, ys),
        (at_b, y, yi, ys, x, xi, xs),
    )

    def line(side, level, second, pair=None):
        if side == 0:
            return ga.at[level, second] if pair is None else ga.at[level, second, pair]
        return gb.at[level, :, second] if pair is None else gb.at[level, pair, second]

    across = []
    for at, one, places, devices, two, _, _ in sides:
        own = at(z, one, two)
        across.append(post(own, own, zp))
    near = {}

    def send_near(side, k):
        at, one, places, devices, two, _, _ = sides[side]
        own = at(levels[k], one, two)
        near[side, k] = [post(own, own, devices[j]) for j in (0, 2)]

    relays = {}

    def relay_near(side, k):
        at, one, places, devices, two, _, _ = sides[side]
        sent = near[side, k]
        sent[0].wait_recv()
        piece = at(levels[k], places[2], two, first_half)
        relays[side, k] = [post(piece, piece, devices[0])]
        sent[1].wait_recv()
        piece = at(levels[k], places[0], two, last_half)
        relays[side, k].append(post(piece, piece, devices[2]))

    lines = {}

    def send_line(side, k):
        _, _, _, _, two, _, devices = sides[side]
        arrive(relays[side, k])
        own = line(side, levels[k], two)
        lines[side, k] = [post(own, own, devices[j]) for j in (0, 2)]

    passed = {}

    def relay_line(side, k):
        _, _, _, _, _, places, devices = sides[side]
        sent = lines[side, k]
        sent[0].wait_recv()
        piece = line(side, levels[k], places[2], pl.ds(0, 2))
        passed[side, k] = [post(piece, piece, devices[0])]
        sent[1].wait_recv()
        piece = line(side, levels[k], places[0], pl.ds(2, 2))
        passed[side, k].append(post(piece, piece, devices[2]))

    both = (0, 1)
    for side in both:
        send_near(side, 0)
    loads[3].wait()
    for m in range(2):
        a = wq[...] if m == 0 else narrow(wq[...])
        wide = nn(normed[m], a) * scale_in
        for h in range(2):
            turned = turn(wide[:, h * HD : (h + 1) * HD], cosine, sine)
            q_ref[m, h * ROWS : (h + 1) * ROWS] = turned.astype(BF)
        fill_turned(dn, normed[m], m)
    arrive(across)
    for side in both:
        send_near(side, 1)
    for k in both:
        for side in both:
            relay_near(side, k)

    acc[...] = jnp.zeros_like(acc)
    mass[...] = jnp.zeros_like(mass)
    where = query_places()
    lane = lax.broadcasted_iota(jnp.int32, (2 * ROWS, KEYS), 1)

    def attend(side, k, second):
        level = levels[k]
        if side == 0:
            held, begin, key_place = ga.at[level, second], level * 16 + second * 4, lane
            stride = 1
        else:
            held, begin, key_place = gb.at[level, :, second], level * 16 + second, lane % ROWS + lane // ROWS * (4 * ROWS)
            stride = 4

        @pl.when(begin <= block)
        def _():
            keys = held[:, :ROWS, :].reshape(KEYS, HD)
            values = held[:, ROWS : 2 * ROWS, :].reshape(KEYS, HD)
            tag = held[:, TAGROW : TAGROW + 16, :ROWS].astype(F32)
            tag_row = jnp.concatenate([tag[i, 0:1, :] for i in range(CHUNK)], axis=1)
            bent = jnp.tanh(nt(q_ref[side], keys) * (HD ** (-0.5) / CAP))
            ok = allowed(key_place + begin * ROWS, tag_row, tag_ref[side], where)
            e = jnp.where(ok, jnp.exp(CAP * bent), 0.0)
            mass[side] += jnp.sum(e, axis=-1, keepdims=True)
            acc[side] += nn(e.astype(BF), values)

    for k in both:
        for side in both:
            send_line(side, k)
    for k in both:
        for side in both:
            attend(side, k, sides[side][4])
    for k in both:
        for side in both:
            relay_line(side, k)
    for k in both:
        for side in both:
            attend(side, k, sides[side][5][0])
            attend(side, k, sides[side][5][2])
    for side in both:
        for k in both:
            arrive(passed[side, k])
            attend(side, k, sides[side][5][1])
    load(ga, all_a)
    load(gb, all_b)

    band_y = pl.ds(pl.multiple_of(y * 256, 256), 256)
    sums = Summed(post, part, t1, th, t2, c, mate, far)
    carried = []
    loads[4].wait()

    def project(m):
        out = acc[m] / mass[m]
        att[m] = out
        lse_ref[m] = jnp.log(mass[m])
        low = out.astype(BF)
        flat[m] = jnp.concatenate([low[:ROWS], low[ROWS:]], axis=1)
        a = wo[...] if m == 0 else narrow(wo[...])
        part[m] = (nn(flat[m], a) * scale_mid).astype(BF)

    def spread(m):
        land = ca_land.at[y, pl.ds(m * ROWS, ROWS)]
        load(flat.at[m], land)
        return [post(flat.at[m], land, ys[j]) for j in range(3)]

    def norms(m):
        def slab(i, carry):
            r = pl.ds(pl.multiple_of(i * 16, 16), 16)
            v = branch[m, r].astype(F32)
            q = lax.rsqrt(jnp.mean(v * v, axis=-1, keepdims=True) + EPS)
            mid = tok[m, r].astype(F32) + v * q * norms_ref[1:2]
            middle[m, r] = mid
            q = lax.rsqrt(jnp.mean(mid * mid, axis=-1, keepdims=True) + EPS)
            ffn_in[m, r] = (mid * q * norms_ref[2:3]).astype(BF)
            return carry

        lax.fori_loop(0, ROWS // 16, slab, 0)
        fill_turned(ft, ffn_in[m], m)

    project(0)
    one = sums.start(0)
    mine = pl.ds(pl.multiple_of(c * ROWS, ROWS), ROWS)
    mine_y = pl.ds(pl.multiple_of(y * 256 + c * ROWS, ROWS), ROWS)
    dn_sent = [post(dn.at[:, yi[j], :, mine], dn_land.at[:, :, mine_y], ys[j]) for j in range(3)]
    load(dn.at[:, y], dn_land.at[:, :, band_y])
    two0 = sums.across(0, one)
    project(1)
    one = sums.start(1)
    two1 = sums.across(1, one)
    carried += spread(0)
    carried += spread(1)
    three = sums.back(0, two0, branch, 0)
    arrive(three)
    norms(0)
    carried += share(post, dn_sent, dn_land, yi, ROWS, c, mate)
    three = sums.back(1, two1, branch, 1)
    arrive(three)
    norms(1)
    arrive(carried)
    for copy in local[5:]:
        copy.wait()
    for copy in copies:
        copy.wait_send()


def front(norms, cosine, sine, tags, tag, tok, wq, wk, wv, wo, scale_in, scale_mid):
    def kernel(*refs):
        front_kernel(*refs, scale_in, scale_mid)

    any_ = whole(pl.ANY)
    both = (2, ROWS, D)
    heads = (2, 2 * ROWS, HD)
    kv = (2, 4, 4, TAGROW + 16, HD)
    turned = (2, 4, 288, 2 * ROWS)
    sems = 34 + 2 * 3 * (HALF // STEP_ROWS) + 12
    return pl.pallas_call(
        kernel,
        out_shape=[
            jax.ShapeDtypeStruct(both, F32),
            jax.ShapeDtypeStruct(both, BF),
            jax.ShapeDtypeStruct(both, BF),
            jax.ShapeDtypeStruct(heads, BF),
            jax.ShapeDtypeStruct(heads, F32),
            jax.ShapeDtypeStruct((2, 2 * ROWS, 1), F32),
            jax.ShapeDtypeStruct(turned, BF),
            jax.ShapeDtypeStruct(kv, BF),
            jax.ShapeDtypeStruct(kv, BF),
            jax.ShapeDtypeStruct((2, 288, 1024), BF),
            jax.ShapeDtypeStruct((4, 2 * ROWS, 2 * HD), BF),
        ],
        in_specs=[whole()] * 5 + [any_] * 5,
        out_specs=[whole()] * 7 + [any_] * 4,
        scratch_shapes=[
            VMEM(both, BF),
            VMEM(wq.shape, BF),
            VMEM(wk.shape, BF),
            VMEM(wv.shape, BF),
            VMEM(wo.shape, BF),
            VMEM(both, BF),
            VMEM(turned, BF),
            VMEM((2, ROWS, 2 * HD), BF),
            VMEM(kv, BF),
            VMEM(kv, BF),
            VMEM(heads, F32),
            VMEM((2, 2 * ROWS, 1), F32),
            VMEM(both, BF),
            VMEM((2, HALF, D), BF),
            VMEM((2, HALF, D), BF),
            VMEM((2, HALF, D), BF),
            pltpu.SemaphoreType.DMA((10,)),
            pltpu.SemaphoreType.DMA((sems,)),
            pltpu.SemaphoreType.DMA((sems,)),
        ],
        compiler_params=params(1, 60),
    )(norms, cosine, sine, tags, tag, tok, wq, wk, wv, wo)


LTILE = 256
FTILE = 768
ROOT = (2.0 / 3.141592653589793) ** 0.5
CUBE = 0.044715


def narrow(codes):
    level = codes * BF(1.0 / 16.0) + BF(1.0 / 32.0)
    level = (level + BF(192.0)) - BF(192.0)
    return jnp.minimum(level, BF(7.0)) * BF(16.0)


def ffn_kernel(
    x_ref, gain_ref, wg_in, wu_in, wd_in, middle_in, up_in, dg_own, du_own,
    out_ref, dup_ref, total_ref, gains, ch, dd_land, dg_land, du_land, cg, cu, pd_out,
    wg, wu, wd, middle, upstream, gate_s, up_s, hid, dgate_ref, acc, part, low, dd,
    t1, th, t2, down_sum,
    wsem, lsem, ssem, rsem,
    scale_in, scale_out,
):
    x, y, z, zh, c = place_of()
    xi = [(x + j) % 4 for j in (1, 2, 3)]
    yi = [(y + j) % 4 for j in (1, 2, 3)]
    xs = [device_at(i, y, z, zh, c) for i in xi]
    ys = [device_at(x, i, z, zh, c) for i in yi]
    mate = device_at(x, y, z, zh, 1 - c)
    far = device_at(x, y, z, 1 - zh, c)
    tiles = wg.shape[1] // FTILE
    copies, local = [], []
    post = poster(ssem, rsem, copies)
    load = loader(lsem, local)

    def weight_copies(t):
        span = pl.ds(pl.multiple_of(t * LTILE, LTILE), LTILE)
        return (
            pltpu.make_async_copy(wg_in.at[:, span], wg.at[:, span], wsem.at[0, t]),
            pltpu.make_async_copy(wu_in.at[:, span], wu.at[:, span], wsem.at[1, t]),
            pltpu.make_async_copy(wd_in.at[span], wd.at[span], wsem.at[2, t]),
        )

    def start_weights(t, carry):
        for copy in weight_copies(t):
            copy.start()
        return carry

    lax.fori_loop(0, wg.shape[1] // LTILE, start_weights, 0)
    loads = [load(middle_in, middle), load(up_in, upstream)]
    greet(xs + ys + [mate, far])
    band_x = pl.ds(pl.multiple_of(x * 256, 256), 256)
    band_y = pl.ds(pl.multiple_of(y * 256, 256), 256)
    carried = []
    mine = pl.ds(pl.multiple_of(c * ROWS, ROWS), ROWS)
    mine_y = pl.ds(pl.multiple_of(y * 256 + c * ROWS, ROWS), ROWS)
    du_sent = [post(du_own.at[:, yi[j], :, mine], du_land.at[:, :, mine_y], ys[j]) for j in range(3)]
    mine_x = pl.ds(pl.multiple_of(x * 256 + c * ROWS, ROWS), ROWS)
    dg_sent = [post(dg_own.at[:, xi[j], :, mine], dg_land.at[:, :, mine_x], xs[j]) for j in range(3)]
    load(dg_own.at[:, x], dg_land.at[:, :, band_x])
    load(du_own.at[:, y], du_land.at[:, :, band_y])

    def forward(m, first, last, wait=False):
        def body(t, carry):
            span = pl.ds(pl.multiple_of(t * FTILE, FTILE), FTILE)
            if wait:
                for k in range(FTILE // LTILE):
                    for copy in weight_copies(t * (FTILE // LTILE) + k):
                        copy.wait()
            a, b, d = wg[:, span], wu[:, span], wd[span]
            if m == 1:
                a, b, d = narrow(a), narrow(b), narrow(d)
            gate = nn(x_ref[m], a) * scale_in
            up = nn(x_ref[m], b) * scale_in
            gate_s[m, :, span] = gate
            up_s[m, :, span] = up
            bent = jnp.tanh(ROOT * (gate + CUBE * gate * gate * gate))
            hidden = (0.5 * gate * (1.0 + bent) * up).astype(BF)
            hid[m, :, span] = hidden
            acc[...] += nn(hidden, d)
            return carry

        lax.fori_loop(first, last, body, 0)

    def backward(m):
        def body(t, carry):
            span = pl.ds(pl.multiple_of(t * FTILE, FTILE), FTILE)
            d = wd[span] if m == 0 else narrow(wd[span])
            grad = nt(low[m], d) * scale_out
            v, u = gate_s[m, :, span], up_s[m, :, span]
            bent = jnp.tanh(ROOT * (v + CUBE * v * v * v))
            half = 0.5 * (1.0 + bent)
            slope = half + 0.5 * v * (1.0 - bent * bent) * (ROOT * (1.0 + 3.0 * CUBE * v * v))
            dgate_ref[m, :, span] = (grad * u * slope).astype(BF)
            dup_ref[m, :, span] = (grad * (v * half)).astype(BF)
            return carry

        lax.fori_loop(0, tiles, body, 0)

    def through(m, first, last):
        def body(t, carry):
            span = pl.ds(pl.multiple_of(t * FTILE, FTILE), FTILE)
            a, b = wg[:, span], wu[:, span]
            if m == 1:
                a, b = narrow(a), narrow(b)
            acc[...] += nt(dgate_ref[m, :, span], a) + nt(dup_ref[m, :, span], b)
            return carry

        lax.fori_loop(first, last, body, 0)

    pieces = [pl.ds(k * STEP_ROWS, STEP_ROWS) for k in range(HALF // STEP_ROWS)]

    def at_rows(core, k):
        return pl.ds(pl.multiple_of(core * HALF + k * STEP_ROWS, STEP_ROWS), STEP_ROWS)

    def sum_start(i, m):
        return [post(part.at[i, at_rows(1 - c, k)], t1.at[i, r], mate) for k, r in enumerate(pieces)]

    def sum_across(i, one):
        sent = []
        for k, r in enumerate(pieces):
            one[k].wait_recv()
            th[i, r] = (part[i, at_rows(c, k)].astype(F32) + t1[i, r].astype(F32)).astype(BF)
            sent.append(post(th.at[i, r], t2.at[i, r], far))
        return sent

    def sum_back(i, two, dst, m):
        sent = []
        for k, r in enumerate(pieces):
            two[k].wait_recv()
            dst[m, at_rows(c, k)] = (th[i, r].astype(F32) + t2[i, r].astype(F32)).astype(BF)
            sent.append(post(dst.at[m, at_rows(c, k)], dst.at[m, at_rows(c, k)], mate))
        return sent

    def arrive(sent):
        for copy in sent:
            copy.wait_recv()

    def spread_hidden(m):
        land = ch.at[y, pl.ds(m * ROWS, ROWS)]
        load(hid.at[m], land)
        return [post(hid.at[m], land, ys[j]) for j in (0, 2)]

    def spread_gate(m):
        land = cg.at[x, pl.ds(m * ROWS, ROWS)]
        load(dgate_ref.at[m], land)
        return [post(dgate_ref.at[m], land, xs[j]) for j in (0, 2)]

    def relay_rows(m, sent, land, places, devices):
        for k, j in ((0, 0), (1, 2)):
            sent[k].wait_recv()
            half = land.at[places[2 - j], pl.ds(m * ROWS + k * HALF, HALF)]
            carried.append(post(half, half, devices[j]))

    def norm(m, sums):
        def slab(i, carry):
            r = pl.ds(pl.multiple_of(i * 16, 16), 16)
            v = down_sum[m, r].astype(F32)
            du = upstream[m, r].astype(F32)
            q = lax.rsqrt(jnp.mean(v * v, axis=-1, keepdims=True) + EPS)
            gain = gain_ref[3:4]
            out_ref[m, r] = (middle[m, r] + v * q * gain).astype(BF)
            lifted = du * gain
            back = q * lifted - v * (q * q * q * jnp.mean(lifted * v, axis=-1, keepdims=True))
            low[m, r] = back.astype(BF)
            return carry + jnp.sum(du * v * q, axis=0, keepdims=True)

        return lax.fori_loop(0, ROWS // 16, slab, sums)

    def swap_down(m):
        turned = low[m].T
        for zi in range(2):
            for k in range(4):
                at = (zi * 4 + k) * 288
                dd[m, zi, k] = turned[at : at + 288]
        band = pl.ds(pl.multiple_of(y * 256, 256) + m * ROWS, ROWS)
        load(dd.at[m, :, y], dd_land.at[:, :, band])

    acc[...] = jnp.zeros_like(acc)
    forward(0, 0, tiles, True)
    part[0] = (acc[...] * scale_out).astype(BF)
    one = sum_start(0, 0)
    hidden0 = spread_hidden(0)
    acc[...] = jnp.zeros_like(acc)
    forward(1, 0, 1)
    two = sum_across(0, one)
    forward(1, 1, tiles)
    part[1] = (acc[...] * scale_out).astype(BF)
    one = sum_start(1, 1)
    hidden1 = spread_hidden(1)
    three = sum_back(0, two, down_sum, 0)
    two = sum_across(1, one)
    arrive(three)
    for copy in loads:
        copy.wait()
    sums = norm(0, jnp.zeros((1, D), F32))
    relay_rows(0, hidden0, ch, yi, ys)
    carried += share(post, du_sent, du_land, yi, ROWS, c, mate)
    carried += share(post, dg_sent, dg_land, xi, ROWS, c, mate)
    swap_down(0)
    acc[...] = jnp.zeros_like(acc)
    backward(0)
    gate0 = spread_gate(0)
    load(dup_ref.at[0], cu.at[y])
    relay_rows(1, hidden1, ch, yi, ys)
    through(0, 0, tiles)
    part[2] = (acc[...] * scale_in).astype(BF)
    one = sum_start(2, 0)
    three = sum_back(1, two, down_sum, 1)
    two = sum_across(2, one)
    arrive(three)
    gains[...] = norm(1, sums)
    swap_down(1)
    dd_sent = [post(dd.at[c, :, yi[j]], dd_land.at[:, :, mine_y], ys[j]) for j in range(3)]
    up_sent = [post(dup_ref.at[0], cu.at[y], ys[j]) for j in (0, 2)]
    acc[...] = jnp.zeros_like(acc)
    backward(1)
    gate1 = spread_gate(1)
    through(1, 0, 2)
    relay_rows(0, gate0, cg, xi, xs)
    carried += share(post, dd_sent, dd_land, yi, ROWS, c, mate)
    through(1, 2, tiles)
    part[3] = (acc[...] * scale_in).astype(BF)
    one = sum_start(3, 1)
    three = sum_back(2, two, total_ref, 0)
    two = sum_across(3, one)
    arrive(carried)
    for copy in local[2:]:
        copy.wait()
    done = len(local)
    width = 4 * 2 * ROWS
    parts = [load(ch.at[i], wg.at[pl.ds(i * 2 * ROWS, 2 * ROWS)]) for i in range(4)]
    parts += [load(dd_land.at[i], wd.at[pl.ds(i * 288, 288), pl.ds(0, width)]) for i in range(2)]
    for copy in parts:
        copy.wait()

    def down_product(t, carry):
        span = pl.ds(pl.multiple_of(t * FTILE, FTILE), FTILE)
        out = nn(wd[:PART, :width], wg[:width, span]).reshape(8, SHARE, FTILE)
        for k in range(8):
            wu[k * 80 : k * 80 + SHARE, span] = out[k].astype(BF)
        return carry

    lax.fori_loop(0, D // FTILE, down_product, 0)
    for k in range(8):
        load(wu.at[pl.ds(k * 80, SHARE)], pd_out.at[k // 4, k % 4])
    arrive(three)
    three = sum_back(3, two, total_ref, 1)
    arrive(three)
    arrive(gate1)
    arrive(up_sent)
    for copy in local[done + 6 :]:
        copy.wait()
    for copy in copies:
        copy.wait_send()


def ffn(x, gain, wg, wu, wd, middle, up, dg, du, scale_in, scale_out):
    def kernel(*refs):
        ffn_kernel(*refs, scale_in, scale_out)

    any_ = whole(pl.ANY)
    both = (2, ROWS, D)
    loads = wg.shape[1] // LTILE
    sems = 6 + 4 * 3 * (HALF // STEP_ROWS) + 8 + 6 + 6 + 12
    return pl.pallas_call(
        kernel,
        out_shape=[
            jax.ShapeDtypeStruct(both, BF),
            jax.ShapeDtypeStruct(both, BF),
            jax.ShapeDtypeStruct(both, BF),
            jax.ShapeDtypeStruct((1, D), F32),
            jax.ShapeDtypeStruct((4, 2 * ROWS, D), BF),
            jax.ShapeDtypeStruct((2, 288, 1024), BF),
            jax.ShapeDtypeStruct((8, SHARE, 1024), BF),
            jax.ShapeDtypeStruct((2, 288, 1024), BF),
            jax.ShapeDtypeStruct((4, 2 * ROWS, D), BF),
            jax.ShapeDtypeStruct((4, ROWS, D), BF),
            jax.ShapeDtypeStruct((2, 4, SHARE, D), BF),
        ],
        in_specs=[whole()] * 2 + [any_] * 7,
        out_specs=[whole()] * 4 + [any_] * 7,
        scratch_shapes=[
            VMEM(wg.shape, BF),
            VMEM(wu.shape, BF),
            VMEM(wd.shape, BF),
            VMEM(both, F32),
            VMEM(both, BF),
            VMEM(both, F32),
            VMEM(both, F32),
            VMEM(both, BF),
            VMEM(both, BF),
            VMEM((ROWS, D), F32),
            VMEM((4, ROWS, D), BF),
            VMEM(both, BF),
            VMEM((2, 2, 4, 288, ROWS), BF),
            VMEM((4, HALF, D), BF),
            VMEM((4, HALF, D), BF),
            VMEM((4, HALF, D), BF),
            VMEM(both, BF),
            pltpu.SemaphoreType.DMA((3, loads)),
            pltpu.SemaphoreType.DMA((32,)),
            pltpu.SemaphoreType.DMA((sems,)),
            pltpu.SemaphoreType.DMA((sems,)),
        ],
        compiler_params=params(5, 63),
    )(x, gain, wg, wu, wd, middle, up, dg, du)


PART = 576
SHARE = 72


def norm_grad(v, gain, grad):
    q = lax.rsqrt(jnp.mean(v * v, axis=-1, keepdims=True) + EPS)
    lifted = grad * gain
    back = q * lifted - v * (q * q * q * jnp.mean(lifted * v, axis=-1, keepdims=True))
    return back, jnp.sum(grad * v * q, axis=0, keepdims=True)


CTILE = 768


def back_kernel(
    norms_ref, q_ref, lse_ref, tag_ref, att_ref, cos_ref, sin_ref, gain_ref,
    total_in, middle_in, branch_in, up_in, wo_in, k_in, v_in, pd_in, du_in, cu0_in, cu_own, dg_in, cg_in,
    wq_in, wk_in, wv_in, tok_in, dn_in, ca_in,
    on, igrad, og, ou, od, oq, mgrad_out, cu1, cg_far, cu_far, db_land,
    dk, dv, dq, gsum, bt, pd, r1a, r1b, r2a, r2b, s2a, s2b, r3a, r3b, cq, part, t1, th, t2, total_ref, gb, rgb, pn,
    rd, ru, rg, rq, rn, zd, zu, zg, zq, zn, stage,
    lsem, csem, ssem, rsem,
    scale_mid, scale_in, scale_ff,
):
    x, y, z, zh, c = place_of()
    xi = [(x + j) % 4 for j in (1, 2, 3)]
    yi = [(y + j) % 4 for j in (1, 2, 3)]
    xs = [device_at(i, y, z, zh, c) for i in xi]
    ys = [device_at(x, i, z, zh, c) for i in yi]
    zp = device_at(x, y, 1 - z, zh, c)
    mate = device_at(x, y, z, zh, 1 - c)
    far = device_at(x, y, z, 1 - zh, c)
    copies, local = [], []
    post = poster(ssem, rsem, copies)
    load = loader(lsem, local)
    mine = pl.ds(pl.multiple_of(c * ROWS, ROWS), ROWS)
    mine_y = pl.ds(pl.multiple_of(y * 256 + c * ROWS, ROWS), ROWS)
    band_y = pl.ds(pl.multiple_of(y * 256, 256), 256)
    where = query_places()
    block = lax.axis_index("blk")
    lane = lax.broadcasted_iota(jnp.int32, (2 * ROWS, KEYS), 1)
    ring_a = Ring(post, lambda level, i: dk.at[level, :, i], r1a, x, xi, xs, add_blocks)
    ring_b = Ring(post, lambda level, i: dv.at[level, i], r1b, y, yi, ys, add_blocks)
    rings = (ring_a, ring_b)

    carried, up_sent, up_far = [], [], []

    ring_d = Ring(post, lambda level, i: pd.at[level, i], rd, x, xi, xs, add_columns)

    def first(k_ref, v_ref, wo, middle, branch, upstream, total, blow, g_ref):
        loads = [
            load(*pair)
            for pair in (
                (middle_in, middle), (branch_in, branch), (up_in, upstream), (total_in, total),
            )
        ]
        got_d = load(pd_in, pd)
        greet(xs + ys + [zp, mate, far])
        got_d.wait()
        ring_d.begin_all()
        up_sent.extend(post(lambda: cu_own.at[1], lambda: cu1.at[y], ys[j], True) for j in (0, 2))
        own_up = load(cu_own.at[1], cu1.at[y])
        for k, j in ((0, 0), (1, 2)):
            src = functools.partial(lambda j, k: cg_in.at[xi[2 - j], pl.ds(ROWS + k * HALF, HALF)], j, k)
            dst = functools.partial(lambda k: cg_far.at[pl.ds(k * HALF, HALF)], k)
            carried.append(post(src, dst, xs[j], True))
            src = functools.partial(lambda j, k: cu0_in.at[yi[2 - j], pl.ds(k * HALF, HALF)], j, k)
            dst = functools.partial(lambda k: cu_far.at[pl.ds(k * HALF, HALF)], k)
            up_far.append(post(src, dst, ys[j], True))
        for copy in loads:
            copy.wait()
        loads = [load(*pair) for pair in ((wo_in, wo), (k_in, k_ref), (v_in, v_ref))]

        sums = (jnp.zeros((1, D), F32), jnp.zeros((1, D), F32))
        for m in range(2):

            def slab(i, carry):
                r = pl.ds(pl.multiple_of(i * 16, 16), 16)
                back, more = norm_grad(middle[m, r], norms_ref[2:3], total[m, r].astype(F32))
                grad = upstream[m, r].astype(F32) + back
                middle[m, r] = grad
                back, most = norm_grad(branch[m, r].astype(F32), norms_ref[1:2], grad)
                blow[m, r] = back.astype(BF)
                return carry[0] + most, carry[1] + more

            sums = lax.fori_loop(0, ROWS // 16, slab, sums)
        gsum[1:2] = sums[0]
        gsum[2:3] = sums[1]
        gsum[3:4] = gain_ref[...]
        keep = load(middle, mgrad_out)
        loads[0].wait()
        for m in range(2):
            weight = wo[...] if m == 0 else narrow(wo[...])
            wide = (nt(blow[m], weight) * scale_mid).astype(BF)
            g_ref[m, :ROWS] = wide[:, :HD]
            g_ref[m, ROWS:] = wide[:, HD:]
        offsets = [jnp.sum(g_ref[m].astype(F32) * att_ref[m], axis=-1, keepdims=True) for m in range(2)]

        loads[1].wait()
        loads[2].wait()
        dq[...] = jnp.zeros_like(dq)

        def chunk(m, level, i):
            if m == 0:
                held, out, begin = k_ref.at[level, :, i], dk.at[level, :, i], level * 16 + i
                key_place = lane % ROWS + lane // ROWS * (4 * ROWS) + begin * ROWS
            else:
                held, out, begin = v_ref.at[level, i], dv.at[level, i], level * 16 + i * 4
                key_place = lane + begin * ROWS

            @pl.when(begin <= block)
            def _():
                q, g = q_ref[m], g_ref[m]
                keys = held[:, :ROWS, :].reshape(KEYS, HD)
                values = held[:, ROWS : 2 * ROWS, :].reshape(KEYS, HD)
                tags = held[:, TAGROW : TAGROW + 16, :ROWS].astype(F32)
                tag_row = jnp.concatenate([tags[k, 0:1, :] for k in range(CHUNK)], axis=1)
                bent = jnp.tanh(nt(q, keys) * (HD ** (-0.5) / CAP))
                ok = allowed(key_place, tag_row, tag_ref[m], where)
                p = jnp.where(ok, jnp.exp(CAP * bent - lse_ref[m]), 0.0)
                dp = nt(g, values)
                ds = (p * (dp - offsets[m]) * (1.0 - bent * bent) * HD ** (-0.5)).astype(BF)
                out[:, :ROWS, :] = tn(ds, q).astype(BF).reshape(CHUNK, ROWS, HD)
                out[:, ROWS:, :] = tn(p.astype(BF), g).astype(BF).reshape(CHUNK, ROWS, HD)
                dq[m] += nn(ds, keys)

            @pl.when(begin > block)
            def _():
                out[...] = jnp.zeros(out.shape, BF)

        for k in range(4):
            for m in range(2):
                chunk(m, *rings[m].order[k])
                rings[m].begin()
            if k == 1:
                up_far.extend(relay(post, up_sent, cu1, yi, ys))
                ring_d.onward()
        for m, places in ((0, xi), (1, yi)):
            chunk(m, 0, places[0])
            chunk(m, 1, places[2])
        for m in range(2):
            fill_turned(bt, blow[m], m)
        own = load(bt.at[:, y], db_land.at[:, :, band_y])
        for m, place in ((0, x), (1, y)):
            chunk(m, 0, place)
            chunk(m, 1, place)
        for copy in (own, keep, own_up):
            copy.wait()

    both = (2, ROWS, D)
    kv = (2, 4, 4, TAGROW + 16, HD)
    pl.run_scoped(
        first,
        VMEM(kv, BF), VMEM(kv, BF), VMEM(wo_in.shape, BF), VMEM(both, F32), VMEM(both, BF), VMEM(both, BF),
        VMEM(both, BF), VMEM(both, BF), VMEM((2, 2 * ROWS, HD), BF),
    )

    def second(pu, pg, pq, cbuf, left):
        begun = len(copies)
        used = [0]

        def fetch(sources, slot):
            out = []
            for src, dst in sources:
                copy = pltpu.make_async_copy(src, cbuf.at[(slot,) + dst], csem.at[used[0]])
                copy.start()
                used[0] += 1
                out.append(copy)
            return out

        rows_0, rows_1 = pl.ds(0, ROWS), pl.ds(ROWS, ROWS)
        everything = slice(None)

        def sources_u(cols):
            out = [(cu0_in.at[i, :, cols], (i, rows_0)) for i in (y, yi[0], yi[2])]
            out.append((cu_far.at[:, cols], (yi[1], rows_0)))
            out.append((cu1.at[:, :, cols], (everything, rows_1)))
            return out

        def sources_g(cols):
            out = [(cg_in.at[i, :, cols], (i,)) for i in (x, xi[0], xi[2])]
            out.append((cg_in.at[xi[1], rows_0, cols], (xi[1], rows_0)))
            out.append((cg_far.at[:, cols], (xi[1], rows_1)))
            return out

        tiles = [pl.ds(t * CTILE, CTILE) for t in range(D // CTILE)]
        flight = {}

        def ahead(name, sources, t, slot):
            flight[name, t] = (fetch(sources(tiles[t]), slot), slot)

        def product(name, t, weights, out):
            pending, slot = flight.pop((name, t))
            for copy in pending:
                copy.wait()
            done = nn(weights[...].reshape(PART, 1024), cbuf[slot].reshape(1024, CTILE))
            out[:, :, :, tiles[t]] = done.reshape(2, 4, SHARE, CTILE).astype(BF)

        def column_ring(p, land, along):
            held = lambda level, i: p.at[level, i]
            if along == "x":
                return Ring(post, held, land, x, xi, xs, add_columns).begin_all()
            return Ring(post, held, land, y, yi, ys, add_columns).begin_all()

        def across(ring, p, land, own):
            ring.close()
            return post(p.at[1 - z, own], land, zp)

        out_copies = {}

        def finish(copy, p, land, own, slot, width, dst, factor):
            copy.wait_recv()
            if slot in out_copies:
                out_copies[slot].wait()
            stage[slot, :, :width] = (p[z, own].astype(F32) + land[...].astype(F32)) * factor
            out_copies[slot] = load(stage.at[slot, :, pl.ds(0, width)], dst)

        left_g = load(dg_in, left.at[0])
        left_u = load(du_in, left.at[1])
        arrive(carried)
        ahead("g", sources_g, 0, 0)
        ahead("g", sources_g, 1, 1)
        ring_a.onward()
        ring_b.onward()
        left_g.wait()
        product("g", 0, left.at[0], pg)
        ahead("g", sources_g, 2, 0)
        product("g", 1, left.at[0], pg)
        product("g", 2, left.at[0], pg)
        ring_a.close()
        two_a = [post(dk.at[:, yi[j], x], r2a.at[j], ys[j]) for j in range(3)]
        ring_b.close()
        two_b = [post(dv.at[:, y, xi[j]], r2b.at[j], xs[j]) for j in range(3)]
        db_sent = [post(bt.at[:, yi[j], :, mine], db_land.at[:, :, mine_y], ys[j]) for j in range(3)]
        three_d = across(ring_d, pd, zd, x)
        arrive(up_far)
        ahead("u", sources_u, 0, 0)
        ahead("u", sources_u, 1, 1)
        left_u.wait()
        product("u", 0, left.at[1], pu)
        ahead("u", sources_u, 2, 0)
        product("u", 1, left.at[1], pu)
        product("u", 2, left.at[1], pu)
        left_n = load(dn_in, left.at[1])
        got_c = fetch([(ca_in, (everything, everything, pl.ds(0, 2 * HD)))], 1)

        def sum_two(arrivals, own, land, half):
            arrive(arrivals)
            for zi in range(2):
                out = own(zi).astype(F32)
                for j in range(3):
                    out = out + land[j, zi].astype(F32)
                half[zi] = out.astype(BF)

        def project(wq, wk, wv):
            begun = len(copies)
            weights = [load(*pair) for pair in ((wq_in, wq), (wk_in, wk), (wv_in, wv))]
            sum_two(two_a, lambda zi: dk[zi, y, x], r2a, s2a)
            three_a = post(s2a.at[1 - z], r3a, zp)
            sum_two(two_b, lambda zi: dv[zi, y, x], r2b, s2b)
            three_b = post(s2b.at[1 - z], r3b, zp)
            ring_u = column_ring(pu, ru, "x")
            carried.extend(share(post, db_sent, db_land, yi, ROWS, c, mate))
            cosine, sine = cos_ref[...], -sin_ref[...]
            for m in range(2):
                r = slice(m * ROWS, (m + 1) * ROWS)
                for h in range(2):
                    turned = turn(dq[m, h * ROWS : (h + 1) * ROWS], cosine, sine)
                    cq[y, r, h * HD : (h + 1) * HD] = turned.astype(BF)
            for m, (copy, half, land) in enumerate(((three_a, s2a, r3a), (three_b, s2b, r3b))):
                r = slice(m * ROWS, (m + 1) * ROWS)
                copy.wait_recv()
                pair = half[z].astype(F32) + land[...].astype(F32)
                cq[y, r, 2 * HD : 3 * HD] = turn(pair[:ROWS], cosine, sine).astype(BF)
                cq[y, r, 3 * HD :] = pair[ROWS:].astype(BF)
            own = lambda: cq.at[y]
            cq_sent = [post(own, own, ys[j], True) for j in (0, 2)]
            for copy in weights:
                copy.wait()
            sums = Summed(post, part, t1, th, t2, c, mate, far)
            ones = []
            for m in range(2):
                r = slice(m * ROWS, (m + 1) * ROWS)
                a, b, v = wq[...], wk[...], wv[...]
                if m == 1:
                    a, b, v = narrow(a), narrow(b), narrow(v)
                out = nt(cq[y, r, : 2 * HD], a) + nt(cq[y, r, 2 * HD : 3 * HD], b) + nt(cq[y, r, 3 * HD :], v)
                part[m] = (out * scale_in).astype(BF)
                ones.append(sums.start(m))
            twos = [sums.across(m, ones[m]) for m in range(2)]
            settle(copies[begun:])
            return ring_u, cq_sent, sums, twos

        between = len(copies)
        state = []
        pl.run_scoped(
            lambda *refs: state.append(project(*refs)),
            VMEM(wq_in.shape, BF), VMEM(wk_in.shape, BF), VMEM(wv_in.shape, BF),
        )
        ring_u, cq_sent, sums, twos = state[0]
        arrive(carried[2:])
        left_b = load(db_land, left.at[0])
        cq_far = relay(post, cq_sent, cq, yi, ys)
        ring_u.onward()
        left_b.wait()
        for copy in got_c:
            copy.wait()
        out = nn(left[0].reshape(PART, 1024), cbuf[1, :, :, : 2 * HD].reshape(1024, 512))
        pq[:, :, :, 1024:] = out.reshape(2, 4, SHARE, 512).astype(BF)
        settle(copies[begun:between])
        left_n.wait()
        arrive(cq_far)
        ring_g = column_ring(pg, rg, "y")
        for t in range(2):
            cols = pl.ds(t * 512, 512)
            out = nn(left[1].reshape(PART, 1024), cq[:, :, cols].reshape(1024, 512))
            pq[:, :, :, cols] = out.reshape(2, 4, SHARE, 512).astype(BF)
        ring_q = column_ring(pq, rq, "x")

        def last(tok, mgrad, gpad):
            begun = len(copies)
            got = [load(tok_in, tok), load(mgrad_out, mgrad)]
            threes = [sums.back(m, twos[m], total_ref, m) for m in range(2)]
            for copy in got:
                copy.wait()
            gain = jnp.zeros((1, D), F32)
            for m in range(2):
                arrive(threes[m])

                def slab(i, carry):
                    r = pl.ds(pl.multiple_of(i * 16, 16), 16)
                    back, more = norm_grad(tok[m, r].astype(F32), norms_ref[0:1], total_ref[m, r].astype(F32))
                    part[m, r] = (mgrad[m, r] + back).astype(BF)
                    return carry + more

                gain = lax.fori_loop(0, ROWS // 16, slab, gain)
            out_grad = load(part, igrad)
            gpad[...] = jnp.zeros_like(gpad)
            gpad[0:1] = gain
            gpad[1:4] = gsum[1:4]
            turned = gpad[...].T.astype(BF)
            for zi in range(2):
                for k in range(4):
                    at = (zi * 4 + k) * 288
                    gb[zi, k] = turned[at : at + 288]
            gains_far = [post(gb.at[:, yi[j]], rgb.at[j], ys[j]) for j in range(3)]
            finish(three_d, pd, zd, x, 0, D, od, scale_ff)
            three_u = across(ring_u, pu, zu, x)
            out = gb[:, y].astype(F32)
            for j in range(3):
                gains_far[j].wait_recv()
                out = out + rgb[j].astype(F32)
            pn[...] = out.reshape(2, 4, SHARE, 128).astype(BF)
            ring_n = column_ring(pn, rn, "x")
            ring_g.onward()
            ring_q.onward()
            finish(three_u, pu, zu, x, 1, D, ou, scale_in)
            ring_n.onward()
            three_g = across(ring_g, pg, zg, y)
            three_q = across(ring_q, pq, zq, x)
            three_n = across(ring_n, pn, zn, x)
            finish(three_g, pg, zg, y, 0, D, og, scale_in)
            finish(three_q, pq, zq, x, 1, 1536, oq, 1.0)
            three_n.wait_recv()
            on[...] = pn[z, x].astype(F32) + zn[...].astype(F32)
            out_grad.wait()
            for copy in out_copies.values():
                copy.wait()
            settle(copies[begun:])

        pl.run_scoped(last, VMEM(both, BF), VMEM(both, F32), VMEM((128, D), F32))
        settle(copies, True)

    wide = (2, 4, SHARE, D)
    pl.run_scoped(
        second,
        VMEM(wide, BF), VMEM(wide, BF), VMEM((2, 4, SHARE, 1536), BF),
        VMEM((2, 4, 2 * ROWS, CTILE), BF), VMEM((2, 2, 288, 1024), BF),
    )


def back(inputs, scale_mid, scale_in, scale_ff):
    def kernel(*refs):
        back_kernel(*refs, scale_mid, scale_in, scale_ff)

    any_ = whole(pl.ANY)
    tile = (2 * ROWS, HD)
    both = (2, ROWS, D)
    sems = 4 + 8 + 12 + 6 + 2 + 6 + 4 * 7 + 7 + 4 + 2 * 3 * (HALF // STEP_ROWS) + 3
    return pl.pallas_call(
        kernel,
        out_shape=[
            jax.ShapeDtypeStruct((SHARE, 128), F32),
            jax.ShapeDtypeStruct(both, BF),
            jax.ShapeDtypeStruct((SHARE, D), F32),
            jax.ShapeDtypeStruct((SHARE, D), F32),
            jax.ShapeDtypeStruct((SHARE, D), F32),
            jax.ShapeDtypeStruct((SHARE, 1536), F32),
            jax.ShapeDtypeStruct(both, F32),
            jax.ShapeDtypeStruct((4, ROWS, D), BF),
            jax.ShapeDtypeStruct((ROWS, D), BF),
            jax.ShapeDtypeStruct((ROWS, D), BF),
            jax.ShapeDtypeStruct((2, 288, 1024), BF),
        ],
        in_specs=[whole()] * 8 + [any_] * 19,
        out_specs=[whole()] + [any_] * 10,
        scratch_shapes=[
            VMEM((2, 4, 4) + tile, BF),
            VMEM((2, 4, 4) + tile, BF),
            VMEM((2,) + tile, F32),
            VMEM((8, D), F32),
            VMEM((2, 4, 288, 2 * ROWS), BF),
            VMEM((2, 4, SHARE, D), BF),
            VMEM((6, 4) + tile, BF),
            VMEM((6, 4) + tile, BF),
            VMEM((3, 2) + tile, BF),
            VMEM((3, 2) + tile, BF),
            VMEM((2,) + tile, BF),
            VMEM((2,) + tile, BF),
            VMEM(tile, BF),
            VMEM(tile, BF),
            VMEM((4, 2 * ROWS, 1024), BF),
            VMEM(both, BF),
            VMEM((2, HALF, D), BF),
            VMEM((2, HALF, D), BF),
            VMEM((2, HALF, D), BF),
            VMEM(both, BF),
            VMEM((2, 4, 288, 128), BF),
            VMEM((3, 2, 288, 128), BF),
            VMEM((2, 4, SHARE, 128), BF),
        ]
        + [VMEM((6, SHARE, w), BF) for w in (D, D, D, 1536, 128)]
        + [VMEM((SHARE, w), BF) for w in (D, D, D, 1536, 128)]
        + [
            VMEM((2, SHARE, D), F32),
            pltpu.SemaphoreType.DMA((48,)),
            pltpu.SemaphoreType.DMA((32,)),
            pltpu.SemaphoreType.DMA((sems,)),
            pltpu.SemaphoreType.DMA((sems,)),
        ],
        compiler_params=params(2, 63),
    )(*inputs)


def shards(
    inputs,
    out_grad,
    segment_ids,
    keep_mask,
    query_codes,
    key_codes,
    value_codes,
    output_codes,
    gate_codes,
    up_codes,
    down_codes,
    norm_attn_in,
    norm_attn_out,
    norm_ffn_in,
    norm_ffn_out,
):
    rows = inputs.shape[1]
    place = lax.axis_index("blk") * rows + jnp.arange(rows, dtype=jnp.int32)
    freqs = 10000.0 ** (-jnp.arange(HD // 2, dtype=F32) * 2.0 / HD)
    angles = place.astype(F32)[:, None] * freqs[None, :]
    cosine = jnp.cos(angles)
    sine = jnp.sin(angles)
    in_scale = LEVEL_SCALE * D ** (-0.5)
    mid_scale = LEVEL_SCALE * (HEADS * HD) ** (-0.5)
    ff_scale = LEVEL_SCALE * FF ** (-0.5)

    norms = jnp.stack([norm_attn_in, norm_attn_out, norm_ffn_in, norm_ffn_out])
    key_tag = jnp.where(keep_mask == 1, segment_ids, -1).astype(BF)
    key_tag = jnp.concatenate([key_tag, jnp.zeros_like(key_tag)], axis=1)
    key_tag = jnp.broadcast_to(key_tag[:, None, :], (2, 16, 2 * rows))
    tag = segment_ids.astype(F32)
    tag = jnp.concatenate([tag, tag], axis=1)[:, :, None]
    (
        middle, branch, ffn_in, queries, attended, lse, ffn_turned, blocks_a, blocks_b, d_normed, all_attended,
    ) = front(
        norms, cosine, sine, key_tag, tag,
        inputs, query_codes, key_codes, value_codes, output_codes, in_scale, mid_scale,
    )
    out_rows, up_low, ffn_in_grad, gain_ffn_out, _, _, d_gate, d_up, cg, cu0, p_down = ffn(
        ffn_in, norms, gate_codes, up_codes, down_codes, middle, out_grad,
        ffn_turned.reshape(8, 4, SHARE, 2 * rows), ffn_turned, in_scale, ff_scale,
    )
    g_gains, input_grad, g_gate, g_up, g_down, g_rest = back(
        (
            norms, queries, lse, tag, attended, cosine, sine, gain_ffn_out,
            ffn_in_grad, middle, branch, out_grad, output_codes, blocks_a, blocks_b,
            p_down, d_up, cu0, up_low, d_gate.reshape(2, 288, 1024), cg,
            query_codes, key_codes, value_codes, inputs, d_normed, all_attended,
        ),
        mid_scale,
        in_scale,
        ff_scale,
    )[:6]
    return (
        out_rows,
        input_grad,
        g_rest[:, :512] * in_scale,
        g_rest[:, 512:768] * in_scale,
        g_rest[:, 768:1024] * in_scale,
        g_rest[:, 1024:1536].T * mid_scale,
        g_gate,
        g_up,
        g_down.T,
        g_gains[:, 0],
        g_gains[:, 1],
        g_gains[:, 2],
        g_gains[:, 3],
    )


def solution(mesh):
    placed = (
        P(None, "blk", None),
        P(None, "blk", None),
        P(None, "blk"),
        P(None, "blk"),
        P(None, "tensor"),
        P(None, "tensor"),
        P(None, "tensor"),
        P("tensor", None),
        P(None, "tensor"),
        P(None, "tensor"),
        P("tensor", None),
        P(),
        P(),
        P(),
        P(),
    )
    return jax.shard_map(
        shards,
        mesh=mesh,
        in_specs=placed,
        out_specs=(
            P(None, "blk", None),
            P(None, "blk", None),
            P("blk", "tensor"),
            P("blk", "tensor"),
            P("blk", "tensor"),
            P("tensor", "blk"),
            P("blk", "tensor"),
            P("blk", "tensor"),
            P("tensor", "blk"),
            P("blk"),
            P("blk"),
            P("blk"),
            P("blk"),
        ),
        check_vma=False,
    )
```

```python
import functools

import jax
import jax.numpy as jnp
from jax import lax
from jax.experimental import pallas as pl
from jax.experimental.pallas import tpu as pltpu
from jax.sharding import PartitionSpec as P

D = 2304
HEADS = 8
HD = 256
FF = 9216

CAP = 50.0
EPS = 1e-06
LEVEL_SCALE = 1.0 / 74.0
WIDTHS = (8, 4, 2)

MESH = pl.DeviceIdType.MESH
VMEM = pltpu.VMEM
BF = jnp.bfloat16
F32 = jnp.float32
SEQ = 4096
ROWS = 128
TAGROW = 256
MASKED = -2.0


def place_of():
    b = lax.axis_index("blk")
    t = lax.axis_index("tensor")
    return b % 4, (b // 4) % 4, b // 16, t // 2, t % 2


def device_at(x, y, z, zh, c):
    return ((z * 4 + y) * 4 + x, zh * 2 + c)


def greet(peers):
    barrier = pltpu.get_barrier_semaphore()
    for peer in peers:
        pl.semaphore_signal(barrier, inc=1, device_id=peer, device_id_type=MESH)
    pl.semaphore_wait(barrier, len(peers))


def send(src, dst, ssem, rsem, peer):
    copy = pltpu.make_async_remote_copy(
        src_ref=src, dst_ref=dst, send_sem=ssem, recv_sem=rsem, device_id=peer, device_id_type=MESH
    )
    copy.start()
    return copy


def params(collective_id=None, limit=60):
    if collective_id is None:
        return pltpu.CompilerParams(vmem_limit_bytes=limit << 20)
    return pltpu.CompilerParams(
        vmem_limit_bytes=limit << 20, collective_id=collective_id, has_side_effects=True
    )


def whole(space=VMEM):
    return pl.BlockSpec(memory_space=space)


CHUNK = 4
KEYS = CHUNK * ROWS


def nt(left, right):
    return lax.dot_general(left, right, (((1,), (1,)), ((), ())), preferred_element_type=F32)


def tn(left, right):
    return lax.dot_general(left, right, (((0,), (0,)), ((), ())), preferred_element_type=F32)


def nn(left, right):
    return jnp.dot(left, right, preferred_element_type=F32)


def allowed(key_place, tag_row, query_tag, query_place):
    ok = (key_place <= query_place) & (tag_row == query_tag)
    return ok | (key_place == query_place)


def query_places():
    row = lax.broadcasted_iota(jnp.int32, (2 * ROWS, 1), 0)
    return lax.axis_index("blk") * ROWS + row % ROWS


class Later:
    def __init__(self, src, dst, ssem, rsem, k, peer):
        self.src, self.dst, self.ssem, self.rsem, self.k, self.peer = src, dst, ssem, rsem, k, peer

    def describe(self):
        return pltpu.make_async_remote_copy(
            src_ref=self.src(),
            dst_ref=self.dst(),
            send_sem=self.ssem.at[self.k],
            recv_sem=self.rsem.at[self.k],
            device_id=self.peer,
            device_id_type=MESH,
        )

    def wait_recv(self):
        self.describe().wait_recv()

    def wait_send(self):
        self.describe().wait_send()


def poster(ssem, rsem, copies):
    def post(src, dst, peer, later=False):
        k = len(copies)
        if later:
            copies.append(Later(src, dst, ssem, rsem, k, peer))
            copies[k].describe().start()
        else:
            copies.append(send(src, dst, ssem.at[k], rsem.at[k], peer))
        return copies[k]

    return post


def settle(copies, later=False):
    for copy in copies:
        if isinstance(copy, Later) == later:
            copy.wait_send()


def loader(sem, copies):
    def load(src, dst):
        copy = pltpu.make_async_copy(src, dst, sem.at[len(copies)])
        copy.start()
        copies.append(copy)
        return copy

    return load


def arrive(copies):
    for copy in copies:
        copy.wait_recv()


def turn(values, cosine, sine):
    half = HD // 2
    first, second = values[:, :half], values[:, half:]
    return jnp.concatenate([first * cosine - second * sine, second * cosine + first * sine], axis=1)


def fill_turned(dst, value, m):
    turned = value.T
    for zi in range(2):
        for k in range(4):
            at = (zi * 4 + k) * 288
            dst[zi, k, :, m * ROWS : (m + 1) * ROWS] = turned[at : at + 288]


HALF = ROWS // 2
STEP_ROWS = 32


class Summed:
    def __init__(self, post, part, t1, th, t2, c, mate, far):
        self.post, self.part, self.t1, self.th, self.t2 = post, part, t1, th, t2
        self.c, self.mate, self.far = c, mate, far
        self.pieces = [pl.ds(k * STEP_ROWS, STEP_ROWS) for k in range(HALF // STEP_ROWS)]

    def rows(self, core, k):
        return pl.ds(pl.multiple_of(core * HALF + k * STEP_ROWS, STEP_ROWS), STEP_ROWS)

    @staticmethod
    def piece(ref, i, r):
        return ref.at[i, r]

    def start(self, i):
        other = 1 - self.c
        return [
            self.post(self.part.at[i, self.rows(other, k)], self.t1.at[i, r], self.mate)
            for k, r in enumerate(self.pieces)
        ]

    def across(self, i, one):
        sent = []
        for k, r in enumerate(self.pieces):
            one[k].wait_recv()
            own = self.part[i, self.rows(self.c, k)].astype(F32)
            self.th[i, r] = (own + self.t1[i, r].astype(F32)).astype(BF)
            src, dst = functools.partial(self.piece, self.th, i, r), functools.partial(self.piece, self.t2, i, r)
            sent.append(self.post(src, dst, self.far, True))
        return sent

    def back(self, i, two, dst, m):
        sent = []
        for k, r in enumerate(self.pieces):
            two[k].wait_recv()
            rows = self.rows(self.c, k)
            dst[m, rows] = (self.th[i, r].astype(F32) + self.t2[i, r].astype(F32)).astype(BF)
            sent.append(self.post(dst.at[m, rows], dst.at[m, rows], self.mate))
        return sent


def relay(post, sent, land, places, devices):
    out = []
    size = land.shape[1] // 2
    for k, j in ((0, 0), (1, 2)):
        sent[k].wait_recv()
        half = functools.partial(lambda place, k: land.at[place, pl.ds(k * size, size)], places[2 - j], k)
        out.append(post(half, half, devices[j], True))
    return out


def share(post, sent, land, places, width, c, mate):
    def band(place):
        begin = pl.multiple_of(place * (2 * width), 2 * width) + c * width
        return land.at[:, :, pl.ds(pl.multiple_of(begin, width), width)]

    out = []
    for j, copy in enumerate(sent):
        copy.wait_recv()
        own = functools.partial(band, places[2 - j])
        out.append(post(own, own, mate, True))
    return out


class Ring:
    def __init__(self, post, held, land, mine, places, devices, add):
        self.post, self.land, self.mine, self.places, self.devices = post, land, mine, places, devices
        self.held, self.add = held, add
        near, across, far = places
        self.order = ((0, across), (1, across), (1, near), (0, far))
        self.sent = []

    def begin(self):
        k = len(self.sent)
        src = functools.partial(self.held, *self.order[k])
        dst = functools.partial(self.slot, k)
        self.sent.append(self.post(src, dst, self.devices[0 if k % 2 == 0 else 2], True))

    def slot(self, k):
        return self.land.at[k]

    def begin_all(self):
        for _ in self.order:
            self.begin()
        return self

    def onward(self):
        self.passed = []
        for level, j in ((0, 0), (1, 2)):
            self.sent[level].wait_recv()
            ref = self.held(level, self.places[j])
            self.add(ref, ref, (self.land.at[level],))
            src = functools.partial(self.held, level, self.places[j])
            dst = functools.partial(self.slot, 4 + level)
            self.passed.append(self.post(src, dst, self.devices[j], True))

    def close(self):
        for level in range(2):
            self.sent[3 - level].wait_recv()
            self.passed[level].wait_recv()
            own = self.held(level, self.mine)
            self.add(own, own, (self.land.at[3 - level], self.land.at[4 + level]))


def add_blocks(dst, own, others):
    def body(k, carry):
        out = own[k].astype(F32)
        for other in others:
            out = out + other[k].astype(F32)
        dst[k] = out.astype(BF)
        return carry

    lax.fori_loop(0, own.shape[0], body, 0)


def add_columns(dst, own, others):
    tile = 256 if own.shape[-1] % 256 == 0 else 128

    def body(t, carry):
        cols = pl.ds(pl.multiple_of(t * tile, tile), tile)
        out = own[:, cols].astype(F32)
        for other in others:
            out = out + other[:, cols].astype(F32)
        dst[:, cols] = out.astype(BF)
        return carry

    lax.fori_loop(0, own.shape[-1] // tile, body, 0)


CUT = 144


def front_kernel(
    norms_ref, cos_ref, sin_ref, tags, tag_ref,
    tok_in, wq_in, wk_in, wv_in, wo_in,
    middle, branch, ffn_in, q_ref, att, lse_ref, ft, all_a, all_b, dn_land, ca_land,
    tok, wq, wk, wv, wo, normed, dn, flat, ga, gb, acc, mass, part, t1, th, t2,
    lsem, ssem, rsem,
    scale_in, scale_mid,
):
    x, y, z, zh, c = place_of()
    block = lax.axis_index("blk")
    xi = [(x + j) % 4 for j in (1, 2, 3)]
    yi = [(y + j) % 4 for j in (1, 2, 3)]
    xs = [device_at(i, y, z, zh, c) for i in xi]
    ys = [device_at(x, i, z, zh, c) for i in yi]
    zp = device_at(x, y, 1 - z, zh, c)
    mate = device_at(x, y, z, zh, 1 - c)
    far = device_at(x, y, z, 1 - zh, c)
    copies, local = [], []
    post = poster(ssem, rsem, copies)
    load = loader(lsem, local)
    loads = [
        load(*pair)
        for pair in ((tok_in, tok), (wk_in, wk), (wv_in, wv), (wq_in, wq), (wo_in, wo))
    ]
    greet(xs + ys + [zp, mate, far])

    loads[0].wait()
    for m in range(2):

        def slab(i, carry):
            r = pl.ds(pl.multiple_of(i * 16, 16), 16)
            v = tok[m, r].astype(F32)
            q = lax.rsqrt(jnp.mean(v * v, axis=-1, keepdims=True) + EPS)
            normed[m, r] = (v * q * norms_ref[0:1]).astype(BF)
            return carry

        lax.fori_loop(0, ROWS // 16, slab, 0)
    loads[1].wait()
    loads[2].wait()
    cosine, sine = cos_ref[...], sin_ref[...]
    for m, held in ((0, ga), (1, gb)):
        a, b = wk[...], wv[...]
        if m == 1:
            a, b = narrow(a), narrow(b)
        held[z, y, x, :ROWS] = turn(nn(normed[m], a) * scale_in, cosine, sine).astype(BF)
        held[z, y, x, ROWS : 2 * ROWS] = (nn(normed[m], b) * scale_in).astype(BF)
        held[z, y, x, TAGROW:] = tags[m]

    levels = (z, 1 - z)

    def at_a(level, along_x, along_y, part=None):
        ref = ga.at[level, along_y, along_x]
        return ref if part is None else ref.at[part]

    def at_b(level, along_y, along_x, part=None):
        ref = gb.at[level, along_y, along_x]
        return ref if part is None else ref.at[part]

    first_half, last_half = pl.ds(0, CUT), pl.ds(CUT, TAGROW + 16 - CUT)
    sides = (
        (at_a, x, xi, xs, y, yi, ys),
        (at_b, y, yi, ys, x, xi, xs),
    )

    def line(side, level, second, pair=None):
        if side == 0:
            return ga.at[level, second] if pair is None else ga.at[level, second, pair]
        return gb.at[level, :, second] if pair is None else gb.at[level, pair, second]

    across = []
    for at, one, places, devices, two, _, _ in sides:
        own = at(z, one, two)
        across.append(post(own, own, zp))
    near = {}

    def send_near(side, k):
        at, one, places, devices, two, _, _ = sides[side]
        own = at(levels[k], one, two)
        near[side, k] = [post(own, own, devices[j]) for j in (0, 2)]

    relays = {}

    def relay_near(side, k):
        at, one, places, devices, two, _, _ = sides[side]
        sent = near[side, k]
        sent[0].wait_recv()
        piece = at(levels[k], places[2], two, first_half)
        relays[side, k] = [post(piece, piece, devices[0])]
        sent[1].wait_recv()
        piece = at(levels[k], places[0], two, last_half)
        relays[side, k].append(post(piece, piece, devices[2]))

    lines = {}

    def send_line(side, k):
        _, _, _, _, two, _, devices = sides[side]
        arrive(relays[side, k])
        own = line(side, levels[k], two)
        lines[side, k] = [post(own, own, devices[j]) for j in (0, 2)]

    passed = {}

    def relay_line(side, k):
        _, _, _, _, _, places, devices = sides[side]
        sent = lines[side, k]
        sent[0].wait_recv()
        piece = line(side, levels[k], places[2], pl.ds(0, 2))
        passed[side, k] = [post(piece, piece, devices[0])]
        sent[1].wait_recv()
        piece = line(side, levels[k], places[0], pl.ds(2, 2))
        passed[side, k].append(post(piece, piece, devices[2]))

    both = (0, 1)
    for side in both:
        send_near(side, 0)
    loads[3].wait()
    for m in range(2):
        a = wq[...] if m == 0 else narrow(wq[...])
        wide = nn(normed[m], a) * scale_in
        for h in range(2):
            turned = turn(wide[:, h * HD : (h + 1) * HD], cosine, sine)
            q_ref[m, h * ROWS : (h + 1) * ROWS] = turned.astype(BF)
        fill_turned(dn, normed[m], m)
    arrive(across)
    for side in both:
        send_near(side, 1)
    for k in both:
        for side in both:
            relay_near(side, k)

    acc[...] = jnp.zeros_like(acc)
    mass[...] = jnp.zeros_like(mass)
    where = query_places()
    lane = lax.broadcasted_iota(jnp.int32, (2 * ROWS, KEYS), 1)

    def attend(side, k, second):
        level = levels[k]
        if side == 0:
            held, begin, key_place = ga.at[level, second], level * 16 + second * 4, lane
            stride = 1
        else:
            held, begin, key_place = gb.at[level, :, second], level * 16 + second, lane % ROWS + lane // ROWS * (4 * ROWS)
            stride = 4

        @pl.when(begin <= block)
        def _():
            keys = held[:, :ROWS, :].reshape(KEYS, HD)
            values = held[:, ROWS : 2 * ROWS, :].reshape(KEYS, HD)
            tag = held[:, TAGROW : TAGROW + 16, :ROWS].astype(F32)
            tag_row = jnp.concatenate([tag[i, 0:1, :] for i in range(CHUNK)], axis=1)
            bent = jnp.tanh(nt(q_ref[side], keys) * (HD ** (-0.5) / CAP))
            ok = allowed(key_place + begin * ROWS, tag_row, tag_ref[side], where)
            e = jnp.where(ok, jnp.exp(CAP * bent), 0.0)
            mass[side] += jnp.sum(e, axis=-1, keepdims=True)
            acc[side] += nn(e.astype(BF), values)

    for k in both:
        for side in both:
            send_line(side, k)
    for k in both:
        for side in both:
            attend(side, k, sides[side][4])
    for k in both:
        for side in both:
            relay_line(side, k)
    for k in both:
        for side in both:
            attend(side, k, sides[side][5][0])
            attend(side, k, sides[side][5][2])
    for side in both:
        for k in both:
            arrive(passed[side, k])
            attend(side, k, sides[side][5][1])
    load(ga, all_a)
    load(gb, all_b)

    band_y = pl.ds(pl.multiple_of(y * 256, 256), 256)
    sums = Summed(post, part, t1, th, t2, c, mate, far)
    carried = []
    loads[4].wait()

    def project(m):
        out = acc[m] / mass[m]
        att[m] = out
        lse_ref[m] = jnp.log(mass[m])
        low = out.astype(BF)
        flat[m] = jnp.concatenate([low[:ROWS], low[ROWS:]], axis=1)
        a = wo[...] if m == 0 else narrow(wo[...])
        part[m] = (nn(flat[m], a) * scale_mid).astype(BF)

    def spread(m):
        land = ca_land.at[y, pl.ds(m * ROWS, ROWS)]
        load(flat.at[m], land)
        return [post(flat.at[m], land, ys[j]) for j in range(3)]

    def norms(m):
        def slab(i, carry):
            r = pl.ds(pl.multiple_of(i * 16, 16), 16)
            v = branch[m, r].astype(F32)
            q = lax.rsqrt(jnp.mean(v * v, axis=-1, keepdims=True) + EPS)
            mid = tok[m, r].astype(F32) + v * q * norms_ref[1:2]
            middle[m, r] = mid
            q = lax.rsqrt(jnp.mean(mid * mid, axis=-1, keepdims=True) + EPS)
            ffn_in[m, r] = (mid * q * norms_ref[2:3]).astype(BF)
            return carry

        lax.fori_loop(0, ROWS // 16, slab, 0)
        fill_turned(ft, ffn_in[m], m)

    project(0)
    one = sums.start(0)
    mine = pl.ds(pl.multiple_of(c * ROWS, ROWS), ROWS)
    mine_y = pl.ds(pl.multiple_of(y * 256 + c * ROWS, ROWS), ROWS)
    dn_sent = [post(dn.at[:, yi[j], :, mine], dn_land.at[:, :, mine_y], ys[j]) for j in range(3)]
    load(dn.at[:, y], dn_land.at[:, :, band_y])
    two0 = sums.across(0, one)
    project(1)
    one = sums.start(1)
    two1 = sums.across(1, one)
    carried += spread(0)
    carried += spread(1)
    three = sums.back(0, two0, branch, 0)
    arrive(three)
    norms(0)
    carried += share(post, dn_sent, dn_land, yi, ROWS, c, mate)
    three = sums.back(1, two1, branch, 1)
    arrive(three)
    norms(1)
    arrive(carried)
    for copy in local[5:]:
        copy.wait()
    for copy in copies:
        copy.wait_send()


def front(norms, cosine, sine, tags, tag, tok, wq, wk, wv, wo, scale_in, scale_mid):
    def kernel(*refs):
        front_kernel(*refs, scale_in, scale_mid)

    any_ = whole(pl.ANY)
    both = (2, ROWS, D)
    heads = (2, 2 * ROWS, HD)
    kv = (2, 4, 4, TAGROW + 16, HD)
    turned = (2, 4, 288, 2 * ROWS)
    sems = 34 + 2 * 3 * (HALF // STEP_ROWS) + 12
    return pl.pallas_call(
        kernel,
        out_shape=[
            jax.ShapeDtypeStruct(both, F32),
            jax.ShapeDtypeStruct(both, BF),
            jax.ShapeDtypeStruct(both, BF),
            jax.ShapeDtypeStruct(heads, BF),
            jax.ShapeDtypeStruct(heads, F32),
            jax.ShapeDtypeStruct((2, 2 * ROWS, 1), F32),
            jax.ShapeDtypeStruct(turned, BF),
            jax.ShapeDtypeStruct(kv, BF),
            jax.ShapeDtypeStruct(kv, BF),
            jax.ShapeDtypeStruct((2, 288, 1024), BF),
            jax.ShapeDtypeStruct((4, 2 * ROWS, 2 * HD), BF),
        ],
        in_specs=[whole()] * 5 + [any_] * 5,
        out_specs=[whole()] * 7 + [any_] * 4,
        scratch_shapes=[
            VMEM(both, BF),
            VMEM(wq.shape, BF),
            VMEM(wk.shape, BF),
            VMEM(wv.shape, BF),
            VMEM(wo.shape, BF),
            VMEM(both, BF),
            VMEM(turned, BF),
            VMEM((2, ROWS, 2 * HD), BF),
            VMEM(kv, BF),
            VMEM(kv, BF),
            VMEM(heads, F32),
            VMEM((2, 2 * ROWS, 1), F32),
            VMEM(both, BF),
            VMEM((2, HALF, D), BF),
            VMEM((2, HALF, D), BF),
            VMEM((2, HALF, D), BF),
            pltpu.SemaphoreType.DMA((10,)),
            pltpu.SemaphoreType.DMA((sems,)),
            pltpu.SemaphoreType.DMA((sems,)),
        ],
        compiler_params=params(1, 60),
    )(norms, cosine, sine, tags, tag, tok, wq, wk, wv, wo)


LTILE = 256
FTILE = 768
ROOT = (2.0 / 3.141592653589793) ** 0.5
CUBE = 0.044715


def narrow(codes):
    level = codes * BF(1.0 / 16.0) + BF(1.0 / 32.0)
    level = (level + BF(192.0)) - BF(192.0)
    return jnp.minimum(level, BF(7.0)) * BF(16.0)


def ffn_kernel(
    x_ref, gain_ref, wg_in, wu_in, wd_in, middle_in, up_in, branch_in, dg_own, du_own,
    out_ref, dup_ref, total_ref, gains, ch, dd_land, dg_land, du_land, cg, cu, pd_out, mgrad_out, blow_out,
    wg, wu, wd, middle, upstream, gate_s, up_s, hid, dgate_ref, acc, part, low, dd,
    t1, th, t2, down_sum, branch,
    wsem, lsem, ssem, rsem,
    scale_in, scale_out,
):
    x, y, z, zh, c = place_of()
    xi = [(x + j) % 4 for j in (1, 2, 3)]
    yi = [(y + j) % 4 for j in (1, 2, 3)]
    xs = [device_at(i, y, z, zh, c) for i in xi]
    ys = [device_at(x, i, z, zh, c) for i in yi]
    mate = device_at(x, y, z, zh, 1 - c)
    far = device_at(x, y, z, 1 - zh, c)
    tiles = wg.shape[1] // FTILE
    copies, local = [], []
    post = poster(ssem, rsem, copies)
    load = loader(lsem, local)

    def weight_copies(t):
        span = pl.ds(pl.multiple_of(t * LTILE, LTILE), LTILE)
        return (
            pltpu.make_async_copy(wg_in.at[:, span], wg.at[:, span], wsem.at[0, t]),
            pltpu.make_async_copy(wu_in.at[:, span], wu.at[:, span], wsem.at[1, t]),
            pltpu.make_async_copy(wd_in.at[span], wd.at[span], wsem.at[2, t]),
        )

    def start_weights(t, carry):
        for copy in weight_copies(t):
            copy.start()
        return carry

    lax.fori_loop(0, wg.shape[1] // LTILE, start_weights, 0)
    loads = [load(middle_in, middle), load(up_in, upstream)]
    greet(xs + ys + [mate, far])
    band_x = pl.ds(pl.multiple_of(x * 256, 256), 256)
    band_y = pl.ds(pl.multiple_of(y * 256, 256), 256)
    carried = []
    mine = pl.ds(pl.multiple_of(c * ROWS, ROWS), ROWS)
    mine_y = pl.ds(pl.multiple_of(y * 256 + c * ROWS, ROWS), ROWS)
    du_sent = [post(du_own.at[:, yi[j], :, mine], du_land.at[:, :, mine_y], ys[j]) for j in range(3)]
    mine_x = pl.ds(pl.multiple_of(x * 256 + c * ROWS, ROWS), ROWS)
    dg_sent = [post(dg_own.at[:, xi[j], :, mine], dg_land.at[:, :, mine_x], xs[j]) for j in range(3)]
    load(dg_own.at[:, x], dg_land.at[:, :, band_x])
    load(du_own.at[:, y], du_land.at[:, :, band_y])

    def forward(m, first, last, wait=False):
        def body(t, carry):
            span = pl.ds(pl.multiple_of(t * FTILE, FTILE), FTILE)
            if wait:
                for k in range(FTILE // LTILE):
                    for copy in weight_copies(t * (FTILE // LTILE) + k):
                        copy.wait()
            a, b, d = wg[:, span], wu[:, span], wd[span]
            if m == 1:
                a, b, d = narrow(a), narrow(b), narrow(d)
            gate = nn(x_ref[m], a) * scale_in
            up = nn(x_ref[m], b) * scale_in
            gate_s[m, :, span] = gate
            up_s[m, :, span] = up
            bent = jnp.tanh(ROOT * (gate + CUBE * gate * gate * gate))
            hidden = (0.5 * gate * (1.0 + bent) * up).astype(BF)
            hid[m, :, span] = hidden
            acc[...] += nn(hidden, d)
            return carry

        lax.fori_loop(first, last, body, 0)

    def backward(m):
        def body(t, carry):
            span = pl.ds(pl.multiple_of(t * FTILE, FTILE), FTILE)
            d = wd[span] if m == 0 else narrow(wd[span])
            grad = nt(low[m], d) * scale_out
            v, u = gate_s[m, :, span], up_s[m, :, span]
            bent = jnp.tanh(ROOT * (v + CUBE * v * v * v))
            half = 0.5 * (1.0 + bent)
            slope = half + 0.5 * v * (1.0 - bent * bent) * (ROOT * (1.0 + 3.0 * CUBE * v * v))
            dgate_ref[m, :, span] = (grad * u * slope).astype(BF)
            dup_ref[m, :, span] = (grad * (v * half)).astype(BF)
            return carry

        lax.fori_loop(0, tiles, body, 0)

    def through(m, first, last):
        def body(t, carry):
            span = pl.ds(pl.multiple_of(t * FTILE, FTILE), FTILE)
            a, b = wg[:, span], wu[:, span]
            if m == 1:
                a, b = narrow(a), narrow(b)
            acc[...] += nt(dgate_ref[m, :, span], a) + nt(dup_ref[m, :, span], b)
            return carry

        lax.fori_loop(first, last, body, 0)

    pieces = [pl.ds(k * STEP_ROWS, STEP_ROWS) for k in range(HALF // STEP_ROWS)]

    def at_rows(core, k):
        return pl.ds(pl.multiple_of(core * HALF + k * STEP_ROWS, STEP_ROWS), STEP_ROWS)

    def sum_start(i, m):
        return [post(part.at[i, at_rows(1 - c, k)], t1.at[i, r], mate) for k, r in enumerate(pieces)]

    def sum_across(i, one):
        sent = []
        for k, r in enumerate(pieces):
            one[k].wait_recv()
            th[i, r] = (part[i, at_rows(c, k)].astype(F32) + t1[i, r].astype(F32)).astype(BF)
            sent.append(post(th.at[i, r], t2.at[i, r], far))
        return sent

    def sum_back(i, two, dst, m):
        sent = []
        for k, r in enumerate(pieces):
            two[k].wait_recv()
            dst[m, at_rows(c, k)] = (th[i, r].astype(F32) + t2[i, r].astype(F32)).astype(BF)
            sent.append(post(dst.at[m, at_rows(c, k)], dst.at[m, at_rows(c, k)], mate))
        return sent

    def arrive(sent):
        for copy in sent:
            copy.wait_recv()

    def spread_hidden(m):
        land = ch.at[y, pl.ds(m * ROWS, ROWS)]
        load(hid.at[m], land)
        return [post(hid.at[m], land, ys[j]) for j in (0, 2)]

    def spread_gate(m):
        land = cg.at[x, pl.ds(m * ROWS, ROWS)]
        load(dgate_ref.at[m], land)
        return [post(dgate_ref.at[m], land, xs[j]) for j in (0, 2)]

    def relay_rows(m, sent, land, places, devices):
        for k, j in ((0, 0), (1, 2)):
            sent[k].wait_recv()
            half = land.at[places[2 - j], pl.ds(m * ROWS + k * HALF, HALF)]
            carried.append(post(half, half, devices[j]))

    def norm(m, sums):
        def slab(i, carry):
            r = pl.ds(pl.multiple_of(i * 16, 16), 16)
            v = down_sum[m, r].astype(F32)
            du = upstream[m, r].astype(F32)
            q = lax.rsqrt(jnp.mean(v * v, axis=-1, keepdims=True) + EPS)
            gain = gain_ref[3:4]
            out_ref[m, r] = (middle[m, r] + v * q * gain).astype(BF)
            lifted = du * gain
            back = q * lifted - v * (q * q * q * jnp.mean(lifted * v, axis=-1, keepdims=True))
            low[m, r] = back.astype(BF)
            return carry + jnp.sum(du * v * q, axis=0, keepdims=True)

        return lax.fori_loop(0, ROWS // 16, slab, sums)

    def swap_down(m):
        turned = low[m].T
        for zi in range(2):
            for k in range(4):
                at = (zi * 4 + k) * 288
                dd[m, zi, k] = turned[at : at + 288]
        band = pl.ds(pl.multiple_of(y * 256, 256) + m * ROWS, ROWS)
        load(dd.at[m, :, y], dd_land.at[:, :, band])

    acc[...] = jnp.zeros_like(acc)
    forward(0, 0, tiles, True)
    part[0] = (acc[...] * scale_out).astype(BF)
    one = sum_start(0, 0)
    hidden0 = spread_hidden(0)
    acc[...] = jnp.zeros_like(acc)
    forward(1, 0, 1)
    two = sum_across(0, one)
    forward(1, 1, tiles)
    part[1] = (acc[...] * scale_out).astype(BF)
    one = sum_start(1, 1)
    hidden1 = spread_hidden(1)
    three = sum_back(0, two, down_sum, 0)
    two = sum_across(1, one)
    arrive(three)
    for copy in loads:
        copy.wait()
    sums = norm(0, jnp.zeros((1, D), F32))
    relay_rows(0, hidden0, ch, yi, ys)
    carried += share(post, du_sent, du_land, yi, ROWS, c, mate)
    carried += share(post, dg_sent, dg_land, xi, ROWS, c, mate)
    swap_down(0)
    acc[...] = jnp.zeros_like(acc)
    backward(0)
    gate0 = spread_gate(0)
    load(dup_ref.at[0], cu.at[y])
    relay_rows(1, hidden1, ch, yi, ys)
    through(0, 0, tiles)
    part[2] = (acc[...] * scale_in).astype(BF)
    one = sum_start(2, 0)
    three = sum_back(1, two, down_sum, 1)
    two = sum_across(2, one)
    arrive(three)
    gains[0:1] = norm(1, sums)
    swap_down(1)
    dd_sent = [post(dd.at[c, :, yi[j]], dd_land.at[:, :, mine_y], ys[j]) for j in range(3)]
    up_sent = [post(dup_ref.at[0], cu.at[y], ys[j]) for j in (0, 2)]
    acc[...] = jnp.zeros_like(acc)
    backward(1)
    gate1 = spread_gate(1)
    through(1, 0, 2)
    relay_rows(0, gate0, cg, xi, xs)
    carried += share(post, dd_sent, dd_land, yi, ROWS, c, mate)
    through(1, 2, tiles)
    part[3] = (acc[...] * scale_in).astype(BF)
    one = sum_start(3, 1)
    three = sum_back(2, two, total_ref, 0)
    two = sum_across(3, one)
    arrive(carried)
    for copy in local[2:]:
        copy.wait()
    done = len(local)
    width = 4 * 2 * ROWS
    parts = [load(ch.at[i], wg.at[pl.ds(i * 2 * ROWS, 2 * ROWS)]) for i in range(4)]
    parts += [load(dd_land.at[i], wd.at[pl.ds(i * 288, 288), pl.ds(0, width)]) for i in range(2)]
    parts.append(load(branch_in.at[0], branch))
    for copy in parts:
        copy.wait()

    def down_product(t, carry):
        span = pl.ds(pl.multiple_of(t * FTILE, FTILE), FTILE)
        out = nn(wd[:PART, :width], wg[:width, span]).reshape(8, SHARE, FTILE)
        for k in range(8):
            wu[k * 80 : k * 80 + SHARE, span] = out[k].astype(BF)
        return carry

    lax.fori_loop(0, D // FTILE, down_product, 0)
    for k in range(8):
        load(wu.at[pl.ds(k * 80, SHARE)], pd_out.at[k // 4, k % 4])
    arrive(three)

    def slab(i, carry):
        r = pl.ds(pl.multiple_of(i * 16, 16), 16)
        back, more = norm_grad(middle[0, r], gain_ref[2:3], total_ref[0, r].astype(F32))
        grad = upstream[0, r].astype(F32) + back
        middle[0, r] = grad
        back, most = norm_grad(branch[r].astype(F32), gain_ref[1:2], grad)
        low[0, r] = back.astype(BF)
        return carry[0] + most, carry[1] + more

    sums_between = lax.fori_loop(0, ROWS // 16, slab, (jnp.zeros((1, D), F32), jnp.zeros((1, D), F32)))
    gains[1:2] = sums_between[0]
    gains[2:3] = sums_between[1]
    load(middle.at[0], mgrad_out)
    load(low.at[0], blow_out)
    three = sum_back(3, two, total_ref, 1)
    arrive(three)
    arrive(gate1)
    arrive(up_sent)
    for copy in local[done + 7 :]:
        copy.wait()
    for copy in copies:
        copy.wait_send()


def ffn(x, gain, wg, wu, wd, middle, up, branch, dg, du, scale_in, scale_out):
    def kernel(*refs):
        ffn_kernel(*refs, scale_in, scale_out)

    any_ = whole(pl.ANY)
    both = (2, ROWS, D)
    loads = wg.shape[1] // LTILE
    sems = 6 + 4 * 3 * (HALF // STEP_ROWS) + 8 + 6 + 6 + 12
    return pl.pallas_call(
        kernel,
        out_shape=[
            jax.ShapeDtypeStruct(both, BF),
            jax.ShapeDtypeStruct(both, BF),
            jax.ShapeDtypeStruct(both, BF),
            jax.ShapeDtypeStruct((3, D), F32),
            jax.ShapeDtypeStruct((4, 2 * ROWS, D), BF),
            jax.ShapeDtypeStruct((2, 288, 1024), BF),
            jax.ShapeDtypeStruct((8, SHARE, 1024), BF),
            jax.ShapeDtypeStruct((2, 288, 1024), BF),
            jax.ShapeDtypeStruct((4, 2 * ROWS, D), BF),
            jax.ShapeDtypeStruct((4, ROWS, D), BF),
            jax.ShapeDtypeStruct((2, 4, SHARE, D), BF),
            jax.ShapeDtypeStruct((ROWS, D), F32),
            jax.ShapeDtypeStruct((ROWS, D), BF),
        ],
        in_specs=[whole()] * 2 + [any_] * 8,
        out_specs=[whole()] * 4 + [any_] * 9,
        scratch_shapes=[
            VMEM(wg.shape, BF),
            VMEM(wu.shape, BF),
            VMEM(wd.shape, BF),
            VMEM(both, F32),
            VMEM(both, BF),
            VMEM(both, F32),
            VMEM(both, F32),
            VMEM(both, BF),
            VMEM(both, BF),
            VMEM((ROWS, D), F32),
            VMEM((4, ROWS, D), BF),
            VMEM(both, BF),
            VMEM((2, 2, 4, 288, ROWS), BF),
            VMEM((4, HALF, D), BF),
            VMEM((4, HALF, D), BF),
            VMEM((4, HALF, D), BF),
            VMEM(both, BF),
            VMEM((ROWS, D), BF),
            pltpu.SemaphoreType.DMA((3, loads)),
            pltpu.SemaphoreType.DMA((32,)),
            pltpu.SemaphoreType.DMA((sems,)),
            pltpu.SemaphoreType.DMA((sems,)),
        ],
        compiler_params=params(5, 63),
    )(x, gain, wg, wu, wd, middle, up, branch, dg, du)


PART = 576
SHARE = 72


def norm_grad(v, gain, grad):
    q = lax.rsqrt(jnp.mean(v * v, axis=-1, keepdims=True) + EPS)
    lifted = grad * gain
    back = q * lifted - v * (q * q * q * jnp.mean(lifted * v, axis=-1, keepdims=True))
    return back, jnp.sum(grad * v * q, axis=0, keepdims=True)


CTILE = 768


def back_kernel(
    norms_ref, q_ref, lse_ref, tag_ref, att_ref, cos_ref, sin_ref, gain_ref,
    total_in, middle_in, branch_in, up_in, mgrad0_in, blow0_in, wo_in, k_in, v_in, pd_in, du_in, cu0_in, cu_own, dg_in, cg_in,
    wq_in, wk_in, wv_in, tok_in, dn_in, ca_in,
    on, igrad, og, ou, od, oq, mgrad_out, cu1, cg_far, cu_far, db_land,
    dk, dv, dq, gsum, bt, pd, r1a, r1b, r2a, r2b, s2a, s2b, r3a, r3b, cq, part, t1, th, t2, total_ref, gb, rgb, pn,
    rd, ru, rg, rq, rn, zd, zu, zg, zq, zn, stage,
    lsem, csem, ssem, rsem,
    scale_mid, scale_in, scale_ff,
):
    x, y, z, zh, c = place_of()
    xi = [(x + j) % 4 for j in (1, 2, 3)]
    yi = [(y + j) % 4 for j in (1, 2, 3)]
    xs = [device_at(i, y, z, zh, c) for i in xi]
    ys = [device_at(x, i, z, zh, c) for i in yi]
    zp = device_at(x, y, 1 - z, zh, c)
    mate = device_at(x, y, z, zh, 1 - c)
    far = device_at(x, y, z, 1 - zh, c)
    copies, local = [], []
    post = poster(ssem, rsem, copies)
    load = loader(lsem, local)
    mine = pl.ds(pl.multiple_of(c * ROWS, ROWS), ROWS)
    mine_y = pl.ds(pl.multiple_of(y * 256 + c * ROWS, ROWS), ROWS)
    band_y = pl.ds(pl.multiple_of(y * 256, 256), 256)
    where = query_places()
    block = lax.axis_index("blk")
    lane = lax.broadcasted_iota(jnp.int32, (2 * ROWS, KEYS), 1)
    ring_a = Ring(post, lambda level, i: dk.at[level, :, i], r1a, x, xi, xs, add_blocks)
    ring_b = Ring(post, lambda level, i: dv.at[level, i], r1b, y, yi, ys, add_blocks)
    rings = (ring_a, ring_b)

    carried, up_sent, up_far = [], [], []

    ring_d = Ring(post, lambda level, i: pd.at[level, i], rd, x, xi, xs, add_columns)

    def first(k_ref, v_ref, wo, middle, branch, upstream, total, blow, g_ref):
        loads = [
            load(*pair)
            for pair in (
                (middle_in.at[1], middle.at[1]), (branch_in.at[1], branch.at[1]), (up_in.at[1], upstream.at[1]),
                (total_in.at[1], total.at[1]), (mgrad0_in, middle.at[0]), (blow0_in, blow.at[0]),
            )
        ]
        got_d = load(pd_in, pd)
        greet(xs + ys + [zp, mate, far])
        got_d.wait()
        ring_d.begin_all()
        up_sent.extend(post(lambda: cu_own.at[1], lambda: cu1.at[y], ys[j], True) for j in (0, 2))
        own_up = load(cu_own.at[1], cu1.at[y])
        for k, j in ((0, 0), (1, 2)):
            src = functools.partial(lambda j, k: cg_in.at[xi[2 - j], pl.ds(ROWS + k * HALF, HALF)], j, k)
            dst = functools.partial(lambda k: cg_far.at[pl.ds(k * HALF, HALF)], k)
            carried.append(post(src, dst, xs[j], True))
            src = functools.partial(lambda j, k: cu0_in.at[yi[2 - j], pl.ds(k * HALF, HALF)], j, k)
            dst = functools.partial(lambda k: cu_far.at[pl.ds(k * HALF, HALF)], k)
            up_far.append(post(src, dst, ys[j], True))
        for copy in loads:
            copy.wait()
        loads = [load(*pair) for pair in ((wo_in, wo), (k_in, k_ref), (v_in, v_ref))]

        sums = (jnp.zeros((1, D), F32), jnp.zeros((1, D), F32))
        for m in (1,):

            def slab(i, carry):
                r = pl.ds(pl.multiple_of(i * 16, 16), 16)
                back, more = norm_grad(middle[m, r], norms_ref[2:3], total[m, r].astype(F32))
                grad = upstream[m, r].astype(F32) + back
                middle[m, r] = grad
                back, most = norm_grad(branch[m, r].astype(F32), norms_ref[1:2], grad)
                blow[m, r] = back.astype(BF)
                return carry[0] + most, carry[1] + more

            sums = lax.fori_loop(0, ROWS // 16, slab, sums)
        gsum[1:2] = sums[0] + gain_ref[1:2]
        gsum[2:3] = sums[1] + gain_ref[2:3]
        gsum[3:4] = gain_ref[0:1]
        keep = load(middle, mgrad_out)
        loads[0].wait()
        for m in range(2):
            weight = wo[...] if m == 0 else narrow(wo[...])
            wide = (nt(blow[m], weight) * scale_mid).astype(BF)
            g_ref[m, :ROWS] = wide[:, :HD]
            g_ref[m, ROWS:] = wide[:, HD:]
        offsets = [jnp.sum(g_ref[m].astype(F32) * att_ref[m], axis=-1, keepdims=True) for m in range(2)]

        loads[1].wait()
        loads[2].wait()
        dq[...] = jnp.zeros_like(dq)

        def chunk(m, level, i):
            if m == 0:
                held, out, begin = k_ref.at[level, :, i], dk.at[level, :, i], level * 16 + i
                key_place = lane % ROWS + lane // ROWS * (4 * ROWS) + begin * ROWS
            else:
                held, out, begin = v_ref.at[level, i], dv.at[level, i], level * 16 + i * 4
                key_place = lane + begin * ROWS

            @pl.when(begin <= block)
            def _():
                q, g = q_ref[m], g_ref[m]
                keys = held[:, :ROWS, :].reshape(KEYS, HD)
                values = held[:, ROWS : 2 * ROWS, :].reshape(KEYS, HD)
                tags = held[:, TAGROW : TAGROW + 16, :ROWS].astype(F32)
                tag_row = jnp.concatenate([tags[k, 0:1, :] for k in range(CHUNK)], axis=1)
                bent = jnp.tanh(nt(q, keys) * (HD ** (-0.5) / CAP))
                ok = allowed(key_place, tag_row, tag_ref[m], where)
                p = jnp.where(ok, jnp.exp(CAP * bent - lse_ref[m]), 0.0)
                dp = nt(g, values)
                ds = (p * (dp - offsets[m]) * (1.0 - bent * bent) * HD ** (-0.5)).astype(BF)
                out[:, :ROWS, :] = tn(ds, q).astype(BF).reshape(CHUNK, ROWS, HD)
                out[:, ROWS:, :] = tn(p.astype(BF), g).astype(BF).reshape(CHUNK, ROWS, HD)
                dq[m] += nn(ds, keys)

            @pl.when(begin > block)
            def _():
                out[...] = jnp.zeros(out.shape, BF)

        for k in range(4):
            for m in range(2):
                chunk(m, *rings[m].order[k])
                rings[m].begin()
            if k == 1:
                up_far.extend(relay(post, up_sent, cu1, yi, ys))
                ring_d.onward()
        for m, places in ((0, xi), (1, yi)):
            chunk(m, 0, places[0])
            chunk(m, 1, places[2])
        for m in range(2):
            fill_turned(bt, blow[m], m)
        own = load(bt.at[:, y], db_land.at[:, :, band_y])
        for m, place in ((0, x), (1, y)):
            chunk(m, 0, place)
            chunk(m, 1, place)
        for copy in (own, keep, own_up):
            copy.wait()

    both = (2, ROWS, D)
    kv = (2, 4, 4, TAGROW + 16, HD)
    pl.run_scoped(
        first,
        VMEM(kv, BF), VMEM(kv, BF), VMEM(wo_in.shape, BF), VMEM(both, F32), VMEM(both, BF), VMEM(both, BF),
        VMEM(both, BF), VMEM(both, BF), VMEM((2, 2 * ROWS, HD), BF),
    )

    def second(pu, pg, pq, cbuf, left):
        begun = len(copies)
        used = [0]

        def fetch(sources, slot):
            out = []
            for src, dst in sources:
                copy = pltpu.make_async_copy(src, cbuf.at[(slot,) + dst], csem.at[used[0]])
                copy.start()
                used[0] += 1
                out.append(copy)
            return out

        rows_0, rows_1 = pl.ds(0, ROWS), pl.ds(ROWS, ROWS)
        everything = slice(None)

        def sources_u(cols):
            out = [(cu0_in.at[i, :, cols], (i, rows_0)) for i in (y, yi[0], yi[2])]
            out.append((cu_far.at[:, cols], (yi[1], rows_0)))
            out.append((cu1.at[:, :, cols], (everything, rows_1)))
            return out

        def sources_g(cols):
            out = [(cg_in.at[i, :, cols], (i,)) for i in (x, xi[0], xi[2])]
            out.append((cg_in.at[xi[1], rows_0, cols], (xi[1], rows_0)))
            out.append((cg_far.at[:, cols], (xi[1], rows_1)))
            return out

        tiles = [pl.ds(t * CTILE, CTILE) for t in range(D // CTILE)]
        flight = {}

        def ahead(name, sources, t, slot):
            flight[name, t] = (fetch(sources(tiles[t]), slot), slot)

        def product(name, t, weights, out):
            pending, slot = flight.pop((name, t))
            for copy in pending:
                copy.wait()
            done = nn(weights[...].reshape(PART, 1024), cbuf[slot].reshape(1024, CTILE))
            out[:, :, :, tiles[t]] = done.reshape(2, 4, SHARE, CTILE).astype(BF)

        def column_ring(p, land, along):
            held = lambda level, i: p.at[level, i]
            if along == "x":
                return Ring(post, held, land, x, xi, xs, add_columns).begin_all()
            return Ring(post, held, land, y, yi, ys, add_columns).begin_all()

        def across(ring, p, land, own):
            ring.close()
            return post(p.at[1 - z, own], land, zp)

        out_copies = {}

        def finish(copy, p, land, own, slot, width, dst, factor):
            copy.wait_recv()
            if slot in out_copies:
                out_copies[slot].wait()
            stage[slot, :, :width] = (p[z, own].astype(F32) + land[...].astype(F32)) * factor
            out_copies[slot] = load(stage.at[slot, :, pl.ds(0, width)], dst)

        left_g = load(dg_in, left.at[0])
        left_u = load(du_in, left.at[1])
        arrive(carried)
        ahead("g", sources_g, 0, 0)
        ahead("g", sources_g, 1, 1)
        ring_a.onward()
        ring_b.onward()
        left_g.wait()
        product("g", 0, left.at[0], pg)
        ahead("g", sources_g, 2, 0)
        product("g", 1, left.at[0], pg)
        product("g", 2, left.at[0], pg)
        ring_a.close()
        two_a = [post(dk.at[:, yi[j], x], r2a.at[j], ys[j]) for j in range(3)]
        ring_b.close()
        two_b = [post(dv.at[:, y, xi[j]], r2b.at[j], xs[j]) for j in range(3)]
        db_sent = [post(bt.at[:, yi[j], :, mine], db_land.at[:, :, mine_y], ys[j]) for j in range(3)]
        three_d = across(ring_d, pd, zd, x)
        arrive(up_far)
        ahead("u", sources_u, 0, 0)
        ahead("u", sources_u, 1, 1)
        left_u.wait()
        product("u", 0, left.at[1], pu)
        ahead("u", sources_u, 2, 0)
        product("u", 1, left.at[1], pu)
        product("u", 2, left.at[1], pu)
        left_n = load(dn_in, left.at[1])
        got_c = fetch([(ca_in, (everything, everything, pl.ds(0, 2 * HD)))], 1)

        def sum_two(arrivals, own, land, half):
            arrive(arrivals)
            for zi in range(2):
                out = own(zi).astype(F32)
                for j in range(3):
                    out = out + land[j, zi].astype(F32)
                half[zi] = out.astype(BF)

        def project(wq, wk, wv):
            begun = len(copies)
            weights = [load(*pair) for pair in ((wq_in, wq), (wk_in, wk), (wv_in, wv))]
            sum_two(two_a, lambda zi: dk[zi, y, x], r2a, s2a)
            three_a = post(s2a.at[1 - z], r3a, zp)
            sum_two(two_b, lambda zi: dv[zi, y, x], r2b, s2b)
            three_b = post(s2b.at[1 - z], r3b, zp)
            ring_u = column_ring(pu, ru, "x")
            carried.extend(share(post, db_sent, db_land, yi, ROWS, c, mate))
            cosine, sine = cos_ref[...], -sin_ref[...]
            for m in range(2):
                r = slice(m * ROWS, (m + 1) * ROWS)
                for h in range(2):
                    turned = turn(dq[m, h * ROWS : (h + 1) * ROWS], cosine, sine)
                    cq[y, r, h * HD : (h + 1) * HD] = turned.astype(BF)
            for m, (copy, half, land) in enumerate(((three_a, s2a, r3a), (three_b, s2b, r3b))):
                r = slice(m * ROWS, (m + 1) * ROWS)
                copy.wait_recv()
                pair = half[z].astype(F32) + land[...].astype(F32)
                cq[y, r, 2 * HD : 3 * HD] = turn(pair[:ROWS], cosine, sine).astype(BF)
                cq[y, r, 3 * HD :] = pair[ROWS:].astype(BF)
            own = lambda: cq.at[y]
            cq_sent = [post(own, own, ys[j], True) for j in (0, 2)]
            for copy in weights:
                copy.wait()
            sums = Summed(post, part, t1, th, t2, c, mate, far)
            ones = []
            for m in range(2):
                r = slice(m * ROWS, (m + 1) * ROWS)
                a, b, v = wq[...], wk[...], wv[...]
                if m == 1:
                    a, b, v = narrow(a), narrow(b), narrow(v)
                out = nt(cq[y, r, : 2 * HD], a) + nt(cq[y, r, 2 * HD : 3 * HD], b) + nt(cq[y, r, 3 * HD :], v)
                part[m] = (out * scale_in).astype(BF)
                ones.append(sums.start(m))
            twos = [sums.across(m, ones[m]) for m in range(2)]
            settle(copies[begun:])
            return ring_u, cq_sent, sums, twos

        between = len(copies)
        state = []
        pl.run_scoped(
            lambda *refs: state.append(project(*refs)),
            VMEM(wq_in.shape, BF), VMEM(wk_in.shape, BF), VMEM(wv_in.shape, BF),
        )
        ring_u, cq_sent, sums, twos = state[0]
        arrive(carried[2:])
        left_b = load(db_land, left.at[0])
        cq_far = relay(post, cq_sent, cq, yi, ys)
        ring_u.onward()
        left_b.wait()
        for copy in got_c:
            copy.wait()
        out = nn(left[0].reshape(PART, 1024), cbuf[1, :, :, : 2 * HD].reshape(1024, 512))
        pq[:, :, :, 1024:] = out.reshape(2, 4, SHARE, 512).astype(BF)
        settle(copies[begun:between])
        left_n.wait()
        arrive(cq_far)
        ring_g = column_ring(pg, rg, "y")
        for t in range(2):
            cols = pl.ds(t * 512, 512)
            out = nn(left[1].reshape(PART, 1024), cq[:, :, cols].reshape(1024, 512))
            pq[:, :, :, cols] = out.reshape(2, 4, SHARE, 512).astype(BF)
        ring_q = column_ring(pq, rq, "x")

        def last(tok, mgrad, gpad):
            begun = len(copies)
            got = [load(tok_in, tok), load(mgrad_out, mgrad)]
            threes = [sums.back(m, twos[m], total_ref, m) for m in range(2)]
            for copy in got:
                copy.wait()
            gain = jnp.zeros((1, D), F32)
            for m in range(2):
                arrive(threes[m])

                def slab(i, carry):
                    r = pl.ds(pl.multiple_of(i * 16, 16), 16)
                    back, more = norm_grad(tok[m, r].astype(F32), norms_ref[0:1], total_ref[m, r].astype(F32))
                    part[m, r] = (mgrad[m, r] + back).astype(BF)
                    return carry + more

                gain = lax.fori_loop(0, ROWS // 16, slab, gain)
            out_grad = load(part, igrad)
            gpad[...] = jnp.zeros_like(gpad)
            gpad[0:1] = gain
            gpad[1:4] = gsum[1:4]
            turned = gpad[...].T.astype(BF)
            for zi in range(2):
                for k in range(4):
                    at = (zi * 4 + k) * 288
                    gb[zi, k] = turned[at : at + 288]
            gains_far = [post(gb.at[:, yi[j]], rgb.at[j], ys[j]) for j in range(3)]
            finish(three_d, pd, zd, x, 0, D, od, scale_ff)
            three_u = across(ring_u, pu, zu, x)
            out = gb[:, y].astype(F32)
            for j in range(3):
                gains_far[j].wait_recv()
                out = out + rgb[j].astype(F32)
            pn[...] = out.reshape(2, 4, SHARE, 128).astype(BF)
            ring_n = column_ring(pn, rn, "x")
            ring_g.onward()
            ring_q.onward()
            finish(three_u, pu, zu, x, 1, D, ou, scale_in)
            ring_n.onward()
            three_g = across(ring_g, pg, zg, y)
            three_q = across(ring_q, pq, zq, x)
            three_n = across(ring_n, pn, zn, x)
            finish(three_g, pg, zg, y, 0, D, og, scale_in)
            finish(three_q, pq, zq, x, 1, 1536, oq, 1.0)
            three_n.wait_recv()
            on[...] = pn[z, x].astype(F32) + zn[...].astype(F32)
            out_grad.wait()
            for copy in out_copies.values():
                copy.wait()
            settle(copies[begun:])

        pl.run_scoped(last, VMEM(both, BF), VMEM(both, F32), VMEM((128, D), F32))
        settle(copies, True)

    wide = (2, 4, SHARE, D)
    pl.run_scoped(
        second,
        VMEM(wide, BF), VMEM(wide, BF), VMEM((2, 4, SHARE, 1536), BF),
        VMEM((2, 4, 2 * ROWS, CTILE), BF), VMEM((2, 2, 288, 1024), BF),
    )


def back(inputs, scale_mid, scale_in, scale_ff):
    def kernel(*refs):
        back_kernel(*refs, scale_mid, scale_in, scale_ff)

    any_ = whole(pl.ANY)
    tile = (2 * ROWS, HD)
    both = (2, ROWS, D)
    sems = 4 + 8 + 12 + 6 + 2 + 6 + 4 * 7 + 7 + 4 + 2 * 3 * (HALF // STEP_ROWS) + 3
    return pl.pallas_call(
        kernel,
        out_shape=[
            jax.ShapeDtypeStruct((SHARE, 128), F32),
            jax.ShapeDtypeStruct(both, BF),
            jax.ShapeDtypeStruct((SHARE, D), F32),
            jax.ShapeDtypeStruct((SHARE, D), F32),
            jax.ShapeDtypeStruct((SHARE, D), F32),
            jax.ShapeDtypeStruct((SHARE, 1536), F32),
            jax.ShapeDtypeStruct(both, F32),
            jax.ShapeDtypeStruct((4, ROWS, D), BF),
            jax.ShapeDtypeStruct((ROWS, D), BF),
            jax.ShapeDtypeStruct((ROWS, D), BF),
            jax.ShapeDtypeStruct((2, 288, 1024), BF),
        ],
        in_specs=[whole()] * 8 + [any_] * 21,
        out_specs=[whole()] + [any_] * 10,
        scratch_shapes=[
            VMEM((2, 4, 4) + tile, BF),
            VMEM((2, 4, 4) + tile, BF),
            VMEM((2,) + tile, F32),
            VMEM((8, D), F32),
            VMEM((2, 4, 288, 2 * ROWS), BF),
            VMEM((2, 4, SHARE, D), BF),
            VMEM((6, 4) + tile, BF),
            VMEM((6, 4) + tile, BF),
            VMEM((3, 2) + tile, BF),
            VMEM((3, 2) + tile, BF),
            VMEM((2,) + tile, BF),
            VMEM((2,) + tile, BF),
            VMEM(tile, BF),
            VMEM(tile, BF),
            VMEM((4, 2 * ROWS, 1024), BF),
            VMEM(both, BF),
            VMEM((2, HALF, D), BF),
            VMEM((2, HALF, D), BF),
            VMEM((2, HALF, D), BF),
            VMEM(both, BF),
            VMEM((2, 4, 288, 128), BF),
            VMEM((3, 2, 288, 128), BF),
            VMEM((2, 4, SHARE, 128), BF),
        ]
        + [VMEM((6, SHARE, w), BF) for w in (D, D, D, 1536, 128)]
        + [VMEM((SHARE, w), BF) for w in (D, D, D, 1536, 128)]
        + [
            VMEM((2, SHARE, D), F32),
            pltpu.SemaphoreType.DMA((48,)),
            pltpu.SemaphoreType.DMA((32,)),
            pltpu.SemaphoreType.DMA((sems,)),
            pltpu.SemaphoreType.DMA((sems,)),
        ],
        compiler_params=params(2, 63),
    )(*inputs)


def shards(
    inputs,
    out_grad,
    segment_ids,
    keep_mask,
    query_codes,
    key_codes,
    value_codes,
    output_codes,
    gate_codes,
    up_codes,
    down_codes,
    norm_attn_in,
    norm_attn_out,
    norm_ffn_in,
    norm_ffn_out,
):
    rows = inputs.shape[1]
    place = lax.axis_index("blk") * rows + jnp.arange(rows, dtype=jnp.int32)
    freqs = 10000.0 ** (-jnp.arange(HD // 2, dtype=F32) * 2.0 / HD)
    angles = place.astype(F32)[:, None] * freqs[None, :]
    cosine = jnp.cos(angles)
    sine = jnp.sin(angles)
    in_scale = LEVEL_SCALE * D ** (-0.5)
    mid_scale = LEVEL_SCALE * (HEADS * HD) ** (-0.5)
    ff_scale = LEVEL_SCALE * FF ** (-0.5)

    norms = jnp.stack([norm_attn_in, norm_attn_out, norm_ffn_in, norm_ffn_out])
    key_tag = jnp.where(keep_mask == 1, segment_ids, -1).astype(BF)
    key_tag = jnp.concatenate([key_tag, jnp.zeros_like(key_tag)], axis=1)
    key_tag = jnp.broadcast_to(key_tag[:, None, :], (2, 16, 2 * rows))
    tag = segment_ids.astype(F32)
    tag = jnp.concatenate([tag, tag], axis=1)[:, :, None]
    (
        middle, branch, ffn_in, queries, attended, lse, ffn_turned, blocks_a, blocks_b, d_normed, all_attended,
    ) = front(
        norms, cosine, sine, key_tag, tag,
        inputs, query_codes, key_codes, value_codes, output_codes, in_scale, mid_scale,
    )
    out_rows, up_low, ffn_in_grad, gain_ffn_out, _, _, d_gate, d_up, cg, cu0, p_down, mgrad0, blow0 = ffn(
        ffn_in, norms, gate_codes, up_codes, down_codes, middle, out_grad, branch,
        ffn_turned.reshape(8, 4, SHARE, 2 * rows), ffn_turned, in_scale, ff_scale,
    )
    g_gains, input_grad, g_gate, g_up, g_down, g_rest = back(
        (
            norms, queries, lse, tag, attended, cosine, sine, gain_ffn_out,
            ffn_in_grad, middle, branch, out_grad, mgrad0, blow0, output_codes, blocks_a, blocks_b,
            p_down, d_up, cu0, up_low, d_gate.reshape(2, 288, 1024), cg,
            query_codes, key_codes, value_codes, inputs, d_normed, all_attended,
        ),
        mid_scale,
        in_scale,
        ff_scale,
    )[:6]
    return (
        out_rows,
        input_grad,
        g_rest[:, :512] * in_scale,
        g_rest[:, 512:768] * in_scale,
        g_rest[:, 768:1024] * in_scale,
        g_rest[:, 1024:1536].T * mid_scale,
        g_gate,
        g_up,
        g_down.T,
        g_gains[:, 0],
        g_gains[:, 1],
        g_gains[:, 2],
        g_gains[:, 3],
    )


def solution(mesh):
    placed = (
        P(None, "blk", None),
        P(None, "blk", None),
        P(None, "blk"),
        P(None, "blk"),
        P(None, "tensor"),
        P(None, "tensor"),
        P(None, "tensor"),
        P("tensor", None),
        P(None, "tensor"),
        P(None, "tensor"),
        P("tensor", None),
        P(),
        P(),
        P(),
        P(),
    )
    return jax.shard_map(
        shards,
        mesh=mesh,
        in_specs=placed,
        out_specs=(
            P(None, "blk", None),
            P(None, "blk", None),
            P("blk", "tensor"),
            P("blk", "tensor"),
            P("blk", "tensor"),
            P("tensor", "blk"),
            P("blk", "tensor"),
            P("blk", "tensor"),
            P("tensor", "blk"),
            P("blk"),
            P("blk"),
            P("blk"),
            P("blk"),
        ),
        check_vma=False,
    )
```
